32 devices in a mesh: groups: 2 (over y), segment: 4 (over x, core), space: 4 (over z).
Axes of the slice: x: 2, y: 2, z: 4, core: 2. Of those that a mesh axis runs over, the one named last changes fastest.
Arguments:
- inputs: bfloat16 [4, 32, 8, 256], P('groups', 'space'), parts along dimension 0, may hold values from -6 to 6
- cotangent: bfloat16 [4, 32, 256], P('groups', 'space'), parts along dimension 0, may hold values from -6 to 6
- lift_weight: bfloat16 [8, 64], replicated, may hold values from -2 to 2
- lift_bias: float32 [64], replicated, may hold values from -3 to 3
- point_weight: bfloat16 [4, 64, 64], P('segment'), may hold values from -0.75 to 0.75
- layer_bias: float32 [4, 64], P('segment'), may hold values from -2 to 2
- spectral_weight: bfloat16 [4, 16, 32, 2, 64, 64], P('segment', 'space'), may hold values from -0.5 to 0.5
- proj_weight: bfloat16 [64, 128], replicated, may hold values from -0.75 to 0.75
- proj_bias: float32 [128], replicated, may hold values from -3 to 3
- out_weight: bfloat16 [128], replicated, may hold values from -0.5 to 0.5
Outputs:
- spectral_grad: float32 [8, 16, 32, 2, 64, 64], P(('groups', 'segment'), 'space'), parts along dimension 0
- point_grad: float32 [8, 64, 64], P(('groups', 'segment')), parts along dimension 0
The draws below stay inside these ranges and needn't reach their ends.
There are 2 independent parts, one for each index of `groups`. The reference program is written for one: setup_inputs(seed, part) draws one part's arguments, and reference() takes and returns one part's arrays. A program takes and returns all parts, laid end to end along the dimension named above; an argument that names none is the same for every part. Nothing has to cross between parts.
All inputs are finite; a program needn't handle non-finite values.
Results may differ from the reference program's by a relative error of at most 0.033.
Values may be sent and summed in bfloat16 or wider, within the bound.
No kernel may reach another device: no remote copies, remote signals or barrier semaphores. Data moves between devices by JAX's collectives and lax.ppermute only.
A program may use at most 64 MiB of HBM per device.

```python
import math
from functools import partial
import jax
import jax.numpy as jnp
from jax import lax

C = 64
MODES = 16
CIN = 8
HID = 128
NY = 256
MB = 2
KX = 32
NX = 32
LAYERS = 4


def levels(stream_key, dims, cuts, low, top_value):
    loudness = 1.0
    for position, parts in cuts:
        heights = jax.random.uniform(jax.random.fold_in(jax.random.fold_in(stream_key, 6), position), (parts,), jnp.float32, low / len(cuts), top_value / len(cuts))
        loudness = loudness * jnp.repeat(jnp.exp(heights), dims[position] // parts).reshape((-1,) + (1,) * (len(dims) - 1 - position))
    return loudness


def gaussian(own_key, dims, deviation, bound, cuts=(), kind=jnp.bfloat16):
    entries = deviation * jax.random.normal(own_key, dims, jnp.float32)
    if cuts:
        entries = entries * levels(own_key, dims, cuts, -0.22, 0.18)
    return jnp.clip(entries, -bound, bound).astype(kind)


def setup_inputs(seed: int = 0, part: int = 0) -> dict:
    splits = jax.random.split(jax.random.key(seed), 11)
    part_splits = jax.random.split(jax.random.fold_in(splits[10], part), 11)
    return {
        "inputs": gaussian(part_splits[0], (MB, NX, CIN, NY), 1.0, 6.0, ((1, 4),)),
        "cotangent": gaussian(part_splits[1], (MB, NX, NY), 1.0, 6.0, ((1, 4),)),
        "lift_weight": gaussian(splits[2], (CIN, C), CIN ** -0.5, 2.0),
        "lift_bias": gaussian(splits[3], (C,), 0.5, 3.0, (), jnp.float32),
        "point_weight": gaussian(splits[4], (LAYERS, C, C), C ** -0.5, 0.75, ((0, 4),)),
        "layer_bias": gaussian(splits[5], (LAYERS, C), 0.3, 2.0, ((0, 4),), jnp.float32),
        "spectral_weight": gaussian(splits[6], (LAYERS, MODES, KX, 2, C, C), (2 * C) ** -0.5, 0.5, ((0, 4), (1, 4))),
        "proj_weight": gaussian(splits[7], (C, HID), C ** -0.5, 0.75),
        "proj_bias": gaussian(splits[8], (HID,), 0.5, 3.0, (), jnp.float32),
        "out_weight": gaussian(splits[9], (HID,), HID ** -0.5, 0.5),
    }


highest = lax.Precision.HIGHEST

def y_tables(col_count, mode_count):
    ycells = jnp.arange(col_count, dtype=jnp.int32)[:, None]
    ymodes = jnp.arange(mode_count, dtype=jnp.int32)[None, :]
    angles = (ycells * ymodes % col_count).astype(jnp.float32) * (2.0 * math.pi / col_count)
    factor = 1.0 / math.sqrt(col_count)
    forward = jnp.stack([jnp.cos(angles), -jnp.sin(angles)], axis=1) * factor
    doubled = jnp.where(ymodes == 0, 1.0, 2.0).astype(jnp.float32)
    inverse = jnp.stack([doubled * jnp.cos(angles), -doubled * jnp.sin(angles)], axis=0) * factor
    return (forward.astype(jnp.bfloat16), jnp.transpose(inverse, (0, 2, 1)).astype(jnp.bfloat16))

def x_tables(row_total, mode_count):
    kx_count = 2 * mode_count
    indices = jnp.arange(kx_count, dtype=jnp.int32)
    freq_values = jnp.where(indices < mode_count, indices, indices - kx_count)
    xcells = jnp.arange(row_total, dtype=jnp.int32)
    angles = (freq_values[:, None] * xcells[None, :] % row_total).astype(jnp.float32) * (2.0 * math.pi / row_total)
    factor = 1.0 / math.sqrt(row_total)
    cosine_part = jnp.cos(angles) * factor
    sine_part = jnp.sin(angles) * factor
    forward = jnp.stack([jnp.stack([cosine_part, sine_part], -1), jnp.stack([-sine_part, cosine_part], -1)], axis=1)
    cosine_flip = cosine_part.T
    sine_flip = sine_part.T
    inverse = jnp.stack([jnp.stack([cosine_flip, -sine_flip], -1), jnp.stack([sine_flip, cosine_flip], -1)], axis=1)
    return (forward, inverse)

def mode_mult(coeffs, kernel):
    real_in, imag_in = (coeffs[:, :, 0], coeffs[:, :, 1])
    real_kernel, imag_kernel = (kernel[:, :, 0], kernel[:, :, 1])
    product = partial(jnp.einsum, 'mjc,mjco->mjo', precision=highest)
    real_out = product(real_in, real_kernel) - product(imag_in, imag_kernel)
    imag_out = product(real_in, imag_kernel) + product(imag_in, real_kernel)
    return jnp.stack([real_out, imag_out], axis=2)

def mode_back(coeffs, mode_grads, kernel):
    real_in, imag_in = (coeffs[:, :, 0], coeffs[:, :, 1])
    real_grad, imag_grad = (mode_grads[:, :, 0], mode_grads[:, :, 1])
    real_kernel, imag_kernel = (kernel[:, :, 0], kernel[:, :, 1])
    outer_sum = partial(jnp.einsum, 'mjc,mjo->mjco', precision=highest)
    inner_sum = partial(jnp.einsum, 'mjo,mjco->mjc', precision=highest)
    kernel_real = outer_sum(real_in, real_grad) + outer_sum(imag_in, imag_grad)
    kernel_imag = outer_sum(real_in, imag_grad) - outer_sum(imag_in, real_grad)
    coeff_real = inner_sum(real_grad, real_kernel) + inner_sum(imag_grad, imag_kernel)
    coeff_imag = inner_sum(imag_grad, real_kernel) - inner_sum(real_grad, imag_kernel)
    return (jnp.stack([kernel_real, kernel_imag], axis=2), jnp.stack([coeff_real, coeff_imag], axis=2))

def gelu_grad(pre_act, upstream):
    _, pullback = jax.vjp(jax.nn.gelu, pre_act)
    return pullback(upstream)[0]

def reference(inputs, cotangent, lift_weight, lift_bias, point_weight, layer_bias, spectral_weight, proj_weight, proj_bias, out_weight):
    y_forward, y_inverse = y_tables(NY, MODES)
    x_forward, x_inverse = x_tables(NX, MODES)
    x_forward_adj = jnp.transpose(x_forward, (2, 3, 0, 1))
    x_inverse_adj = jnp.transpose(x_inverse, (2, 3, 0, 1))
    y_forward_wide = y_forward.astype(jnp.float32)
    y_inverse_wide = y_inverse.astype(jnp.float32)
    kernel_grads = [jnp.zeros((MODES, KX, 2, C, C), jnp.float32) for which_layer in range(LAYERS)]
    point_grads = [jnp.zeros((C, C), jnp.float32) for which_layer in range(LAYERS)]
    for which_batch in range(MB):
        sample = inputs[which_batch].astype(jnp.float32)
        activity = jnp.einsum('xty,tc->xcy', sample, lift_weight.astype(jnp.float32), precision=highest)
        activity = (activity + lift_bias[None, :, None]).astype(jnp.bfloat16)
        stored = []
        for which_layer in range(LAYERS):
            kernel = spectral_weight[which_layer].astype(jnp.float32)
            wide_act = activity.astype(jnp.float32)
            ycoef = jnp.einsum('xcy,ypm->xmpc', wide_act, y_forward_wide, precision=highest)
            coeffs = jnp.einsum('jqxp,xmpc->mjqc', x_forward, ycoef, precision=highest)
            spread = jnp.einsum('xpjq,mjqc->xmpc', x_inverse, mode_mult(coeffs, kernel), precision=highest)
            branch = jnp.einsum('xmpc,pmy->xcy', spread, y_inverse_wide, precision=highest)
            pointwise = jnp.einsum('xcy,co->xoy', wide_act, point_weight[which_layer].astype(jnp.float32), precision=highest)
            pre_act = pointwise + branch + layer_bias[which_layer][None, :, None]
            stored.append((activity, pre_act, coeffs))
            activity = jax.nn.gelu(pre_act).astype(jnp.bfloat16)
        hidden = jnp.einsum('xcy,ck->xky', activity.astype(jnp.float32), proj_weight.astype(jnp.float32), precision=highest)
        hidden = hidden + proj_bias[None, :, None]
        upstream = out_weight.astype(jnp.float32)[None, :, None] * cotangent[which_batch].astype(jnp.float32)[:, None, :]
        hidden_grad = gelu_grad(hidden, upstream).astype(jnp.bfloat16)
        grad_acts = jnp.einsum('xky,ck->xcy', hidden_grad.astype(jnp.float32), proj_weight.astype(jnp.float32), precision=highest).astype(jnp.bfloat16)
        for which_layer in reversed(range(LAYERS)):
            layer_in, pre_act, coeffs = stored[which_layer]
            kernel = spectral_weight[which_layer].astype(jnp.float32)
            pre_grad = gelu_grad(pre_act, grad_acts.astype(jnp.float32)).astype(jnp.bfloat16)
            pre_wide = pre_grad.astype(jnp.float32)
            point_grads[which_layer] = point_grads[which_layer] + jnp.einsum('xcy,xoy->co', layer_in.astype(jnp.float32), pre_wide, precision=highest)
            y_grads = jnp.einsum('xoy,pmy->xmpo', pre_wide, y_inverse_wide, precision=highest)
            mode_grads = jnp.einsum('jqxp,xmpo->mjqo', x_inverse_adj, y_grads, precision=highest)
            kernel_step, coeff_step = mode_back(coeffs, mode_grads, kernel)
            kernel_grads[which_layer] = kernel_grads[which_layer] + kernel_step
            back_rows = jnp.einsum('xpjq,mjqc->xmpc', x_forward_adj, coeff_step, precision=highest)
            back_branch = jnp.einsum('xmpc,ypm->xcy', back_rows, y_forward_wide, precision=highest)
            pointwise_back = jnp.einsum('co,xoy->xcy', point_weight[which_layer].astype(jnp.float32), pre_wide, precision=highest)
            grad_acts = (pointwise_back + back_branch).astype(jnp.bfloat16)
    factor = 1.0 / math.sqrt(MB * NX * NY)
    return (jnp.stack(kernel_grads), jnp.stack(point_grads) * factor)
```

```python
from functools import partial
import math

import jax
import jax.numpy as jnp
import numpy as np
from jax import lax
from jax.experimental import pallas as pl
from jax.experimental.pallas import tpu as pltpu
from jax.sharding import PartitionSpec as P

highest = lax.Precision.HIGHEST


def as_sent(array):
    return jax.tree.map(lambda a: a.astype(jnp.bfloat16) if a.dtype == jnp.float32 else a, array)


def passed_along(block, axis, distance):
    devices = range(lax.axis_size(axis))
    route = [(i - distance, i) for i in devices if i - distance in devices]
    return lax.ppermute(block, axis, route)


def y_tables(col_count, mode_count):
    ycells = jnp.arange(col_count, dtype=jnp.int32)[:, None]
    ymodes = jnp.arange(mode_count, dtype=jnp.int32)[None, :]
    angles = (ycells * ymodes % col_count).astype(jnp.float32) * (2.0 * math.pi / col_count)
    factor = 1.0 / math.sqrt(col_count)
    forward = jnp.stack([jnp.cos(angles), -jnp.sin(angles)], axis=1) * factor
    doubled = jnp.where(ymodes == 0, 1.0, 2.0).astype(jnp.float32)
    inverse = jnp.stack([doubled * jnp.cos(angles), -doubled * jnp.sin(angles)], axis=0) * factor
    return (forward.astype(jnp.bfloat16), jnp.transpose(inverse, (0, 2, 1)).astype(jnp.bfloat16))


def x_tables(row_total, mode_count):
    kx_count = 2 * mode_count
    indices = jnp.arange(kx_count, dtype=jnp.int32)
    freq_values = jnp.where(indices < mode_count, indices, indices - kx_count)
    xcells = jnp.arange(row_total, dtype=jnp.int32)
    angles = (freq_values[:, None] * xcells[None, :] % row_total).astype(jnp.float32) * (
        2.0 * math.pi / row_total
    )
    factor = 1.0 / math.sqrt(row_total)
    cosine_part = jnp.cos(angles) * factor
    sine_part = jnp.sin(angles) * factor
    forward = jnp.stack(
        [jnp.stack([cosine_part, sine_part], -1), jnp.stack([-sine_part, cosine_part], -1)], axis=1
    )
    cosine_flip = cosine_part.T
    sine_flip = sine_part.T
    inverse = jnp.stack(
        [jnp.stack([cosine_flip, -sine_flip], -1), jnp.stack([sine_flip, cosine_flip], -1)], axis=1
    )
    return (forward, inverse)


def mode_mult(coeffs, kernel):
    real_in, imag_in = (coeffs[:, :, 0], coeffs[:, :, 1])
    real_kernel, imag_kernel = (kernel[:, :, 0], kernel[:, :, 1])
    product = partial(jnp.einsum, "mjc,mjco->mjo", precision=highest)
    real_out = product(real_in, real_kernel) - product(imag_in, imag_kernel)
    imag_out = product(real_in, imag_kernel) + product(imag_in, real_kernel)
    return jnp.stack([real_out, imag_out], axis=2)


def mode_back(coeffs, mode_grads, kernel):
    real_in, imag_in = (coeffs[:, :, 0], coeffs[:, :, 1])
    real_grad, imag_grad = (mode_grads[:, :, 0], mode_grads[:, :, 1])
    real_kernel, imag_kernel = (kernel[:, :, 0], kernel[:, :, 1])
    outer_sum = partial(jnp.einsum, "mjc,mjo->mjco", precision=highest)
    inner_sum = partial(jnp.einsum, "mjo,mjco->mjc", precision=highest)
    kernel_real = outer_sum(real_in, real_grad) + outer_sum(imag_in, imag_grad)
    kernel_imag = outer_sum(real_in, imag_grad) - outer_sum(imag_in, real_grad)
    coeff_real = inner_sum(real_grad, real_kernel) + inner_sum(imag_grad, imag_kernel)
    coeff_imag = inner_sum(imag_grad, real_kernel) - inner_sum(real_grad, imag_kernel)
    return (
        jnp.stack([kernel_real, kernel_imag], axis=2),
        jnp.stack([coeff_real, coeff_imag], axis=2),
    )


def gelu_grad(pre_act, upstream):
    _, pullback = jax.vjp(jax.nn.gelu, pre_act)
    return pullback(upstream)[0]


def store_slot(buffer, value, slot_clip, is_valid):
    previous = lax.dynamic_index_in_dim(buffer, slot_clip, 0, keepdims=False)
    return lax.dynamic_update_index_in_dim(
        buffer, jnp.where(is_valid, value, previous), slot_clip, 0
    )


def on_device(
    inputs,
    cotangent,
    lift_weight,
    lift_bias,
    point_weight,
    layer_bias,
    spectral_weight,
    proj_weight,
    proj_bias,
    out_weight,
):
    batch_count, row_count, _, col_count = inputs.shape
    segment_count = lax.axis_size("segment")
    segment_index = lax.axis_index("segment")
    space_count = lax.axis_size("space")
    owned_modes = spectral_weight.shape[1]
    kx_count = spectral_weight.shape[2]
    channels = point_weight.shape[1]
    mode_count = kx_count // 2
    y_forward, y_inverse = y_tables(col_count, mode_count)
    x_forward, x_inverse = x_tables(row_count * space_count, mode_count)
    x_forward_adj = jnp.transpose(x_forward, (2, 3, 0, 1))
    x_inverse_adj = jnp.transpose(x_inverse, (2, 3, 0, 1))
    y_forward_wide = y_forward.astype(jnp.float32)
    y_inverse_wide = y_inverse.astype(jnp.float32)
    kernel = spectral_weight[0].astype(jnp.float32)
    point_matrix = point_weight[0]
    bias_vector = layer_bias[0]
    tick_count = batch_count + segment_count - 1

    def to_owners(y_coeffs, x_table):
        exchanged = lax.all_to_all(
            y_coeffs.astype(jnp.bfloat16), "space", split_axis=1, concat_axis=0, tiled=True
        ).astype(y_coeffs.dtype)
        return jnp.einsum("jqxp,xmpc->mjqc", x_table, exchanged, precision=highest)

    def from_owners(owned, x_table):
        spread = jnp.einsum("xpjq,mjqc->xmpc", x_table, owned, precision=highest)
        return lax.all_to_all(
            as_sent(spread), "space", split_axis=0, concat_axis=1, tiled=True
        ).astype(spread.dtype)

    def lifted(pick_slot):
        sample = lax.dynamic_index_in_dim(inputs, pick_slot, 0, keepdims=False)
        mixed = jnp.einsum("xty,tc->xcy", sample, lift_weight, preferred_element_type=jnp.float32)
        return (mixed + lift_bias[None, :, None]).astype(jnp.bfloat16)

    def forward_tick(state_now, tick_now):
        incoming, pre_store, act_store, mode_store = state_now
        pick_slot = jnp.clip(tick_now, 0, batch_count - 1)
        layer_in = lax.cond(segment_index == 0, lambda: lifted(pick_slot), lambda: incoming)
        y_coeffs = jnp.einsum(
            "xcy,ypm->xmpc", layer_in, y_forward, preferred_element_type=jnp.float32
        )
        coeffs = to_owners(y_coeffs, x_forward)
        back_rows = from_owners(mode_mult(coeffs, kernel), x_inverse)
        branch = jnp.einsum("xmpc,pmy->xcy", back_rows, y_inverse_wide, precision=highest)
        pointwise = jnp.einsum(
            "xcy,co->xoy", layer_in, point_matrix, preferred_element_type=jnp.float32
        )
        pre_act = pointwise + branch + bias_vector[None, :, None]
        slot_index = tick_now - segment_index
        is_valid = (slot_index >= 0) & (slot_index < batch_count)
        slot_clip = jnp.clip(slot_index, 0, batch_count - 1)
        pre_store = store_slot(pre_store, pre_act, slot_clip, is_valid)
        act_store = store_slot(act_store, layer_in, slot_clip, is_valid)
        mode_store = store_slot(mode_store, coeffs, slot_clip, is_valid)
        layer_out = jax.nn.gelu(pre_act).astype(jnp.bfloat16)
        sent = passed_along(layer_out, "segment", 1)
        return ((sent, pre_store, act_store, mode_store), None)

    start_state = (
        jnp.zeros((row_count, channels, col_count), jnp.bfloat16),
        jnp.zeros((batch_count, row_count, channels, col_count), jnp.float32),
        jnp.zeros((batch_count, row_count, channels, col_count), jnp.bfloat16),
        jnp.zeros((batch_count, owned_modes, kx_count, 2, channels), jnp.float32),
    )
    final_state, _ = lax.scan(forward_tick, start_state, jnp.arange(tick_count, dtype=jnp.int32))
    _, pre_store, act_store, mode_store = final_state

    def top_grad(slot_clip, pre_act):
        top_act = jax.nn.gelu(pre_act).astype(jnp.bfloat16)
        hidden = jnp.einsum("xcy,ck->xky", top_act, proj_weight, preferred_element_type=jnp.float32)
        hidden = hidden + proj_bias[None, :, None]
        target = lax.dynamic_index_in_dim(cotangent, slot_clip, 0, keepdims=False)
        upstream = (
            out_weight.astype(jnp.float32)[None, :, None] * target.astype(jnp.float32)[:, None, :]
        )
        hidden_grad = gelu_grad(hidden, upstream).astype(jnp.bfloat16)
        return jnp.einsum(
            "xky,ck->xcy", hidden_grad, proj_weight, preferred_element_type=jnp.float32
        ).astype(jnp.bfloat16)

    def backward_tick(state_now, tick_now):
        incoming, point_sum, kernel_sum = state_now
        slot_index = tick_now - (segment_count - 1 - segment_index)
        is_valid = (slot_index >= 0) & (slot_index < batch_count)
        slot_clip = jnp.clip(slot_index, 0, batch_count - 1)
        pre_act = lax.dynamic_index_in_dim(pre_store, slot_clip, 0, keepdims=False)
        layer_in = lax.dynamic_index_in_dim(act_store, slot_clip, 0, keepdims=False)
        coeffs = lax.dynamic_index_in_dim(mode_store, slot_clip, 0, keepdims=False)
        grad_out = lax.cond(
            segment_index == segment_count - 1,
            lambda: top_grad(slot_clip, pre_act),
            lambda: incoming,
        )
        pre_grad = gelu_grad(pre_act, grad_out.astype(jnp.float32)).astype(jnp.bfloat16)
        point_term = jnp.einsum(
            "xcy,xoy->co", layer_in, pre_grad, preferred_element_type=jnp.float32
        )
        y_grads = jnp.einsum(
            "xoy,pmy->xmpo", pre_grad, y_inverse, preferred_element_type=jnp.float32
        )
        mode_grads = to_owners(y_grads, x_inverse_adj)
        kernel_step, coeff_step = mode_back(coeffs, mode_grads, kernel)
        back_rows = from_owners(coeff_step, x_forward_adj)
        back_branch = jnp.einsum("xmpc,ypm->xcy", back_rows, y_forward_wide, precision=highest)
        pointwise_back = jnp.einsum(
            "co,xoy->xcy", point_matrix, pre_grad, preferred_element_type=jnp.float32
        )
        grad_in = (pointwise_back + back_branch).astype(jnp.bfloat16)
        point_sum = point_sum + jnp.where(is_valid, point_term, 0.0)
        kernel_sum = kernel_sum + jnp.where(is_valid, kernel_step, 0.0)
        sent = passed_along(grad_in, "segment", -1)
        return ((sent, point_sum, kernel_sum), None)

    back_start = (
        jnp.zeros((row_count, channels, col_count), jnp.bfloat16),
        jnp.zeros((channels, channels), jnp.float32),
        jnp.zeros((owned_modes, kx_count, 2, channels, channels), jnp.float32),
    )
    back_state, _ = lax.scan(backward_tick, back_start, jnp.arange(tick_count, dtype=jnp.int32))
    _, point_sum, kernel_sum = back_state
    point_total = lax.psum(point_sum, "space")
    factor = 1.0 / math.sqrt(batch_count * row_count * space_count * col_count)
    return (kernel_sum[None], (point_total * factor)[None])


f32, bf16 = (jnp.float32, jnp.bfloat16)
NT = (((1,), (1,)), ((), ()))
VMEM_LIMIT = 48 << 20


def np_y_tables(col_count, mode_count):
    ycells = np.arange(col_count)[:, None]
    ymodes = np.arange(mode_count)[None, :]
    angles = (ycells * ymodes % col_count) * (2.0 * math.pi / col_count)
    factor = 1.0 / math.sqrt(col_count)
    doubled = np.where(ymodes == 0, 1.0, 2.0)
    forward = np.stack([np.cos(angles), -np.sin(angles)], axis=0) * factor
    inverse = np.stack([doubled * np.cos(angles), -doubled * np.sin(angles)], axis=0) * factor
    return (forward.transpose(2, 0, 1), inverse.transpose(2, 0, 1))


def np_x_tables(row_total, mode_count):
    kx_count = 2 * mode_count
    indices = np.arange(kx_count)
    freq = np.where(indices < mode_count, indices, indices - kx_count)
    angles = (freq[:, None] * np.arange(row_total)[None, :] % row_total) * (2.0 * math.pi / row_total)
    factor = 1.0 / math.sqrt(row_total)
    c, s = (np.cos(angles) * factor, np.sin(angles) * factor)
    forward = np.stack([np.stack([c, s], -1), np.stack([-s, c], -1)], axis=1)
    inverse = np.stack([np.stack([c.T, -s.T], -1), np.stack([s.T, c.T], -1)], axis=1)
    return (forward, inverse)


def hdot(a, b):
    return jnp.dot(a, b, precision=highest, preferred_element_type=f32)


def split_rows(a):
    hi = a.astype(bf16)
    lo = (a - hi.astype(f32)).astype(bf16)
    return jnp.concatenate([hi, lo], axis=0)


def gelu_both(v, with_value=True):
    k0 = math.sqrt(2.0 / math.pi)
    k1 = k0 * 0.044715
    v2 = v * v
    t = jnp.tanh(v * (k0 + k1 * v2))
    half = 0.5 * v
    slope = (0.5 + 0.5 * t) + half * (1.0 - t * t) * (k0 + (3.0 * k1) * v2)
    return (half + half * t if with_value else None, slope)


def low_half(shape):
    return lax.broadcasted_iota(jnp.int32, shape, 1) < shape[1] // 2


def swap_halves(a):
    return pltpu.roll(a, a.shape[1] // 2, 1)


def own_rows(y_ref, row, x_count):
    return jnp.concatenate(
        [y_ref[pl.ds(row + p, x_count, stride=16), :] for p in range(2)], axis=0
    )


def forward_modes(y_ref, w_ref, lx_ref, xi_ref, t_ref, m_ref, out_ref):
    pairs, lanes = (w_ref.shape[0], w_ref.shape[2])
    x_count = y_ref.shape[0] // 16
    half = t_ref.shape[0] // 2
    ys = own_rows(y_ref, 8, x_count)
    sw = swap_halves(ys)
    low = low_half(ys.shape)
    zero = jnp.zeros_like(ys)
    rhs0 = jnp.concatenate([jnp.where(low, ys, zero), jnp.where(low, zero, sw)], axis=0)
    rhs1 = jnp.concatenate([jnp.where(low, sw, zero), jnp.where(low, zero, ys)], axis=0)
    t_ref[:half] = hdot(lx_ref[...], rhs0)
    t_ref[half:] = hdot(lx_ref[...], rhs1)
    for j in range(pairs):
        rows = split_rows(t_ref[pl.ds(j, 8, stride=pairs), :])
        prod = jnp.dot(rows, w_ref[j], preferred_element_type=f32)
        m_ref[pl.ds(j, 8, stride=pairs), :] = prod[:8] + prod[8:]
    m0, m1 = (m_ref[:half], m_ref[half:])
    lowm = low_half(m0.shape)
    first = (lax.broadcasted_iota(jnp.int32, m0.shape, 0) // pairs) % 2 == 0
    s0 = jnp.where(first, m0, swap_halves(m0))
    s1 = jnp.where(first, swap_halves(m1), m1)
    out_ref[...] = hdot(xi_ref[...], jnp.where(lowm, s0, s1)).astype(bf16)


def backward_modes(y_ref, w_ref, xa_ref, xf_ref, t_ref, m_ref, out_ref):
    pairs = w_ref.shape[0]
    x_count = y_ref.shape[0] // 16
    half = t_ref.shape[0] // 2
    g = hdot(xa_ref[...], own_rows(y_ref, 8, x_count))
    sw = swap_halves(g)
    low = low_half(g.shape)
    first = (lax.broadcasted_iota(jnp.int32, g.shape, 0) // pairs) % 2 == 0
    keep = low == first
    zero = jnp.zeros_like(g)
    t_ref[:half] = jnp.where(keep, jnp.where(first, g, sw), zero)
    t_ref[half:] = jnp.where(keep, jnp.where(first, sw, g), zero)
    for j in range(pairs):
        rows = split_rows(t_ref[pl.ds(j, 8, stride=pairs), :])
        prod = lax.dot_general(rows, w_ref[j], NT, preferred_element_type=f32)
        m_ref[pl.ds(j, 8, stride=pairs), :] = prod[:8] + prod[8:]
    quarter = half // 2
    pr0, pi0, pr1, pi1 = (m_ref[i * quarter : (i + 1) * quarter] for i in range(4))
    lowq = low_half(pr0.shape)
    real = jnp.where(lowq, pr0 + swap_halves(pi0), swap_halves(pr1) + pi1)
    imag = jnp.where(lowq, pi0 - swap_halves(pr0), swap_halves(pi1) - pr1)
    out_ref[...] = hdot(xf_ref[...], jnp.concatenate([real, imag], axis=0)).astype(bf16)


def widen(recv_ref, r_ref):
    chunks, rows, _ = recv_ref.shape
    for k in range(chunks):
        r_ref[k * rows : (k + 1) * rows] = recv_ref[k].astype(f32)


def row_product(weight, field, r_ref, table, x, x_count):
    rows = r_ref[pl.ds(x, table.shape[0], stride=x_count), :]
    lhs = jnp.concatenate([weight, rows.T.astype(bf16)], axis=1)
    return jnp.dot(lhs, jnp.concatenate([field, table], axis=0), preferred_element_type=f32)


def lift_kernel(in_ref, lw_ref, lb_ref, tab_ref, act_ref, y_ref, *, space, per_chunk, depth):
    chunks = in_ref.shape[0]
    for k in range(chunks):
        base = (k % space) * (chunks // space) * per_chunk + (k // space) * per_chunk
        for i in range(per_chunk):
            cells = in_ref[k, i * depth : (i + 1) * depth, :]
            act = jnp.dot(lw_ref[...], cells, preferred_element_type=f32) + lb_ref[...]
            act = act.astype(bf16)
            act_ref[base + i] = act
            y_ref[(base + i) * 16 : (base + i + 1) * 16] = lax.dot_general(
                tab_ref[...], act, NT, preferred_element_type=f32
            )


def first_modes_kernel(y_ref, w_ref, lx_ref, xi_ref, out_ref, t_ref, m_ref):
    forward_modes(y_ref, w_ref, lx_ref, xi_ref, t_ref, m_ref, out_ref)


def forward_kernel(
    recv_ref, act_ref, pw_ref, pb_ref, inv_ref, tab_ref, w_ref, lx_ref, xi_ref,
    next_ref, slope_ref, y_ref, out_ref, r_ref, t_ref, m_ref,
):
    step = pl.program_id(0)
    block = act_ref.shape[0]
    x_count = y_ref.shape[0] // 16

    @pl.when(step == 0)
    def _():
        widen(recv_ref, r_ref)

    def one(i, carry):
        x = step * block + i
        pre = row_product(pw_ref[...], act_ref[i], r_ref, inv_ref[...], x, x_count) + pb_ref[...]
        value, slope = gelu_both(pre)
        value = value.astype(bf16)
        next_ref[i] = value
        slope_ref[i] = slope.astype(bf16)
        y_ref[pl.ds(pl.multiple_of(x * 16, 16), 16), :] = lax.dot_general(
            tab_ref[...], value, NT, preferred_element_type=f32
        )
        return carry

    lax.fori_loop(0, block, one, 0, unroll=2)

    @pl.when(step == pl.num_programs(0) - 1)
    def _():
        forward_modes(y_ref, w_ref, lx_ref, xi_ref, t_ref, m_ref, out_ref)


def adjoint_rows(x, i, grad, act, tab_ref, pre_ref, y_ref, point_ref):
    pre_grad = grad.astype(bf16)
    pre_ref[i] = pre_grad
    both = lax.dot_general(
        jnp.concatenate([tab_ref[...], act], axis=0), pre_grad, NT, preferred_element_type=f32
    )
    y_ref[pl.ds(pl.multiple_of(x * 16, 16), 16), :] = both[:16]
    point_ref[...] += both[16:]


def top_kernel(
    recv_ref, act_ref, in_ref, pw_ref, pb_ref, inv_ref, up_ref, hb_ref, down_ref, ow_ref, tab_ref,
    w_ref, xa_ref, xf_ref,
    pre_ref, y_ref, point_ref, out_ref, r_ref, t_ref, m_ref, *, space, per_chunk, first_row, batch,
):
    step = pl.program_id(0)
    block = act_ref.shape[0]
    x_count = y_ref.shape[0] // 16
    parts = in_ref.shape[0] // space

    @pl.when(step == 0)
    def _():
        widen(recv_ref, r_ref)
        point_ref[...] = jnp.zeros_like(point_ref)

    def one(i, carry):
        x = step * block + i
        act = act_ref[i]
        pre = row_product(pw_ref[...], act, r_ref, inv_ref[...], x, x_count) + pb_ref[...]
        value, slope = gelu_both(pre)
        value = value.astype(bf16)
        pair = x // per_chunk
        chunk = (pair % parts) * space + pair // parts
        within = x % per_chunk
        cots = in_ref[chunk, first_row : first_row + per_chunk * batch, :].astype(f32)
        grads = []
        size = value.shape[0] // batch
        for b in range(batch):
            hidden = jnp.dot(up_ref[...], value[b * size : (b + 1) * size], preferred_element_type=f32)
            _, hidden_slope = gelu_both(hidden + hb_ref[...], False)
            cot = cots[b : b + 1]
            for other in range(1, per_chunk):
                row = other * batch + b
                cot = jnp.where(within == other, cots[row : row + 1], cot)
            hidden_grad = (hidden_slope * (ow_ref[...] * cot)).astype(bf16)
            grads.append(jnp.dot(down_ref[...], hidden_grad, preferred_element_type=f32))
        grad = jnp.concatenate(grads, axis=0).astype(bf16).astype(f32)
        adjoint_rows(x, i, grad * slope, act, tab_ref, pre_ref, y_ref, point_ref)
        return carry

    lax.fori_loop(0, block, one, 0)

    @pl.when(step == pl.num_programs(0) - 1)
    def _():
        backward_modes(y_ref, w_ref, xa_ref, xf_ref, t_ref, m_ref, out_ref)


def backward_kernel(
    recv_ref, grad_ref, slope_ref, act_ref, pw_ref, fwd_ref, tab_ref, w_ref, xa_ref, xf_ref,
    pre_ref, y_ref, point_ref, out_ref, r_ref, t_ref, m_ref, *, send,
):
    step = pl.program_id(0)
    block = act_ref.shape[0]
    x_count = y_ref.shape[0] // 16

    @pl.when(step == 0)
    def _():
        widen(recv_ref, r_ref)
        point_ref[...] = jnp.zeros_like(point_ref)

    def one(i, carry):
        x = step * block + i
        grad = row_product(pw_ref[...], grad_ref[i], r_ref, fwd_ref[...], x, x_count)
        grad = grad.astype(bf16).astype(f32) * slope_ref[i].astype(f32)
        adjoint_rows(x, i, grad, act_ref[i], tab_ref, pre_ref, y_ref, point_ref)
        return carry

    lax.fori_loop(0, block, one, 0, unroll=2)

    @pl.when(step == pl.num_programs(0) - 1)
    def _():
        if send:
            backward_modes(y_ref, w_ref, xa_ref, xf_ref, t_ref, m_ref, out_ref)
        else:
            out_ref[...] = jnp.zeros_like(out_ref)


def grads_kernel(seg_ref, *refs, layers, scale):
    ya_refs, yg_refs, pg_refs = (refs[:layers], refs[layers : 2 * layers], refs[2 * layers : 3 * layers])
    xz_ref, xa_ref, out_ref, point_ref, ya, yg, a_ref, b_ref = refs[3 * layers :]
    mode = pl.program_id(0)
    x_count = ya.shape[0] // 16

    @pl.when(mode == 0)
    def _():
        for layer in range(layers):
            @pl.when(seg_ref[0] == layer)
            def _():
                ya[...] = ya_refs[layer][...]
                yg[...] = yg_refs[layer][...]
                pg = pg_refs[layer][...]
                c = point_ref.shape[0]
                point_ref[...] = (pg[:c, :c] + pg[c:, c:]) * scale

    z = hdot(xz_ref[...], own_rows(ya, 2 * mode, x_count))
    g = hdot(xa_ref[...], own_rows(yg, 2 * mode, x_count))
    rows = z.shape[0]
    kx = rows // 2
    zs, gs = (swap_halves(z), swap_halves(g))
    c = z.shape[1] // 2
    a_ref[:rows] = z
    a_ref[rows:] = zs
    low = low_half((kx, z.shape[1]))
    b_ref[:kx] = jnp.where(low, g[:kx], gs[kx:])
    b_ref[kx:rows] = jnp.where(low, g[kx:], -gs[:kx])
    b_ref[rows : rows + kx] = jnp.where(low, gs[:kx], g[kx:])
    b_ref[rows + kx :] = jnp.where(low, gs[kx:], -g[:kx])
    for j in range(kx):
        a = a_ref[pl.ds(j, 4, stride=kx), :][:, :c]
        b = b_ref[pl.ds(j, 4, stride=kx), :]
        ah, bh = (a.astype(bf16), b.astype(bf16))
        al, bl = ((a - ah.astype(f32)).astype(bf16), (b - bh.astype(f32)).astype(bf16))
        left = jnp.concatenate([ah.astype(f32), al.astype(f32), ah.astype(f32)], axis=0)
        right = jnp.concatenate([bh.astype(f32), bh.astype(f32), bl.astype(f32)], axis=0).astype(bf16)
        left = left.T.astype(bf16)
        out_ref[0, j, 0] = jnp.dot(left, right[:, :c], preferred_element_type=f32)
        out_ref[0, j, 1] = jnp.dot(left, right[:, c:], preferred_element_type=f32)


def replicated(
    inputs, cotangent, lift_weight, lift_bias, point_weight, layer_bias, spectral_weight,
    proj_weight, proj_bias, out_weight,
):
    batch, row_count, depth, cols = inputs.shape
    segments, space = (lax.axis_size("segment"), lax.axis_size("space"))
    seg, place = (lax.axis_index("segment"), lax.axis_index("space"))
    both = ("segment", "space")
    chunks = segments * space
    owned, kx = spectral_weight.shape[1:3]
    c = point_weight.shape[1]
    bc = batch * c
    x_count = row_count * space
    mode_count = owned * space
    per_chunk = row_count // segments
    pairs = kx // 2

    stack = spectral_weight[0].reshape(owned, 2, pairs, 2 * c, c)
    packed = [
        jnp.concatenate([w[0], w[1]], axis=-1)
        for w in (
            lax.dynamic_index_in_dim(stack, (seg + d) % segments, 0, keepdims=False)
            for d in range(segments)
        )
    ]
    moved = []
    for parity in range(2):
        moved.append([
            lax.ppermute(
                packed[d], "segment",
                [(i, (i + d) % segments) for i in range(parity, segments, 2)],
            )
            for d in range(1, segments)
        ])

    def layer_kernel(layer):
        options = [packed[0]] + moved[layer % 2]
        result = options[0]
        shift = (seg - layer) % segments
        for d in range(1, segments):
            result = jnp.where(shift == d, options[d], result)
        return result

    cells = lax.dynamic_slice_in_dim(inputs, seg * per_chunk, per_chunk, 1)
    cells = jnp.transpose(cells, (1, 0, 2, 3)).reshape(per_chunk * batch * depth, cols)
    cots = lax.dynamic_slice_in_dim(cotangent, seg * per_chunk, per_chunk, 1)
    cots = jnp.transpose(cots, (1, 0, 2)).reshape(per_chunk * batch, cols)
    weight_rows = c * c // space // cols
    share = lax.dynamic_index_in_dim(
        point_weight.reshape(space, weight_rows, cols), place, 0, keepdims=False
    )
    high = lax.reduce_precision(layer_bias[0], 8, 7)
    mid = lax.reduce_precision(layer_bias[0] - high, 8, 7)
    rest = layer_bias[0] - high - mid
    bias_row = jnp.concatenate([high, mid, rest, jnp.zeros((cols - 3 * c,), f32)]).astype(bf16)
    chunk = jnp.concatenate([cells, cots, share, bias_row[None]], axis=0)
    cot_row = per_chunk * batch * depth
    share_row = cot_row + per_chunk * batch
    bias_at = share_row + weight_rows
    chunk = jnp.pad(chunk, ((0, -chunk.shape[0] % 16), (0, 0)))

    def to_all(block):
        return lax.all_to_all(
            jnp.broadcast_to(block[None], (chunks,) + block.shape), both, 0, 0, tiled=True
        )

    grid_in = to_all(chunk)
    points = grid_in[:, share_row:bias_at].reshape(segments, c, c)
    bias_parts = grid_in[::space, bias_at, : 3 * c].astype(f32).reshape(segments, 3, c)
    biases = bias_parts[:, 0] + bias_parts[:, 1] + bias_parts[:, 2]
    blank = jnp.zeros((segments, c, c), bf16)

    def doubled(mats):
        return jnp.concatenate(
            [jnp.concatenate([mats, blank], axis=2), jnp.concatenate([blank, mats], axis=2)], axis=1
        )

    point_back = doubled(points)
    point_fwd = doubled(jnp.transpose(points, (0, 2, 1)))
    bias_cols = jnp.concatenate([biases] * batch, axis=1)[:, :, None]

    y_forward, y_inverse = np_y_tables(cols, mode_count)
    x_forward, x_inverse = np_x_tables(x_count, kx // 2)
    order = [(k % space) * owned + k // space for k in range(chunks)]

    def gathered(table):
        return jnp.asarray(table[order].reshape(2 * chunks, cols), bf16)

    def analysis(table):
        full = np.zeros((chunks, 16, cols))
        for k in range(chunks):
            s = k % space
            full[k, : 2 * owned] = table[s * owned : (s + 1) * owned].reshape(2 * owned, cols)
            full[k, 8:10] = table[order[k]]
        return lax.dynamic_index_in_dim(
            jnp.asarray(full, bf16), seg * space + place, 0, keepdims=False
        )

    inv_table, fwd_table = (gathered(y_inverse), gathered(y_forward))
    act_table, grad_table = (analysis(y_forward), analysis(y_inverse))
    xf = x_forward.transpose(0, 1, 3, 2).reshape(kx, 2, 2 * x_count)
    lx = np.concatenate(
        [np.concatenate([xf[:, 0], -xf[:, 1]], 1), np.concatenate([xf[:, 1], xf[:, 0]], 1)], 0
    )
    xz = xf.transpose(1, 0, 2).reshape(2 * kx, 2 * x_count)
    xi = x_inverse.transpose(1, 0, 3, 2).reshape(2 * x_count, 2 * kx)
    lx, xz, xi, xa, xb = (jnp.asarray(t, f32) for t in (lx, xz, xi, xi.T.copy(), xz.T.copy()))

    def whole(array):
        rank = len(array.shape)
        return pl.BlockSpec(array.shape, lambda *i: (0,) * rank)

    def call(kernel, args, blocked, outs, scratch, steps, name):
        def spec(array, is_blocked):
            if is_blocked:
                return pl.BlockSpec((array.shape[0] // steps,) + array.shape[1:], lambda i: (i, 0, 0))
            return whole(array)

        return pl.pallas_call(
            kernel,
            grid=(steps,),
            in_specs=[spec(a, n in blocked) for n, a in enumerate(args)],
            out_specs=[spec(a, is_blocked) for a, is_blocked in outs],
            out_shape=[a for a, _ in outs],
            scratch_shapes=scratch,
            compiler_params=pltpu.CompilerParams(vmem_limit_bytes=VMEM_LIMIT),
            name=name,
        )(*args)

    field = jax.ShapeDtypeStruct((x_count, bc, cols), bf16)
    ycoef = jax.ShapeDtypeStruct((x_count * 16, bc), f32)
    sent = jax.ShapeDtypeStruct((2 * x_count, bc), bf16)
    point = jax.ShapeDtypeStruct((bc, bc), f32)
    mode_scratch = [pltpu.VMEM((2 * batch * kx, 2 * c), f32)] * 2
    row_scratch = [pltpu.VMEM((chunks * 2 * x_count, bc), f32)]
    steps = 4

    zero = jnp.zeros_like(lift_weight.T)
    lift = jnp.concatenate(
        [jnp.concatenate([lift_weight.T, zero], 1), jnp.concatenate([zero, lift_weight.T], 1)], 0
    )
    lift_col = jnp.concatenate([lift_bias] * batch)[:, None]
    act, y0 = call(
        partial(lift_kernel, space=space, per_chunk=per_chunk, depth=batch * depth),
        (grid_in, lift, lift_col, act_table), (), [(field, False), (ycoef, False)], [], 1, "lift",
    )
    acts, slopes, ya = ([act], [], [y0])
    kernels = [layer_kernel(layer) for layer in range(segments)]
    (mine,) = call(
        first_modes_kernel, (y0, kernels[0], lx, xi), (), [(sent, False)], mode_scratch, 1, "modes"
    )
    for layer in range(1, segments):
        recv = to_all(mine)
        act, slope, y, mine = call(
            forward_kernel,
            (recv, acts[-1], point_fwd[layer - 1], bias_cols[layer - 1], inv_table, act_table,
             kernels[layer], lx, xi),
            (1,), [(field, True), (field, True), (ycoef, False), (sent, False)],
            row_scratch + mode_scratch, steps, "forward",
        )
        acts.append(act)
        slopes.append(slope)
        ya.append(y)

    recv = to_all(mine)
    last = segments - 1
    pre_grad, y, pg, mine = call(
        partial(top_kernel, space=space, per_chunk=per_chunk, first_row=cot_row, batch=batch),
        (recv, acts[last], grid_in, point_fwd[last], bias_cols[last], inv_table,
         proj_weight.T, proj_bias[:, None], proj_weight, out_weight.astype(f32)[:, None],
         grad_table, kernels[last], xa, xb),
        (1,), [(field, True), (ycoef, False), (point, False), (sent, False)],
        row_scratch + mode_scratch, steps, "top",
    )
    yg, pgs = ([y], [pg])
    for layer in reversed(range(last)):
        recv = to_all(mine)
        pre_grad, y, pg, mine = call(
            partial(backward_kernel, send=layer > 0),
            (recv, pre_grad, slopes[layer], acts[layer], point_back[layer + 1], fwd_table,
             grad_table, kernels[layer], xa, xb),
            (1, 2, 3), [(field, True), (ycoef, False), (point, False), (sent, False)],
            row_scratch + mode_scratch, steps, "backward",
        )
        yg.insert(0, y)
        pgs.insert(0, pg)

    scale = 1.0 / math.sqrt(batch * x_count * cols)
    pieces = ya + yg + pgs + [xz, xa]
    spectral, point_out = pl.pallas_call(
        partial(grads_kernel, layers=segments, scale=scale),
        grid=(owned,),
        in_specs=[pl.BlockSpec(memory_space=pltpu.SMEM)] + [whole(a) for a in pieces],
        out_specs=[
            pl.BlockSpec((1, kx, 2, c, c), lambda m: (m, 0, 0, 0, 0)),
            pl.BlockSpec((c, c), lambda m: (0, 0)),
        ],
        out_shape=[
            jax.ShapeDtypeStruct((owned, kx, 2, c, c), f32),
            jax.ShapeDtypeStruct((c, c), f32),
        ],
        scratch_shapes=[pltpu.VMEM((x_count * 16, bc), f32)] * 2
        + [pltpu.VMEM((2 * batch * kx, bc), f32)] * 2,
        compiler_params=pltpu.CompilerParams(vmem_limit_bytes=VMEM_LIMIT),
        name="grads",
    )(seg.astype(jnp.int32).reshape(1), *pieces)
    return (spectral[None], point_out[None])


def fits_replicated(mesh, inputs, point_weight, spectral_weight):
    segments, space = (mesh.shape["segment"], mesh.shape["space"])
    batch = inputs.shape[0] // mesh.shape["groups"]
    _, rows, depth, cols = inputs.shape
    layers, c, _ = point_weight.shape
    modes, kx = spectral_weight.shape[1:3]
    return (
        batch == 2
        and batch * c == 128
        and layers == segments
        and segments * space <= 16
        and modes == segments * space
        and modes // space <= 4
        and rows % (segments * space) == 0
        and rows % 32 == 0
        and rows <= 64
        and kx % 16 == 0
        and kx <= 64
        and batch * depth == 16
        and cols % 128 == 0
        and cols >= 3 * c
        and c * c % (space * cols) == 0
    )


def solution(mesh):
    in_specs = (
        P("groups", "space", None, None),
        P("groups", "space", None),
        P(),
        P(),
        P("segment", None, None),
        P("segment", None),
        P("segment", "space", None, None, None, None),
        P(),
        P(),
        P(),
    )
    out_specs = (
        P(("groups", "segment"), "space", None, None, None, None),
        P(("groups", "segment"), None, None),
    )

    def step(inputs, cotangent, lift_weight, lift_bias, point_weight, layer_bias, spectral_weight, *rest):
        fits = fits_replicated(mesh, inputs, point_weight, spectral_weight)
        mapped = jax.shard_map(
            replicated if fits else on_device,
            mesh=mesh, in_specs=in_specs, out_specs=out_specs, check_vma=False,
        )
        return mapped(
            inputs, cotangent, lift_weight, lift_bias, point_weight, layer_bias, spectral_weight, *rest
        )

    return step
```

```python
from functools import partial
import math

import jax
import jax.numpy as jnp
import numpy as np
from jax import lax
from jax.experimental import pallas as pl
from jax.experimental.pallas import tpu as pltpu
from jax.sharding import PartitionSpec as P

highest = lax.Precision.HIGHEST


def as_sent(array):
    return jax.tree.map(lambda a: a.astype(jnp.bfloat16) if a.dtype == jnp.float32 else a, array)


def passed_along(block, axis, distance):
    devices = range(lax.axis_size(axis))
    route = [(i - distance, i) for i in devices if i - distance in devices]
    return lax.ppermute(block, axis, route)


def y_tables(col_count, mode_count):
    ycells = jnp.arange(col_count, dtype=jnp.int32)[:, None]
    ymodes = jnp.arange(mode_count, dtype=jnp.int32)[None, :]
    angles = (ycells * ymodes % col_count).astype(jnp.float32) * (2.0 * math.pi / col_count)
    factor = 1.0 / math.sqrt(col_count)
    forward = jnp.stack([jnp.cos(angles), -jnp.sin(angles)], axis=1) * factor
    doubled = jnp.where(ymodes == 0, 1.0, 2.0).astype(jnp.float32)
    inverse = jnp.stack([doubled * jnp.cos(angles), -doubled * jnp.sin(angles)], axis=0) * factor
    return (forward.astype(jnp.bfloat16), jnp.transpose(inverse, (0, 2, 1)).astype(jnp.bfloat16))


def x_tables(row_total, mode_count):
    kx_count = 2 * mode_count
    indices = jnp.arange(kx_count, dtype=jnp.int32)
    freq_values = jnp.where(indices < mode_count, indices, indices - kx_count)
    xcells = jnp.arange(row_total, dtype=jnp.int32)
    angles = (freq_values[:, None] * xcells[None, :] % row_total).astype(jnp.float32) * (
        2.0 * math.pi / row_total
    )
    factor = 1.0 / math.sqrt(row_total)
    cosine_part = jnp.cos(angles) * factor
    sine_part = jnp.sin(angles) * factor
    forward = jnp.stack(
        [jnp.stack([cosine_part, sine_part], -1), jnp.stack([-sine_part, cosine_part], -1)], axis=1
    )
    cosine_flip = cosine_part.T
    sine_flip = sine_part.T
    inverse = jnp.stack(
        [jnp.stack([cosine_flip, -sine_flip], -1), jnp.stack([sine_flip, cosine_flip], -1)], axis=1
    )
    return (forward, inverse)


def mode_mult(coeffs, kernel):
    real_in, imag_in = (coeffs[:, :, 0], coeffs[:, :, 1])
    real_kernel, imag_kernel = (kernel[:, :, 0], kernel[:, :, 1])
    product = partial(jnp.einsum, "mjc,mjco->mjo", precision=highest)
    real_out = product(real_in, real_kernel) - product(imag_in, imag_kernel)
    imag_out = product(real_in, imag_kernel) + product(imag_in, real_kernel)
    return jnp.stack([real_out, imag_out], axis=2)


def mode_back(coeffs, mode_grads, kernel):
    real_in, imag_in = (coeffs[:, :, 0], coeffs[:, :, 1])
    real_grad, imag_grad = (mode_grads[:, :, 0], mode_grads[:, :, 1])
    real_kernel, imag_kernel = (kernel[:, :, 0], kernel[:, :, 1])
    outer_sum = partial(jnp.einsum, "mjc,mjo->mjco", precision=highest)
    inner_sum = partial(jnp.einsum, "mjo,mjco->mjc", precision=highest)
    kernel_real = outer_sum(real_in, real_grad) + outer_sum(imag_in, imag_grad)
    kernel_imag = outer_sum(real_in, imag_grad) - outer_sum(imag_in, real_grad)
    coeff_real = inner_sum(real_grad, real_kernel) + inner_sum(imag_grad, imag_kernel)
    coeff_imag = inner_sum(imag_grad, real_kernel) - inner_sum(real_grad, imag_kernel)
    return (
        jnp.stack([kernel_real, kernel_imag], axis=2),
        jnp.stack([coeff_real, coeff_imag], axis=2),
    )


def gelu_grad(pre_act, upstream):
    _, pullback = jax.vjp(jax.nn.gelu, pre_act)
    return pullback(upstream)[0]


def store_slot(buffer, value, slot_clip, is_valid):
    previous = lax.dynamic_index_in_dim(buffer, slot_clip, 0, keepdims=False)
    return lax.dynamic_update_index_in_dim(
        buffer, jnp.where(is_valid, value, previous), slot_clip, 0
    )


def on_device(
    inputs,
    cotangent,
    lift_weight,
    lift_bias,
    point_weight,
    layer_bias,
    spectral_weight,
    proj_weight,
    proj_bias,
    out_weight,
):
    batch_count, row_count, _, col_count = inputs.shape
    segment_count = lax.axis_size("segment")
    segment_index = lax.axis_index("segment")
    space_count = lax.axis_size("space")
    owned_modes = spectral_weight.shape[1]
    kx_count = spectral_weight.shape[2]
    channels = point_weight.shape[1]
    mode_count = kx_count // 2
    y_forward, y_inverse = y_tables(col_count, mode_count)
    x_forward, x_inverse = x_tables(row_count * space_count, mode_count)
    x_forward_adj = jnp.transpose(x_forward, (2, 3, 0, 1))
    x_inverse_adj = jnp.transpose(x_inverse, (2, 3, 0, 1))
    y_forward_wide = y_forward.astype(jnp.float32)
    y_inverse_wide = y_inverse.astype(jnp.float32)
    kernel = spectral_weight[0].astype(jnp.float32)
    point_matrix = point_weight[0]
    bias_vector = layer_bias[0]
    tick_count = batch_count + segment_count - 1

    def to_owners(y_coeffs, x_table):
        exchanged = lax.all_to_all(
            y_coeffs.astype(jnp.bfloat16), "space", split_axis=1, concat_axis=0, tiled=True
        ).astype(y_coeffs.dtype)
        return jnp.einsum("jqxp,xmpc->mjqc", x_table, exchanged, precision=highest)

    def from_owners(owned, x_table):
        spread = jnp.einsum("xpjq,mjqc->xmpc", x_table, owned, precision=highest)
        return lax.all_to_all(
            as_sent(spread), "space", split_axis=0, concat_axis=1, tiled=True
        ).astype(spread.dtype)

    def lifted(pick_slot):
        sample = lax.dynamic_index_in_dim(inputs, pick_slot, 0, keepdims=False)
        mixed = jnp.einsum("xty,tc->xcy", sample, lift_weight, preferred_element_type=jnp.float32)
        return (mixed + lift_bias[None, :, None]).astype(jnp.bfloat16)

    def forward_tick(state_now, tick_now):
        incoming, pre_store, act_store, mode_store = state_now
        pick_slot = jnp.clip(tick_now, 0, batch_count - 1)
        layer_in = lax.cond(segment_index == 0, lambda: lifted(pick_slot), lambda: incoming)
        y_coeffs = jnp.einsum(
            "xcy,ypm->xmpc", layer_in, y_forward, preferred_element_type=jnp.float32
        )
        coeffs = to_owners(y_coeffs, x_forward)
        back_rows = from_owners(mode_mult(coeffs, kernel), x_inverse)
        branch = jnp.einsum("xmpc,pmy->xcy", back_rows, y_inverse_wide, precision=highest)
        pointwise = jnp.einsum(
            "xcy,co->xoy", layer_in, point_matrix, preferred_element_type=jnp.float32
        )
        pre_act = pointwise + branch + bias_vector[None, :, None]
        slot_index = tick_now - segment_index
        is_valid = (slot_index >= 0) & (slot_index < batch_count)
        slot_clip = jnp.clip(slot_index, 0, batch_count - 1)
        pre_store = store_slot(pre_store, pre_act, slot_clip, is_valid)
        act_store = store_slot(act_store, layer_in, slot_clip, is_valid)
        mode_store = store_slot(mode_store, coeffs, slot_clip, is_valid)
        layer_out = jax.nn.gelu(pre_act).astype(jnp.bfloat16)
        sent = passed_along(layer_out, "segment", 1)
        return ((sent, pre_store, act_store, mode_store), None)

    start_state = (
        jnp.zeros((row_count, channels, col_count), jnp.bfloat16),
        jnp.zeros((batch_count, row_count, channels, col_count), jnp.float32),
        jnp.zeros((batch_count, row_count, channels, col_count), jnp.bfloat16),
        jnp.zeros((batch_count, owned_modes, kx_count, 2, channels), jnp.float32),
    )
    final_state, _ = lax.scan(forward_tick, start_state, jnp.arange(tick_count, dtype=jnp.int32))
    _, pre_store, act_store, mode_store = final_state

    def top_grad(slot_clip, pre_act):
        top_act = jax.nn.gelu(pre_act).astype(jnp.bfloat16)
        hidden = jnp.einsum("xcy,ck->xky", top_act, proj_weight, preferred_element_type=jnp.float32)
        hidden = hidden + proj_bias[None, :, None]
        target = lax.dynamic_index_in_dim(cotangent, slot_clip, 0, keepdims=False)
        upstream = (
            out_weight.astype(jnp.float32)[None, :, None] * target.astype(jnp.float32)[:, None, :]
        )
        hidden_grad = gelu_grad(hidden, upstream).astype(jnp.bfloat16)
        return jnp.einsum(
            "xky,ck->xcy", hidden_grad, proj_weight, preferred_element_type=jnp.float32
        ).astype(jnp.bfloat16)

    def backward_tick(state_now, tick_now):
        incoming, point_sum, kernel_sum = state_now
        slot_index = tick_now - (segment_count - 1 - segment_index)
        is_valid = (slot_index >= 0) & (slot_index < batch_count)
        slot_clip = jnp.clip(slot_index, 0, batch_count - 1)
        pre_act = lax.dynamic_index_in_dim(pre_store, slot_clip, 0, keepdims=False)
        layer_in = lax.dynamic_index_in_dim(act_store, slot_clip, 0, keepdims=False)
        coeffs = lax.dynamic_index_in_dim(mode_store, slot_clip, 0, keepdims=False)
        grad_out = lax.cond(
            segment_index == segment_count - 1,
            lambda: top_grad(slot_clip, pre_act),
            lambda: incoming,
        )
        pre_grad = gelu_grad(pre_act, grad_out.astype(jnp.float32)).astype(jnp.bfloat16)
        point_term = jnp.einsum(
            "xcy,xoy->co", layer_in, pre_grad, preferred_element_type=jnp.float32
        )
        y_grads = jnp.einsum(
            "xoy,pmy->xmpo", pre_grad, y_inverse, preferred_element_type=jnp.float32
        )
        mode_grads = to_owners(y_grads, x_inverse_adj)
        kernel_step, coeff_step = mode_back(coeffs, mode_grads, kernel)
        back_rows = from_owners(coeff_step, x_forward_adj)
        back_branch = jnp.einsum("xmpc,ypm->xcy", back_rows, y_forward_wide, precision=highest)
        pointwise_back = jnp.einsum(
            "co,xoy->xcy", point_matrix, pre_grad, preferred_element_type=jnp.float32
        )
        grad_in = (pointwise_back + back_branch).astype(jnp.bfloat16)
        point_sum = point_sum + jnp.where(is_valid, point_term, 0.0)
        kernel_sum = kernel_sum + jnp.where(is_valid, kernel_step, 0.0)
        sent = passed_along(grad_in, "segment", -1)
        return ((sent, point_sum, kernel_sum), None)

    back_start = (
        jnp.zeros((row_count, channels, col_count), jnp.bfloat16),
        jnp.zeros((channels, channels), jnp.float32),
        jnp.zeros((owned_modes, kx_count, 2, channels, channels), jnp.float32),
    )
    back_state, _ = lax.scan(backward_tick, back_start, jnp.arange(tick_count, dtype=jnp.int32))
    _, point_sum, kernel_sum = back_state
    point_total = lax.psum(point_sum, "space")
    factor = 1.0 / math.sqrt(batch_count * row_count * space_count * col_count)
    return (kernel_sum[None], (point_total * factor)[None])


f32, bf16 = (jnp.float32, jnp.bfloat16)
NT = (((1,), (1,)), ((), ()))
NN = (((1,), (0,)), ((), ()))
STEPS = 2
VMEM_LIMIT = 48 << 20


def np_y_tables(col_count, mode_count):
    ycells = np.arange(col_count)[:, None]
    ymodes = np.arange(mode_count)[None, :]
    angles = (ycells * ymodes % col_count) * (2.0 * math.pi / col_count)
    factor = 1.0 / math.sqrt(col_count)
    doubled = np.where(ymodes == 0, 1.0, 2.0)
    forward = np.stack([np.cos(angles), -np.sin(angles)], axis=0) * factor
    inverse = np.stack([doubled * np.cos(angles), -doubled * np.sin(angles)], axis=0) * factor
    return (forward.transpose(2, 0, 1), inverse.transpose(2, 0, 1))


def np_x_tables(row_total, mode_count):
    kx_count = 2 * mode_count
    indices = np.arange(kx_count)
    freq = np.where(indices < mode_count, indices, indices - kx_count)
    angles = (freq[:, None] * np.arange(row_total)[None, :] % row_total) * (2.0 * math.pi / row_total)
    factor = 1.0 / math.sqrt(row_total)
    c, s = (np.cos(angles) * factor, np.sin(angles) * factor)
    forward = np.stack([np.stack([c, s], -1), np.stack([-s, c], -1)], axis=1)
    inverse = np.stack([np.stack([c.T, -s.T], -1), np.stack([s.T, c.T], -1)], axis=1)
    return (forward, inverse)


def hdot(a, b):
    return jnp.dot(a, b, precision=highest, preferred_element_type=f32)


def gelu_both(v):
    k0 = math.sqrt(2.0 / math.pi)
    k1 = k0 * 0.044715
    v2 = v * v
    share = 0.5 + 0.5 * jnp.tanh(v * (k0 + k1 * v2))
    value = v * share
    slope = share + value * (1.0 - share) * (2.0 * k0 + (6.0 * k1) * v2)
    return (value, slope)


def low_half(shape):
    return lax.broadcasted_iota(jnp.int32, shape, 1) < shape[1] // 2


def swap_halves(a):
    return pltpu.roll(a, a.shape[1] // 2, 1)


def cross(a, b):
    low = low_half(a.shape)
    return (jnp.where(low, a, swap_halves(b)), jnp.where(low, swap_halves(a), b))


def grid_rows(first_ref, first, second_ref, second, x_half):
    parts = []
    for p in range(2):
        parts += cross(
            first_ref[pl.ds(first + p, x_half, stride=16), :],
            second_ref[pl.ds(second + p, x_half, stride=16), :],
        )
    return jnp.concatenate(parts, axis=0)


def own_grid(y_ref, row=8):
    return grid_rows(y_ref, row, y_ref, row + 2, y_ref.shape[0] // 16)


def put_chunk(grid, out_ref, first=0):
    x_half = grid.shape[0] // 4
    for p in range(2):
        base = 2 * p * x_half
        pair = cross(grid[base : base + x_half], grid[base + x_half : base + 2 * x_half])
        for mode in range(2):
            at = first + (2 * mode + p) * x_half
            block = pair[mode].astype(bf16)
            for k in range(out_ref.shape[0]):
                out_ref[k, at : at + x_half] = block


def put_split(t_ref, mode, rows):
    count = rows.shape[0]
    high = rows.astype(bf16).astype(f32)
    t_ref[2 * mode * count : (2 * mode + 1) * count] = high
    t_ref[(2 * mode + 1) * count : (2 * mode + 2) * count] = rows - high


def mode_products(t_ref, w_ref, m_ref, dims, start=0):
    pairs = w_ref.shape[1]
    for j in range(pairs):
        for mode in range(2):
            at = pl.ds(mode * 8 * pairs + j, 8, stride=pairs)
            m_ref[at, :] = lax.dot_general(
                t_ref[at, :].astype(bf16), w_ref[start + mode, j], dims, preferred_element_type=f32
            )
    count = 4 * pairs
    return [
        m_ref[2 * mode * count : (2 * mode + 1) * count]
        + m_ref[(2 * mode + 1) * count : (2 * mode + 2) * count]
        for mode in range(2)
    ]


def first_kx(shape, pairs):
    return (lax.broadcasted_iota(jnp.int32, shape, 0) // pairs) % 2 == 0


def forward_modes(y_ref, w_ref, lx_ref, xi_ref, t_ref, m_ref, out_ref, row=8, start=0):
    pairs = w_ref.shape[1]
    ys = own_grid(y_ref, row)
    sw = swap_halves(ys)
    low = low_half(ys.shape)
    zero = jnp.zeros_like(ys)
    put_split(t_ref, 0, hdot(lx_ref[...], jnp.concatenate([jnp.where(low, ys, zero), jnp.where(low, zero, sw)], axis=0)))
    put_split(t_ref, 1, hdot(lx_ref[...], jnp.concatenate([jnp.where(low, sw, zero), jnp.where(low, zero, ys)], axis=0)))
    m0, m1 = mode_products(t_ref, w_ref, m_ref, NN, start)
    first = first_kx(m0.shape, pairs)
    s0 = jnp.where(first, m0, swap_halves(m0))
    s1 = jnp.where(first, swap_halves(m1), m1)
    first_row = start * out_ref.shape[1] // w_ref.shape[0]
    put_chunk(hdot(xi_ref[...], jnp.where(low_half(m0.shape), s0, s1)), out_ref, first_row)


def backward_modes(y_ref, w_ref, xa_ref, xf_ref, t_ref, m_ref, out_ref):
    pairs = w_ref.shape[1]
    g = hdot(xa_ref[...], own_grid(y_ref))
    sw = swap_halves(g)
    first = first_kx(g.shape, pairs)
    keep = low_half(g.shape) == first
    zero = jnp.zeros_like(g)
    put_split(t_ref, 0, jnp.where(keep, jnp.where(first, g, sw), zero))
    put_split(t_ref, 1, jnp.where(keep, jnp.where(first, sw, g), zero))
    m0, m1 = mode_products(t_ref, w_ref, m_ref, NT)
    half = 2 * pairs
    pr0, pi0, pr1, pi1 = (m0[:half], m0[half:], m1[:half], m1[half:])
    low = low_half(pr0.shape)
    real = jnp.where(low, pr0 + swap_halves(pi0), swap_halves(pr1) + pi1)
    imag = jnp.where(low, pi0 - swap_halves(pr0), swap_halves(pi1) - pr1)
    put_chunk(hdot(xf_ref[...], jnp.concatenate([real, imag], axis=0)), out_ref)


def choose_kernel(seg_ref, layer, w_refs, w_ref, sem, start):
    for seg in range(4):
        pair = seg // 2
        source = w_refs[(0 if seg % 2 == layer % 2 else 1) + (0 if pair == layer // 2 else 2)]
        if pair == layer // 2:
            source = source.at[2 * pair : 2 * pair + 2]

        @pl.when(seg_ref[0] == seg)
        def _(source=source):
            copy = pltpu.make_async_copy(source, w_ref, sem)
            if start:
                copy.start()
            else:
                copy.wait()


def choose_all(seg_ref, w_refs, w_ref, sem, start):
    for lane in range(2):
        @pl.when(seg_ref[0] % 2 == lane)
        def _(lane=lane):
            copy = pltpu.make_async_copy(w_refs[lane], w_ref, sem)
            if start:
                copy.start()
            else:
                copy.wait()


def pack_kernel(in_ref, out_ref):
    out_ref[...] = jnp.concatenate([in_ref[:, 0], in_ref[:, 1]], axis=-1)


def widen(recv_ref, r_ref):
    chunks, rows, _ = recv_ref.shape
    for k in range(chunks):
        r_ref[k * rows : (k + 1) * rows] = recv_ref[k].astype(f32)


def row_product(weight, field, r_ref, table, x, x_half):
    rows = r_ref[pl.ds(x, table.shape[0], stride=x_half), :]
    lhs = jnp.concatenate([weight, rows.T.astype(bf16)], axis=1)
    return jnp.dot(lhs, jnp.concatenate([field, table], axis=0), preferred_element_type=f32)


def chunk_of(x, half_side, space, rows, per_chunk):
    inner = x % rows
    return ((inner // per_chunk) * space + half_side * (space // 2) + x // rows, inner % per_chunk)


def lift_kernel(in_ref, lw_ref, lb_ref, tab_ref, act_ref, y_ref, *, space, rows, per_chunk, depth):
    for x in range(act_ref.shape[0]):
        cells = []
        for side in range(2):
            k, i = chunk_of(x, side, space, rows, per_chunk)
            cells.append(in_ref[k, i * depth : (i + 1) * depth, :])
        cells = jnp.concatenate(cells, axis=0)
        act = jnp.dot(lw_ref[...], cells, preferred_element_type=f32) + lb_ref[...]
        act = act.astype(bf16)
        act_ref[x] = act
        y_ref[x * 16 : (x + 1) * 16] = lax.dot_general(
            tab_ref[...], act, NT, preferred_element_type=f32
        )


def first_modes_kernel(seg_ref, y_ref, lx_ref, xi_ref, w0, w1, out_ref, w_ref, sem, t_ref, m_ref):
    choose_all(seg_ref, (w0, w1), w_ref, sem, True)
    choose_all(seg_ref, (w0, w1), w_ref, sem, False)
    for start in range(0, w_ref.shape[0], 2):
        forward_modes(y_ref, w_ref, lx_ref, xi_ref, t_ref, m_ref, out_ref, 2 * start, start)


def forward_kernel(
    seg_ref, recv_ref, act_ref, pw_ref, pb_ref, inv_ref, tab_ref, lx_ref, xi_ref, w0, w1, w2, w3,
    next_ref, slope_ref, y_ref, out_ref, w_ref, sem, t_ref, m_ref, r_ref, *, layer,
):
    step = pl.program_id(0)
    block = act_ref.shape[0]
    x_half = y_ref.shape[0] // 16

    @pl.when(step == 0)
    def _():
        choose_kernel(seg_ref, layer, (w0, w1, w2, w3), w_ref, sem, True)
        widen(recv_ref, r_ref)

    def one(i, carry):
        x = step * block + i
        pre = row_product(pw_ref[layer - 1], act_ref[i], r_ref, inv_ref[...], x, x_half)
        pre = pre + pb_ref[layer - 1]
        value, slope = gelu_both(pre)
        value = value.astype(bf16)
        next_ref[i] = value
        slope_ref[i] = slope.astype(bf16)
        y_ref[pl.ds(pl.multiple_of(x * 16, 16), 16), :] = lax.dot_general(
            tab_ref[...], value, NT, preferred_element_type=f32
        )
        return carry

    lax.fori_loop(0, block, one, 0, unroll=2)

    @pl.when(step == pl.num_programs(0) - 1)
    def _():
        choose_kernel(seg_ref, layer, (w0, w1, w2, w3), w_ref, sem, False)
        forward_modes(y_ref, w_ref, lx_ref, xi_ref, t_ref, m_ref, out_ref)


def adjoint_rows(x, i, grad, act, tab_ref, pre_ref, y_ref, point_ref):
    pre_grad = grad.astype(bf16)
    pre_ref[i] = pre_grad
    both = lax.dot_general(
        jnp.concatenate([tab_ref[...], act], axis=0), pre_grad, NT, preferred_element_type=f32
    )
    y_ref[pl.ds(pl.multiple_of(x * 16, 16), 16), :] = both[:16]
    point_ref[...] += both[16:]


def top_kernel(
    seg_ref, recv_ref, act_ref, in_ref, pw_ref, pb_ref, inv_ref, up_ref, hb_ref, down_ref, ow_ref,
    tab_ref, xa_ref, xf_ref, w0, w1, w2, w3,
    pre_ref, y_ref, point_ref, out_ref, w_ref, sem, t_ref, m_ref, r_ref,
    *, layer, space, rows, per_chunk, first_row,
):
    step = pl.program_id(0)
    block = act_ref.shape[0]
    x_half = y_ref.shape[0] // 16

    @pl.when(step == 0)
    def _():
        choose_kernel(seg_ref, layer, (w0, w1, w2, w3), w_ref, sem, True)
        widen(recv_ref, r_ref)
        point_ref[...] = jnp.zeros_like(point_ref)

    def one(i, carry):
        x = step * block + i
        act = act_ref[i]
        pre = row_product(pw_ref[layer], act, r_ref, inv_ref[...], x, x_half) + pb_ref[layer]
        value, slope = gelu_both(pre)
        value = value.astype(bf16)
        grads = []
        size = value.shape[0] // 2
        for side in range(2):
            hidden = jnp.dot(
                up_ref[...], value[side * size : (side + 1) * size], preferred_element_type=f32
            )
            _, hidden_slope = gelu_both(hidden + hb_ref[...])
            chunk, within = chunk_of(x, side, space, rows, per_chunk)
            cots = in_ref[chunk, first_row : first_row + per_chunk, :].astype(f32)
            cot = cots[:1]
            for other in range(1, per_chunk):
                cot = jnp.where(within == other, cots[other : other + 1], cot)
            grads.append(
                cot * jnp.dot(
                    down_ref[...], (hidden_slope * ow_ref[...]).astype(bf16), preferred_element_type=f32
                )
            )
        grad = jnp.concatenate(grads, axis=0)
        adjoint_rows(x, i, grad * slope, act, tab_ref, pre_ref, y_ref, point_ref)
        return carry

    lax.fori_loop(0, block, one, 0)

    @pl.when(step == pl.num_programs(0) - 1)
    def _():
        choose_kernel(seg_ref, layer, (w0, w1, w2, w3), w_ref, sem, False)
        backward_modes(y_ref, w_ref, xa_ref, xf_ref, t_ref, m_ref, out_ref)


def backward_kernel(
    seg_ref, recv_ref, grad_ref, slope_ref, act_ref, pw_ref, fwd_ref, tab_ref, xa_ref, xf_ref,
    w0, w1, w2, w3,
    pre_ref, y_ref, point_ref, out_ref, w_ref, sem, t_ref, m_ref, r_ref, *, layer,
):
    step = pl.program_id(0)
    block = act_ref.shape[0]
    x_half = y_ref.shape[0] // 16

    @pl.when(step == 0)
    def _():
        if layer:
            choose_kernel(seg_ref, layer, (w0, w1, w2, w3), w_ref, sem, True)
        widen(recv_ref, r_ref)
        point_ref[...] = jnp.zeros_like(point_ref)

    def one(i, carry):
        x = step * block + i
        grad = row_product(pw_ref[layer + 1], grad_ref[i], r_ref, fwd_ref[...], x, x_half)
        adjoint_rows(
            x, i, grad * slope_ref[i].astype(f32), act_ref[i], tab_ref, pre_ref, y_ref, point_ref
        )
        return carry

    lax.fori_loop(0, block, one, 0, unroll=2)

    @pl.when(step == pl.num_programs(0) - 1)
    def _():
        if layer:
            choose_kernel(seg_ref, layer, (w0, w1, w2, w3), w_ref, sem, False)
            backward_modes(y_ref, w_ref, xa_ref, xf_ref, t_ref, m_ref, out_ref)
        else:
            out_ref[...] = jnp.zeros_like(out_ref)


def pick_kernel(seg_ref, *refs, layers):
    ya_refs, yg_refs, pg_refs = (refs[:layers], refs[layers : 2 * layers], refs[2 * layers : 3 * layers])
    count = ya_refs[0].shape[0]
    seg = seg_ref[0]
    partner = seg + 1 - 2 * (seg % 2)
    for out_ref, wanted in zip(refs[3 * layers :], (seg, partner)):
        for layer in range(layers):
            @pl.when(wanted == layer)
            def _(layer=layer, out_ref=out_ref):
                out_ref[:count] = ya_refs[layer][...]
                out_ref[count : 2 * count] = yg_refs[layer][...]
                pg = pg_refs[layer][...]
                half = pg.shape[0] // 2
                out_ref[2 * count :] = pg[:half] + swap_halves(pg[half:])


def grads_kernel(mine_ref, theirs_ref, xz_ref, xa_ref, out_ref, point_ref, a_ref, b_ref, *, scale):
    mode = pl.program_id(0)
    c = point_ref.shape[0]
    count = (mine_ref.shape[0] - c) // 2
    x_half = count // 16

    @pl.when(mode == 0)
    def _():
        point_ref[...] = (mine_ref[2 * count :, :c] + theirs_ref[2 * count :, :c]) * scale

    z = hdot(xz_ref[...], grid_rows(mine_ref, 2 * mode, theirs_ref, 2 * mode, x_half))
    at = count + 2 * mode
    g = hdot(xa_ref[...], grid_rows(mine_ref, at, theirs_ref, at, x_half))
    rows = z.shape[0]
    kx = rows // 2
    zs, gs = (swap_halves(z), swap_halves(g))
    a_ref[:rows] = z
    a_ref[rows:] = zs
    low = low_half((kx, z.shape[1]))
    b_ref[:kx] = jnp.where(low, g[:kx], gs[kx:])
    b_ref[kx:rows] = jnp.where(low, g[kx:], -gs[:kx])
    b_ref[rows : rows + kx] = jnp.where(low, gs[:kx], g[kx:])
    b_ref[rows + kx :] = jnp.where(low, gs[kx:], -g[:kx])
    for j in range(kx):
        a = a_ref[pl.ds(j, 4, stride=kx), :][:, :c]
        b = b_ref[pl.ds(j, 4, stride=kx), :]
        ah, bh = (a.astype(bf16).astype(f32), b.astype(bf16).astype(f32))
        left = jnp.concatenate([ah, a - ah, ah], axis=0).T.astype(bf16)
        right = jnp.concatenate([bh, bh, b - bh], axis=0).astype(bf16)
        out_ref[0, j, 0] = jnp.dot(left, right[:, :c], preferred_element_type=f32)
        out_ref[0, j, 1] = jnp.dot(left, right[:, c:], preferred_element_type=f32)


def replicated(
    inputs, cotangent, lift_weight, lift_bias, point_weight, layer_bias, spectral_weight,
    proj_weight, proj_bias, out_weight,
):
    batch, row_count, depth, cols = inputs.shape
    segments, space = (lax.axis_size("segment"), lax.axis_size("space"))
    seg, place = (lax.axis_index("segment"), lax.axis_index("space"))
    pair = seg // 2
    both = ("segment", "space")
    owned, kx = spectral_weight.shape[1:3]
    c = point_weight.shape[1]
    x_count = row_count * space
    x_half = x_count // 2
    mode_count = owned * space
    per_chunk = row_count // segments
    pairs = kx // 2
    group = segments // 2 * space

    stack = spectral_weight[0].reshape(owned, 2, pairs, 2 * c, c)
    own = pl.pallas_call(
        pack_kernel,
        grid=(owned,),
        in_specs=[pl.BlockSpec((1, 2, pairs, 2 * c, c), lambda m: (m, 0, 0, 0, 0))],
        out_specs=pl.BlockSpec((1, pairs, 2 * c, 2 * c), lambda m: (m, 0, 0, 0)),
        out_shape=jax.ShapeDtypeStruct((owned, pairs, 2 * c, 2 * c), bf16),
        compiler_params=pltpu.CompilerParams(vmem_limit_bytes=VMEM_LIMIT),
        name="pack",
    )(stack)
    swap = [(0, 1), (1, 0), (2, 3), (3, 2)]
    neighbour = lax.ppermute(own, "segment", swap)
    away = lax.dynamic_slice_in_dim(own, 2 * (1 - pair), 2, 0)
    across_odd = lax.ppermute(away, "segment", [(1, 3), (3, 1)])

    cells = lax.dynamic_slice_in_dim(inputs, seg * per_chunk, per_chunk, 1)
    cells = cells.reshape(batch, per_chunk * depth, cols)
    cots = lax.dynamic_slice_in_dim(cotangent, seg * per_chunk, per_chunk, 1)
    weight_rows = c * c // space // cols
    share = lax.dynamic_index_in_dim(
        point_weight.reshape(space, weight_rows, cols), place, 0, keepdims=False
    )
    high = lax.reduce_precision(layer_bias[0], 8, 7)
    mid = lax.reduce_precision(layer_bias[0] - high, 8, 7)
    rest = layer_bias[0] - high - mid
    bias_row = jnp.concatenate([high, mid, rest, jnp.zeros((cols - 3 * c,), f32)]).astype(bf16)
    common = jnp.concatenate([share, bias_row[None]], axis=0)
    chunk = jnp.concatenate([cells, cots, jnp.broadcast_to(common[None], (batch,) + common.shape)], axis=1)
    cot_row = per_chunk * depth
    share_row = cot_row + per_chunk
    bias_at = share_row + weight_rows
    chunk = jnp.pad(chunk, ((0, 0), (0, -chunk.shape[1] % 8), (0, 0)))
    chunk = jnp.broadcast_to(chunk[None, :, None], (segments // 2, batch, space) + chunk.shape[1:])
    grid_in = lax.all_to_all(
        chunk.reshape((segments * space,) + chunk.shape[3:]), both, 0, 0, tiled=True
    )
    across_odd_on = lax.ppermute(across_odd, "segment", [(1, 0), (3, 2)])

    def weights_of(layer):
        if layer % 2:
            return (own, neighbour, across_odd, across_odd_on)
        return (own, neighbour, across_even, across_even_on)

    points = grid_in[:, share_row:bias_at].reshape(segments, c, c)
    bias_parts = grid_in[::space, bias_at, : 3 * c].astype(f32).reshape(segments, 3, c)
    biases = bias_parts[:, 0] + bias_parts[:, 1] + bias_parts[:, 2]
    blank = jnp.zeros((segments, c, c), bf16)

    def doubled(mats):
        return jnp.concatenate(
            [jnp.concatenate([mats, blank], axis=2), jnp.concatenate([blank, mats], axis=2)], axis=1
        )

    point_back = doubled(points)
    point_fwd = doubled(jnp.transpose(points, (0, 2, 1)))
    bias_cols = jnp.concatenate([biases] * 2, axis=1)[:, :, None]

    y_forward, y_inverse = np_y_tables(cols, mode_count)
    x_forward, x_inverse = np_x_tables(x_count, kx // 2)
    firsts = [k % space * owned + k // space * 2 for k in range(group)]
    order = [first + i for first in firsts for i in range(2)]

    def gathered(table):
        return jnp.asarray(table[order].reshape(4 * group, cols), bf16)

    def analysis(table):
        full = np.zeros((group, 16, cols))
        for k in range(group):
            s = k % space
            full[k, : 2 * owned] = table[s * owned : (s + 1) * owned].reshape(2 * owned, cols)
            full[k, 8:12] = table[firsts[k] : firsts[k] + 2].reshape(4, cols)
        return lax.dynamic_index_in_dim(
            jnp.asarray(full, bf16), pair * space + place, 0, keepdims=False
        )

    inv_table, fwd_table = (gathered(y_inverse), gathered(y_forward))
    act_table, grad_table = (analysis(y_forward), analysis(y_inverse))
    xf = x_forward.transpose(0, 1, 3, 2).reshape(kx, 2, 2 * x_count)
    lx = np.concatenate(
        [np.concatenate([xf[:, 0], -xf[:, 1]], 1), np.concatenate([xf[:, 1], xf[:, 0]], 1)], 0
    )
    xz = xf.transpose(1, 0, 2).reshape(2 * kx, 2 * x_count)
    xi = x_inverse.transpose(1, 0, 3, 2).reshape(2 * x_count, 2 * kx)
    lx, xz, xi, xa, xb = (jnp.asarray(t, f32) for t in (lx, xz, xi, xi.T.copy(), xz.T.copy()))

    device_lists = [
        [(2 * k + lane) * space + s for k in range(segments // 2) for s in range(space)]
        for lane in range(2)
    ]

    def to_all(block):
        return lax.all_to_all(block, both, 0, 0, tiled=True, axis_index_groups=device_lists)

    def whole(array):
        rank = len(array.shape)
        return pl.BlockSpec(array.shape, lambda *i: (0,) * rank)

    seg_scalar = seg.astype(jnp.int32).reshape(1)

    def call(kernel, args, blocked, weights, outs, scratch, steps, name):
        def spec(array, is_blocked):
            if is_blocked:
                return pl.BlockSpec((array.shape[0] // steps,) + array.shape[1:], lambda i: (i, 0, 0))
            if array.shape == sent_first.shape and steps > 1:
                return pl.BlockSpec((space,) + array.shape[1:], lambda i: (0, 0, 0))
            return whole(array)

        return pl.pallas_call(
            kernel,
            grid=(steps,),
            in_specs=[pl.BlockSpec(memory_space=pltpu.SMEM)]
            + [spec(a, n in blocked) for n, a in enumerate(args)]
            + [pl.BlockSpec(memory_space=pl.ANY)] * len(weights),
            out_specs=[spec(a, is_blocked) for a, is_blocked in outs],
            out_shape=[a for a, _ in outs],
            scratch_shapes=scratch,
            compiler_params=pltpu.CompilerParams(vmem_limit_bytes=VMEM_LIMIT),
            name=name,
        )(seg_scalar, *args, *weights)

    lanes = 2 * c
    field = jax.ShapeDtypeStruct((x_half, lanes, cols), bf16)
    ycoef = jax.ShapeDtypeStruct((x_half * 16, lanes), f32)
    sent = jax.ShapeDtypeStruct((group, 2 * x_count, lanes), bf16)
    sent_first = jax.ShapeDtypeStruct((group, 4 * x_count, lanes), bf16)
    point = jax.ShapeDtypeStruct((lanes, lanes), f32)
    mode_scratch = [
        pltpu.VMEM((2,) + own.shape[1:], bf16), pltpu.SemaphoreType.DMA(()),
        pltpu.VMEM((8 * kx, lanes), f32), pltpu.VMEM((8 * kx, lanes), f32),
    ]
    row_scratch = [pltpu.VMEM((group * 2 * x_count, lanes), f32)]

    zero = jnp.zeros_like(lift_weight.T)
    lift = jnp.concatenate(
        [jnp.concatenate([lift_weight.T, zero], 1), jnp.concatenate([zero, lift_weight.T], 1)], 0
    )
    lift_col = jnp.concatenate([lift_bias] * 2)[:, None]
    where = dict(space=space, rows=row_count, per_chunk=per_chunk)
    act, y0 = pl.pallas_call(
        partial(lift_kernel, depth=depth, **where),
        out_shape=[field, ycoef],
        compiler_params=pltpu.CompilerParams(vmem_limit_bytes=VMEM_LIMIT),
        name="lift",
    )(grid_in, lift, lift_col, act_table)
    acts, slopes, ya = ([act], [], [y0])
    (mine,) = call(
        first_modes_kernel, (y0, lx, xi), (), (own, neighbour), [(sent_first, False)],
        [pltpu.VMEM(own.shape, bf16)] + mode_scratch[1:], 1, "modes",
    )
    across_even = lax.ppermute(
        lax.optimization_barrier((away, mine))[0], "segment", [(2, 0)]
    )
    for layer in range(1, segments):
        recv = to_all(mine)
        table = inv_table
        if layer == 1:
            table = jnp.asarray(y_inverse.reshape(2 * mode_count, cols), bf16)
        act, slope, y, mine = call(
            partial(forward_kernel, layer=layer),
            (recv, acts[-1], point_fwd, bias_cols, table, act_table, lx, xi),
            (1,), weights_of(layer), [(field, True), (field, True), (ycoef, False), (sent, False)],
            mode_scratch + row_scratch, STEPS, "forward",
        )
        acts.append(act)
        slopes.append(slope)
        ya.append(y)
        if layer == 1:
            across_even_on = lax.ppermute(
                lax.optimization_barrier((across_even, mine))[0], "segment", [(0, 1)]
            )

    recv = to_all(mine)
    last = segments - 1
    pre_grad, y, pg, mine = call(
        partial(top_kernel, layer=last, first_row=cot_row, **where),
        (recv, acts[last], grid_in, point_fwd, bias_cols, inv_table,
         proj_weight.T, proj_bias[:, None], proj_weight, out_weight.astype(f32)[:, None],
         grad_table, xa, xb),
        (1,), weights_of(last), [(field, True), (ycoef, False), (point, False), (sent, False)],
        mode_scratch + row_scratch, STEPS, "top",
    )
    yg, pgs = ([y], [pg])
    for layer in reversed(range(last)):
        recv = to_all(mine)
        pre_grad, y, pg, mine = call(
            partial(backward_kernel, layer=layer),
            (recv, pre_grad, slopes[layer], acts[layer], point_back, fwd_table,
             grad_table, xa, xb),
            (1, 2, 3), weights_of(layer),
            [(field, True), (ycoef, False), (point, False), (sent, False)],
            mode_scratch + row_scratch, STEPS, "backward",
        )
        yg.insert(0, y)
        pgs.insert(0, pg)

    pieces = ya + yg + pgs
    summary = jax.ShapeDtypeStruct((2 * x_half * 16 + c, lanes), f32)
    mine, theirs = pl.pallas_call(
        partial(pick_kernel, layers=segments),
        in_specs=[pl.BlockSpec(memory_space=pltpu.SMEM)] + [pl.BlockSpec()] * len(pieces),
        out_shape=[summary, summary],
        compiler_params=pltpu.CompilerParams(vmem_limit_bytes=VMEM_LIMIT),
        name="pick",
    )(seg_scalar, *pieces)
    theirs = lax.ppermute(theirs, "segment", [(0, 1), (1, 0), (2, 3), (3, 2)])
    pieces = [mine, theirs, xz, xa]
    spectral, point_out = pl.pallas_call(
        partial(grads_kernel, scale=1.0 / math.sqrt(batch * x_count * cols)),
        grid=(owned,),
        in_specs=[whole(a) for a in pieces],
        out_specs=[
            pl.BlockSpec((1, kx, 2, c, c), lambda m: (m, 0, 0, 0, 0)),
            pl.BlockSpec((c, c), lambda m: (0, 0)),
        ],
        out_shape=[
            jax.ShapeDtypeStruct((owned, kx, 2, c, c), f32),
            jax.ShapeDtypeStruct((c, c), f32),
        ],
        scratch_shapes=[pltpu.VMEM((4 * kx, lanes), f32)] * 2,
        compiler_params=pltpu.CompilerParams(vmem_limit_bytes=VMEM_LIMIT),
        name="grads",
    )(*pieces)
    return (spectral[None], point_out[None])


def fits_replicated(mesh, inputs, point_weight, spectral_weight):
    segments, space = (mesh.shape["segment"], mesh.shape["space"])
    batch = inputs.shape[0] // mesh.shape["groups"]
    _, rows, depth, cols = inputs.shape
    layers, c, _ = point_weight.shape
    modes, kx = spectral_weight.shape[1:3]
    return (
        batch == 2
        and 2 * c == 128
        and layers == segments == 4
        and modes == 4 * space
        and space in (2, 4)
        and rows % (segments * space) == 0
        and rows % 32 == 0
        and rows <= 64
        and kx == 32
        and depth == 8
        and cols % 128 == 0
        and cols >= 3 * c
        and c * c % (space * cols) == 0
    )


def solution(mesh):
    in_specs = (
        P("groups", "space", None, None),
        P("groups", "space", None),
        P(),
        P(),
        P("segment", None, None),
        P("segment", None),
        P("segment", "space", None, None, None, None),
        P(),
        P(),
        P(),
    )
    out_specs = (
        P(("groups", "segment"), "space", None, None, None, None),
        P(("groups", "segment"), None, None),
    )

    def step(inputs, cotangent, lift_weight, lift_bias, point_weight, layer_bias, spectral_weight, *rest):
        fits = fits_replicated(mesh, inputs, point_weight, spectral_weight)
        mapped = jax.shard_map(
            replicated if fits else on_device,
            mesh=mesh, in_specs=in_specs, out_specs=out_specs, check_vma=False,
        )
        return mapped(
            inputs, cotangent, lift_weight, lift_bias, point_weight, layer_bias, spectral_weight, *rest
        )

    return step
```

```python
from functools import partial
import math

import jax
import jax.numpy as jnp
import numpy as np
from jax import lax
from jax.experimental import pallas as pl
from jax.experimental.pallas import tpu as pltpu
from jax.sharding import PartitionSpec as P

highest = lax.Precision.HIGHEST


def as_sent(array):
    return jax.tree.map(lambda a: a.astype(jnp.bfloat16) if a.dtype == jnp.float32 else a, array)


def passed_along(block, axis, distance):
    devices = range(lax.axis_size(axis))
    route = [(i - distance, i) for i in devices if i - distance in devices]
    return lax.ppermute(block, axis, route)


def y_tables(col_count, mode_count):
    ycells = jnp.arange(col_count, dtype=jnp.int32)[:, None]
    ymodes = jnp.arange(mode_count, dtype=jnp.int32)[None, :]
    angles = (ycells * ymodes % col_count).astype(jnp.float32) * (2.0 * math.pi / col_count)
    factor = 1.0 / math.sqrt(col_count)
    forward = jnp.stack([jnp.cos(angles), -jnp.sin(angles)], axis=1) * factor
    doubled = jnp.where(ymodes == 0, 1.0, 2.0).astype(jnp.float32)
    inverse = jnp.stack([doubled * jnp.cos(angles), -doubled * jnp.sin(angles)], axis=0) * factor
    return (forward.astype(jnp.bfloat16), jnp.transpose(inverse, (0, 2, 1)).astype(jnp.bfloat16))


def x_tables(row_total, mode_count):
    kx_count = 2 * mode_count
    indices = jnp.arange(kx_count, dtype=jnp.int32)
    freq_values = jnp.where(indices < mode_count, indices, indices - kx_count)
    xcells = jnp.arange(row_total, dtype=jnp.int32)
    angles = (freq_values[:, None] * xcells[None, :] % row_total).astype(jnp.float32) * (
        2.0 * math.pi / row_total
    )
    factor = 1.0 / math.sqrt(row_total)
    cosine_part = jnp.cos(angles) * factor
    sine_part = jnp.sin(angles) * factor
    forward = jnp.stack(
        [jnp.stack([cosine_part, sine_part], -1), jnp.stack([-sine_part, cosine_part], -1)], axis=1
    )
    cosine_flip = cosine_part.T
    sine_flip = sine_part.T
    inverse = jnp.stack(
        [jnp.stack([cosine_flip, -sine_flip], -1), jnp.stack([sine_flip, cosine_flip], -1)], axis=1
    )
    return (forward, inverse)


def mode_mult(coeffs, kernel):
    real_in, imag_in = (coeffs[:, :, 0], coeffs[:, :, 1])
    real_kernel, imag_kernel = (kernel[:, :, 0], kernel[:, :, 1])
    product = partial(jnp.einsum, "mjc,mjco->mjo", precision=highest)
    real_out = product(real_in, real_kernel) - product(imag_in, imag_kernel)
    imag_out = product(real_in, imag_kernel) + product(imag_in, real_kernel)
    return jnp.stack([real_out, imag_out], axis=2)


def mode_back(coeffs, mode_grads, kernel):
    real_in, imag_in = (coeffs[:, :, 0], coeffs[:, :, 1])
    real_grad, imag_grad = (mode_grads[:, :, 0], mode_grads[:, :, 1])
    real_kernel, imag_kernel = (kernel[:, :, 0], kernel[:, :, 1])
    outer_sum = partial(jnp.einsum, "mjc,mjo->mjco", precision=highest)
    inner_sum = partial(jnp.einsum, "mjo,mjco->mjc", precision=highest)
    kernel_real = outer_sum(real_in, real_grad) + outer_sum(imag_in, imag_grad)
    kernel_imag = outer_sum(real_in, imag_grad) - outer_sum(imag_in, real_grad)
    coeff_real = inner_sum(real_grad, real_kernel) + inner_sum(imag_grad, imag_kernel)
    coeff_imag = inner_sum(imag_grad, real_kernel) - inner_sum(real_grad, imag_kernel)
    return (
        jnp.stack([kernel_real, kernel_imag], axis=2),
        jnp.stack([coeff_real, coeff_imag], axis=2),
    )


def gelu_grad(pre_act, upstream):
    _, pullback = jax.vjp(jax.nn.gelu, pre_act)
    return pullback(upstream)[0]


def store_slot(buffer, value, slot_clip, is_valid):
    previous = lax.dynamic_index_in_dim(buffer, slot_clip, 0, keepdims=False)
    return lax.dynamic_update_index_in_dim(
        buffer, jnp.where(is_valid, value, previous), slot_clip, 0
    )


def on_device(
    inputs,
    cotangent,
    lift_weight,
    lift_bias,
    point_weight,
    layer_bias,
    spectral_weight,
    proj_weight,
    proj_bias,
    out_weight,
):
    batch_count, row_count, _, col_count = inputs.shape
    segment_count = lax.axis_size("segment")
    segment_index = lax.axis_index("segment")
    space_count = lax.axis_size("space")
    owned_modes = spectral_weight.shape[1]
    kx_count = spectral_weight.shape[2]
    channels = point_weight.shape[1]
    mode_count = kx_count // 2
    y_forward, y_inverse = y_tables(col_count, mode_count)
    x_forward, x_inverse = x_tables(row_count * space_count, mode_count)
    x_forward_adj = jnp.transpose(x_forward, (2, 3, 0, 1))
    x_inverse_adj = jnp.transpose(x_inverse, (2, 3, 0, 1))
    y_forward_wide = y_forward.astype(jnp.float32)
    y_inverse_wide = y_inverse.astype(jnp.float32)
    kernel = spectral_weight[0].astype(jnp.float32)
    point_matrix = point_weight[0]
    bias_vector = layer_bias[0]
    tick_count = batch_count + segment_count - 1

    def to_owners(y_coeffs, x_table):
        exchanged = lax.all_to_all(
            y_coeffs.astype(jnp.bfloat16), "space", split_axis=1, concat_axis=0, tiled=True
        ).astype(y_coeffs.dtype)
        return jnp.einsum("jqxp,xmpc->mjqc", x_table, exchanged, precision=highest)

    def from_owners(owned, x_table):
        spread = jnp.einsum("xpjq,mjqc->xmpc", x_table, owned, precision=highest)
        return lax.all_to_all(
            as_sent(spread), "space", split_axis=0, concat_axis=1, tiled=True
        ).astype(spread.dtype)

    def lifted(pick_slot):
        sample = lax.dynamic_index_in_dim(inputs, pick_slot, 0, keepdims=False)
        mixed = jnp.einsum("xty,tc->xcy", sample, lift_weight, preferred_element_type=jnp.float32)
        return (mixed + lift_bias[None, :, None]).astype(jnp.bfloat16)

    def forward_tick(state_now, tick_now):
        incoming, pre_store, act_store, mode_store = state_now
        pick_slot = jnp.clip(tick_now, 0, batch_count - 1)
        layer_in = lax.cond(segment_index == 0, lambda: lifted(pick_slot), lambda: incoming)
        y_coeffs = jnp.einsum(
            "xcy,ypm->xmpc", layer_in, y_forward, preferred_element_type=jnp.float32
        )
        coeffs = to_owners(y_coeffs, x_forward)
        back_rows = from_owners(mode_mult(coeffs, kernel), x_inverse)
        branch = jnp.einsum("xmpc,pmy->xcy", back_rows, y_inverse_wide, precision=highest)
        pointwise = jnp.einsum(
            "xcy,co->xoy", layer_in, point_matrix, preferred_element_type=jnp.float32
        )
        pre_act = pointwise + branch + bias_vector[None, :, None]
        slot_index = tick_now - segment_index
        is_valid = (slot_index >= 0) & (slot_index < batch_count)
        slot_clip = jnp.clip(slot_index, 0, batch_count - 1)
        pre_store = store_slot(pre_store, pre_act, slot_clip, is_valid)
        act_store = store_slot(act_store, layer_in, slot_clip, is_valid)
        mode_store = store_slot(mode_store, coeffs, slot_clip, is_valid)
        layer_out = jax.nn.gelu(pre_act).astype(jnp.bfloat16)
        sent = passed_along(layer_out, "segment", 1)
        return ((sent, pre_store, act_store, mode_store), None)

    start_state = (
        jnp.zeros((row_count, channels, col_count), jnp.bfloat16),
        jnp.zeros((batch_count, row_count, channels, col_count), jnp.float32),
        jnp.zeros((batch_count, row_count, channels, col_count), jnp.bfloat16),
        jnp.zeros((batch_count, owned_modes, kx_count, 2, channels), jnp.float32),
    )
    final_state, _ = lax.scan(forward_tick, start_state, jnp.arange(tick_count, dtype=jnp.int32))
    _, pre_store, act_store, mode_store = final_state

    def top_grad(slot_clip, pre_act):
        top_act = jax.nn.gelu(pre_act).astype(jnp.bfloat16)
        hidden = jnp.einsum("xcy,ck->xky", top_act, proj_weight, preferred_element_type=jnp.float32)
        hidden = hidden + proj_bias[None, :, None]
        target = lax.dynamic_index_in_dim(cotangent, slot_clip, 0, keepdims=False)
        upstream = (
            out_weight.astype(jnp.float32)[None, :, None] * target.astype(jnp.float32)[:, None, :]
        )
        hidden_grad = gelu_grad(hidden, upstream).astype(jnp.bfloat16)
        return jnp.einsum(
            "xky,ck->xcy", hidden_grad, proj_weight, preferred_element_type=jnp.float32
        ).astype(jnp.bfloat16)

    def backward_tick(state_now, tick_now):
        incoming, point_sum, kernel_sum = state_now
        slot_index = tick_now - (segment_count - 1 - segment_index)
        is_valid = (slot_index >= 0) & (slot_index < batch_count)
        slot_clip = jnp.clip(slot_index, 0, batch_count - 1)
        pre_act = lax.dynamic_index_in_dim(pre_store, slot_clip, 0, keepdims=False)
        layer_in = lax.dynamic_index_in_dim(act_store, slot_clip, 0, keepdims=False)
        coeffs = lax.dynamic_index_in_dim(mode_store, slot_clip, 0, keepdims=False)
        grad_out = lax.cond(
            segment_index == segment_count - 1,
            lambda: top_grad(slot_clip, pre_act),
            lambda: incoming,
        )
        pre_grad = gelu_grad(pre_act, grad_out.astype(jnp.float32)).astype(jnp.bfloat16)
        point_term = jnp.einsum(
            "xcy,xoy->co", layer_in, pre_grad, preferred_element_type=jnp.float32
        )
        y_grads = jnp.einsum(
            "xoy,pmy->xmpo", pre_grad, y_inverse, preferred_element_type=jnp.float32
        )
        mode_grads = to_owners(y_grads, x_inverse_adj)
        kernel_step, coeff_step = mode_back(coeffs, mode_grads, kernel)
        back_rows = from_owners(coeff_step, x_forward_adj)
        back_branch = jnp.einsum("xmpc,ypm->xcy", back_rows, y_forward_wide, precision=highest)
        pointwise_back = jnp.einsum(
            "co,xoy->xcy", point_matrix, pre_grad, preferred_element_type=jnp.float32
        )
        grad_in = (pointwise_back + back_branch).astype(jnp.bfloat16)
        point_sum = point_sum + jnp.where(is_valid, point_term, 0.0)
        kernel_sum = kernel_sum + jnp.where(is_valid, kernel_step, 0.0)
        sent = passed_along(grad_in, "segment", -1)
        return ((sent, point_sum, kernel_sum), None)

    back_start = (
        jnp.zeros((row_count, channels, col_count), jnp.bfloat16),
        jnp.zeros((channels, channels), jnp.float32),
        jnp.zeros((owned_modes, kx_count, 2, channels, channels), jnp.float32),
    )
    back_state, _ = lax.scan(backward_tick, back_start, jnp.arange(tick_count, dtype=jnp.int32))
    _, point_sum, kernel_sum = back_state
    point_total = lax.psum(point_sum, "space")
    factor = 1.0 / math.sqrt(batch_count * row_count * space_count * col_count)
    return (kernel_sum[None], (point_total * factor)[None])


f32, bf16 = (jnp.float32, jnp.bfloat16)
NT = (((1,), (1,)), ((), ()))
NN = (((1,), (0,)), ((), ()))
VMEM_LIMIT = 48 << 20


def np_y_tables(col_count, mode_count):
    ycells = np.arange(col_count)[:, None]
    ymodes = np.arange(mode_count)[None, :]
    angles = (ycells * ymodes % col_count) * (2.0 * math.pi / col_count)
    factor = 1.0 / math.sqrt(col_count)
    doubled = np.where(ymodes == 0, 1.0, 2.0)
    forward = np.stack([np.cos(angles), -np.sin(angles)], axis=0) * factor
    inverse = np.stack([doubled * np.cos(angles), -doubled * np.sin(angles)], axis=0) * factor
    return (forward.transpose(2, 0, 1), inverse.transpose(2, 0, 1))


def np_x_tables(row_total, mode_count):
    kx_count = 2 * mode_count
    indices = np.arange(kx_count)
    freq = np.where(indices < mode_count, indices, indices - kx_count)
    angles = (freq[:, None] * np.arange(row_total)[None, :] % row_total) * (2.0 * math.pi / row_total)
    factor = 1.0 / math.sqrt(row_total)
    c, s = (np.cos(angles) * factor, np.sin(angles) * factor)
    forward = np.stack([np.stack([c, s], -1), np.stack([-s, c], -1)], axis=1)
    inverse = np.stack([np.stack([c.T, -s.T], -1), np.stack([s.T, c.T], -1)], axis=1)
    return (forward, inverse)


def hdot(a, b):
    return jnp.dot(a, b, precision=highest, preferred_element_type=f32)


def gelu_both(v):
    k0 = math.sqrt(2.0 / math.pi)
    k1 = k0 * 0.044715
    v2 = v * v
    share = 0.5 + 0.5 * jnp.tanh(v * (k0 + k1 * v2))
    value = v * share
    slope = share + value * (1.0 - share) * (2.0 * k0 + (6.0 * k1) * v2)
    return (value, slope)


def low_half(shape):
    return lax.broadcasted_iota(jnp.int32, shape, 1) < shape[1] // 2


def swap_halves(a):
    return pltpu.roll(a, a.shape[1] // 2, 1)


def cross(a, b):
    low = low_half(a.shape)
    return (jnp.where(low, a, swap_halves(b)), jnp.where(low, swap_halves(a), b))


def grid_rows(first_ref, first, second_ref, second, x_half):
    parts = []
    for p in range(2):
        parts += cross(
            first_ref[pl.ds(first + p, x_half, stride=16), :],
            second_ref[pl.ds(second + p, x_half, stride=16), :],
        )
    return jnp.concatenate(parts, axis=0)


def own_grid(y_ref, row=8):
    return grid_rows(y_ref, row, y_ref, row + 2, y_ref.shape[0] // 16)


def put_chunk(grid, out_ref, first=0):
    x_half = grid.shape[0] // 4
    for p in range(2):
        base = 2 * p * x_half
        pair = cross(grid[base : base + x_half], grid[base + x_half : base + 2 * x_half])
        for mode in range(2):
            at = first + (2 * mode + p) * x_half
            block = pair[mode].astype(bf16)
            for k in range(out_ref.shape[0]):
                out_ref[k, at : at + x_half] = block


def put_split(t_ref, mode, rows):
    count = rows.shape[0]
    high = rows.astype(bf16).astype(f32)
    t_ref[2 * mode * count : (2 * mode + 1) * count] = high
    t_ref[(2 * mode + 1) * count : (2 * mode + 2) * count] = rows - high


def mode_products(t_ref, w_ref, m_ref, dims, start=0):
    pairs = w_ref.shape[1]
    for j in range(pairs):
        for mode in range(2):
            at = pl.ds(mode * 8 * pairs + j, 8, stride=pairs)
            m_ref[at, :] = lax.dot_general(
                t_ref[at, :].astype(bf16), w_ref[start + mode, j], dims, preferred_element_type=f32
            )
    count = 4 * pairs
    return [
        m_ref[2 * mode * count : (2 * mode + 1) * count]
        + m_ref[(2 * mode + 1) * count : (2 * mode + 2) * count]
        for mode in range(2)
    ]


def first_kx(shape, pairs):
    return (lax.broadcasted_iota(jnp.int32, shape, 0) // pairs) % 2 == 0


def forward_modes(y_ref, w_ref, lx_ref, xi_ref, t_ref, m_ref, out_ref, row=8, start=0):
    pairs = w_ref.shape[1]
    ys = own_grid(y_ref, row)
    sw = swap_halves(ys)
    low = low_half(ys.shape)
    zero = jnp.zeros_like(ys)
    put_split(t_ref, 0, hdot(lx_ref[...], jnp.concatenate([jnp.where(low, ys, zero), jnp.where(low, zero, sw)], axis=0)))
    put_split(t_ref, 1, hdot(lx_ref[...], jnp.concatenate([jnp.where(low, sw, zero), jnp.where(low, zero, ys)], axis=0)))
    m0, m1 = mode_products(t_ref, w_ref, m_ref, NN, start)
    first = first_kx(m0.shape, pairs)
    s0 = jnp.where(first, m0, swap_halves(m0))
    s1 = jnp.where(first, swap_halves(m1), m1)
    first_row = start * out_ref.shape[1] // w_ref.shape[0]
    put_chunk(hdot(xi_ref[...], jnp.where(low_half(m0.shape), s0, s1)), out_ref, first_row)


def backward_modes(y_ref, w_ref, xa_ref, xf_ref, t_ref, m_ref, out_ref):
    pairs = w_ref.shape[1]
    g = hdot(xa_ref[...], own_grid(y_ref))
    sw = swap_halves(g)
    first = first_kx(g.shape, pairs)
    keep = low_half(g.shape) == first
    zero = jnp.zeros_like(g)
    put_split(t_ref, 0, jnp.where(keep, jnp.where(first, g, sw), zero))
    put_split(t_ref, 1, jnp.where(keep, jnp.where(first, sw, g), zero))
    m0, m1 = mode_products(t_ref, w_ref, m_ref, NT)
    half = 2 * pairs
    pr0, pi0, pr1, pi1 = (m0[:half], m0[half:], m1[:half], m1[half:])
    low = low_half(pr0.shape)
    real = jnp.where(low, pr0 + swap_halves(pi0), swap_halves(pr1) + pi1)
    imag = jnp.where(low, pi0 - swap_halves(pr0), swap_halves(pi1) - pr1)
    put_chunk(hdot(xf_ref[...], jnp.concatenate([real, imag], axis=0)), out_ref)


def choose_kernel(seg_ref, layer, w_refs, w_ref, sem, start):
    for seg in range(4):
        pair = seg // 2
        source = w_refs[(0 if seg % 2 == layer % 2 else 1) + (0 if pair == layer // 2 else 2)]
        if pair == layer // 2:
            source = source.at[2 * pair : 2 * pair + 2]

        @pl.when(seg_ref[0] == seg)
        def _(source=source):
            copy = pltpu.make_async_copy(source, w_ref, sem)
            if start:
                copy.start()
            else:
                copy.wait()


def choose_all(seg_ref, w_refs, w_ref, sem, start):
    for lane in range(2):
        @pl.when(seg_ref[0] % 2 == lane)
        def _(lane=lane):
            copy = pltpu.make_async_copy(w_refs[lane], w_ref, sem)
            if start:
                copy.start()
            else:
                copy.wait()


def pack_kernel(in_ref, out_ref):
    out_ref[...] = jnp.concatenate([in_ref[:, 0], in_ref[:, 1]], axis=-1)


def widen(recv_ref, r_ref):
    rows = recv_ref.shape[1]
    for k in range(r_ref.shape[0] // rows):
        r_ref[k * rows : (k + 1) * rows] = recv_ref[k].astype(f32)


def row_product(weight, field, r_ref, table, x, x_half):
    rows = r_ref[pl.ds(x, table.shape[0], stride=x_half), :]
    lhs = jnp.concatenate([weight, rows.T.astype(bf16)], axis=1)
    return jnp.dot(lhs, jnp.concatenate([field, table], axis=0), preferred_element_type=f32)


def chunk_of(x, half_side, space, rows, per_chunk):
    inner = x % rows
    return ((inner // per_chunk) * space + half_side * (space // 2) + x // rows, inner % per_chunk)


def lift_kernel(seg_ref, in_ref, lw_ref, lb_ref, tab_ref, act_ref, y_ref, *, space, rows, per_chunk, depth):
    table = tab_ref[seg_ref[1]]
    for x in range(act_ref.shape[0]):
        cells = []
        for side in range(2):
            k, i = chunk_of(x, side, space, rows, per_chunk)
            cells.append(in_ref[k, i * depth : (i + 1) * depth, :])
        cells = jnp.concatenate(cells, axis=0)
        act = jnp.dot(lw_ref[...], cells, preferred_element_type=f32) + lb_ref[...]
        act = act.astype(bf16)
        act_ref[x] = act
        y_ref[x * 16 : (x + 1) * 16] = lax.dot_general(
            table, act, NT, preferred_element_type=f32
        )


def first_modes_kernel(seg_ref, y_ref, lx_ref, xi_ref, w0, w1, out_ref, w_ref, sem, t_ref, m_ref):
    choose_all(seg_ref, (w0, w1), w_ref, sem, True)
    choose_all(seg_ref, (w0, w1), w_ref, sem, False)
    for start in range(0, w_ref.shape[0], 2):
        forward_modes(y_ref, w_ref, lx_ref, xi_ref, t_ref, m_ref, out_ref, 2 * start, start)


def in_pairs(count, start, finish, scratch):
    start(0, scratch[0])

    def two(i, carry):
        x = 2 * i
        start(x + 1, scratch[1])
        finish(x, scratch[0])
        start(jnp.minimum(x + 2, count - 1), scratch[0])
        finish(x + 1, scratch[1])
        return carry

    lax.fori_loop(0, count // 2, two, 0)


def put_rows(y_ref, x, rows):
    y_ref[pl.ds(pl.multiple_of(x * 16, 16), 16), :] = rows


def forward_kernel(
    seg_ref, recv_ref, act_ref, pw_ref, pb_ref, inv_ref, tab_ref, lx_ref, xi_ref, w0, w1, w2, w3,
    next_ref, slope_ref, y_ref, out_ref, w_ref, sem, t_ref, m_ref, r_ref, p0_ref, p1_ref, *, layer,
):
    x_half = act_ref.shape[0]
    choose_kernel(seg_ref, layer, (w0, w1, w2, w3), w_ref, sem, True)
    widen(recv_ref, r_ref)
    table = tab_ref.at[seg_ref[1]]

    def start(x, ref):
        ref[...] = row_product(pw_ref[layer - 1], act_ref[x], r_ref, inv_ref[...], x, x_half)

    def finish(x, ref):
        value, slope = gelu_both(ref[...] + pb_ref[layer - 1])
        value = value.astype(bf16)
        next_ref[x] = value
        slope_ref[x] = slope.astype(bf16)
        put_rows(y_ref, x, lax.dot_general(table[...], value, NT, preferred_element_type=f32))

    in_pairs(x_half, start, finish, (p0_ref, p1_ref))
    choose_kernel(seg_ref, layer, (w0, w1, w2, w3), w_ref, sem, False)
    forward_modes(y_ref, w_ref, lx_ref, xi_ref, t_ref, m_ref, out_ref)


def adjoint_rows(x, grad, act, table, pre_ref, y_ref, point_ref):
    pre_grad = grad.astype(bf16)
    pre_ref[x] = pre_grad
    both = lax.dot_general(
        jnp.concatenate([table[...], act], axis=0), pre_grad, NT, preferred_element_type=f32
    )
    put_rows(y_ref, x, both[:16])
    point_ref[...] += both[16:]


def top_kernel(
    seg_ref, recv_ref, act_ref, in_ref, pw_ref, pb_ref, inv_ref, up_ref, hb_ref, down_ref, ow_ref,
    tab_ref, xa_ref, xf_ref, w0, w1, w2, w3,
    pre_ref, y_ref, point_ref, out_ref, w_ref, sem, t_ref, m_ref, r_ref,
    p0_ref, p1_ref, s0_ref, s1_ref, h0_ref, h1_ref,
    *, layer, space, rows, per_chunk, first_row,
):
    x_half = act_ref.shape[0]
    choose_kernel(seg_ref, layer, (w0, w1, w2, w3), w_ref, sem, True)
    widen(recv_ref, r_ref)
    point_ref[...] = jnp.zeros_like(point_ref)
    table = tab_ref.at[seg_ref[1]]
    hidden_count = up_ref.shape[0]
    size = act_ref.shape[1] // 2

    def start(x, ref):
        ref[...] = row_product(pw_ref[layer], act_ref[x], r_ref, inv_ref[...], x, x_half)

    def middle(ref, slope_ref, hidden_ref):
        value, slope = gelu_both(ref[...] + pb_ref[layer])
        slope_ref[...] = slope
        value = value.astype(bf16)
        for side in range(2):
            hidden_ref[side * hidden_count : (side + 1) * hidden_count] = jnp.dot(
                up_ref[...], value[side * size : (side + 1) * size], preferred_element_type=f32
            )

    def finish(x, slope_ref, hidden_ref):
        grads = []
        for side in range(2):
            hidden = hidden_ref[side * hidden_count : (side + 1) * hidden_count]
            _, hidden_slope = gelu_both(hidden + hb_ref[...])
            chunk, within = chunk_of(x, side, space, rows, per_chunk)
            cots = in_ref[chunk, first_row : first_row + per_chunk, :].astype(f32)
            cot = cots[:1]
            for other in range(1, per_chunk):
                cot = jnp.where(within == other, cots[other : other + 1], cot)
            grads.append(
                cot * jnp.dot(
                    down_ref[...], (hidden_slope * ow_ref[...]).astype(bf16), preferred_element_type=f32
                )
            )
        grad = jnp.concatenate(grads, axis=0) * slope_ref[...]
        adjoint_rows(x, grad, act_ref[x], table, pre_ref, y_ref, point_ref)

    last = x_half - 1
    start(0, p0_ref)
    middle(p0_ref, s0_ref, h0_ref)
    start(1, p1_ref)

    def two(i, carry):
        x = 2 * i
        start(jnp.minimum(x + 2, last), p0_ref)
        middle(p1_ref, s1_ref, h1_ref)
        finish(x, s0_ref, h0_ref)
        start(jnp.minimum(x + 3, last), p1_ref)
        middle(p0_ref, s0_ref, h0_ref)
        finish(x + 1, s1_ref, h1_ref)
        return carry

    lax.fori_loop(0, x_half // 2, two, 0)
    choose_kernel(seg_ref, layer, (w0, w1, w2, w3), w_ref, sem, False)
    backward_modes(y_ref, w_ref, xa_ref, xf_ref, t_ref, m_ref, out_ref)


def backward_kernel(
    seg_ref, recv_ref, grad_ref, slope_ref, act_ref, pw_ref, fwd_ref, tab_ref, xa_ref, xf_ref,
    w0, w1, w2, w3,
    pre_ref, y_ref, point_ref, out_ref, w_ref, sem, t_ref, m_ref, r_ref, p0_ref, p1_ref, *, layer,
):
    x_half = act_ref.shape[0]
    if layer:
        choose_kernel(seg_ref, layer, (w0, w1, w2, w3), w_ref, sem, True)
    widen(recv_ref, r_ref)
    point_ref[...] = jnp.zeros_like(point_ref)
    table = tab_ref.at[seg_ref[1]]

    def start(x, ref):
        ref[...] = row_product(pw_ref[layer + 1], grad_ref[x], r_ref, fwd_ref[...], x, x_half)

    def finish(x, ref):
        grad = ref[...] * slope_ref[x].astype(f32)
        adjoint_rows(x, grad, act_ref[x], table, pre_ref, y_ref, point_ref)

    in_pairs(x_half, start, finish, (p0_ref, p1_ref))
    if layer:
        choose_kernel(seg_ref, layer, (w0, w1, w2, w3), w_ref, sem, False)
        backward_modes(y_ref, w_ref, xa_ref, xf_ref, t_ref, m_ref, out_ref)
    else:
        out_ref[...] = jnp.zeros_like(out_ref)


def pick_kernel(seg_ref, *refs, layers):
    ya_refs, yg_refs, pg_refs = (refs[:layers], refs[layers : 2 * layers], refs[2 * layers : 3 * layers])
    count = ya_refs[0].shape[0]
    seg = seg_ref[0]
    partner = seg + 1 - 2 * (seg % 2)
    for out_ref, wanted in zip(refs[3 * layers :], (seg, partner)):
        for layer in range(layers):
            @pl.when(wanted == layer)
            def _(layer=layer, out_ref=out_ref):
                out_ref[:count] = ya_refs[layer][...]
                out_ref[count : 2 * count] = yg_refs[layer][...]
                pg = pg_refs[layer][...]
                half = pg.shape[0] // 2
                out_ref[2 * count :] = pg[:half] + swap_halves(pg[half:])


def grads_kernel(mine_ref, theirs_ref, xz_ref, xa_ref, out_ref, point_ref, a_ref, b_ref, *, scale):
    mode = pl.program_id(0)
    c = point_ref.shape[0]
    count = (mine_ref.shape[0] - c) // 2
    x_half = count // 16

    @pl.when(mode == 0)
    def _():
        point_ref[...] = (mine_ref[2 * count :, :c] + theirs_ref[2 * count :, :c]) * scale

    z = hdot(xz_ref[...], grid_rows(mine_ref, 2 * mode, theirs_ref, 2 * mode, x_half))
    at = count + 2 * mode
    g = hdot(xa_ref[...], grid_rows(mine_ref, at, theirs_ref, at, x_half))
    rows = z.shape[0]
    kx = rows // 2
    zs, gs = (swap_halves(z), swap_halves(g))
    a_ref[:rows] = z
    a_ref[rows:] = zs
    low = low_half((kx, z.shape[1]))
    b_ref[:kx] = jnp.where(low, g[:kx], gs[kx:])
    b_ref[kx:rows] = jnp.where(low, g[kx:], -gs[:kx])
    b_ref[rows : rows + kx] = jnp.where(low, gs[:kx], g[kx:])
    b_ref[rows + kx :] = jnp.where(low, gs[kx:], -g[:kx])
    for j in range(kx):
        a = a_ref[pl.ds(j, 4, stride=kx), :][:, :c]
        b = b_ref[pl.ds(j, 4, stride=kx), :]
        ah, bh = (a.astype(bf16).astype(f32), b.astype(bf16).astype(f32))
        left = jnp.concatenate([ah, a - ah, ah], axis=0).T.astype(bf16)
        right = jnp.concatenate([bh, bh, b - bh], axis=0).astype(bf16)
        out_ref[0, j, 0] = jnp.dot(left, right[:, :c], preferred_element_type=f32)
        out_ref[0, j, 1] = jnp.dot(left, right[:, c:], preferred_element_type=f32)


def replicated(
    inputs, cotangent, lift_weight, lift_bias, point_weight, layer_bias, spectral_weight,
    proj_weight, proj_bias, out_weight,
):
    batch, row_count, depth, cols = inputs.shape
    segments, space = (lax.axis_size("segment"), lax.axis_size("space"))
    seg, place = (lax.axis_index("segment"), lax.axis_index("space"))
    pair = seg // 2
    both = ("segment", "space")
    owned, kx = spectral_weight.shape[1:3]
    c = point_weight.shape[1]
    x_count = row_count * space
    x_half = x_count // 2
    mode_count = owned * space
    per_chunk = row_count // segments
    pairs = kx // 2
    group = segments // 2 * space

    cells = lax.dynamic_slice_in_dim(inputs, seg * per_chunk, per_chunk, 1)
    cells = cells.reshape(batch, per_chunk * depth, cols)
    cots = lax.dynamic_slice_in_dim(cotangent, seg * per_chunk, per_chunk, 1)
    weight_rows = c * c // space // cols
    share = lax.dynamic_index_in_dim(
        point_weight.reshape(space, weight_rows, cols), place, 0, keepdims=False
    )
    high = lax.reduce_precision(layer_bias[0], 8, 7)
    mid = lax.reduce_precision(layer_bias[0] - high, 8, 7)
    rest = layer_bias[0] - high - mid
    bias_row = jnp.concatenate([high, mid, rest, jnp.zeros((cols - 3 * c,), f32)]).astype(bf16)
    common = jnp.concatenate([share, bias_row[None]], axis=0)
    chunk = jnp.concatenate([cells, cots, jnp.broadcast_to(common[None], (batch,) + common.shape)], axis=1)
    cot_row = per_chunk * depth
    share_row = cot_row + per_chunk
    bias_at = share_row + weight_rows
    chunk = jnp.pad(chunk, ((0, 0), (0, -chunk.shape[1] % 8), (0, 0)))
    chunk = jnp.broadcast_to(chunk[None, :, None], (segments // 2, batch, space) + chunk.shape[1:])
    stack = spectral_weight[0].reshape(owned, 2, pairs, 2 * c, c)
    pack = pl.pallas_call(
        pack_kernel,
        grid=(owned,),
        in_specs=[pl.BlockSpec((1, 2, pairs, 2 * c, c), lambda m: (m, 0, 0, 0, 0))],
        out_specs=pl.BlockSpec((1, pairs, 2 * c, 2 * c), lambda m: (m, 0, 0, 0)),
        out_shape=jax.ShapeDtypeStruct((owned, pairs, 2 * c, 2 * c), bf16),
        compiler_params=pltpu.CompilerParams(vmem_limit_bytes=VMEM_LIMIT),
        name="pack",
    )
    own = pack(stack)
    swap = [(0, 1), (1, 0), (2, 3), (3, 2)]
    neighbour = lax.ppermute(own, "segment", swap)
    away = lax.dynamic_slice_in_dim(own, 2 * (1 - pair), 2, 0)
    across_odd = lax.ppermute(away, "segment", [(1, 3), (3, 1)])

    grid_in = lax.all_to_all(
        chunk.reshape((segments * space,) + chunk.shape[3:]), both, 0, 0, tiled=True
    )
    across_odd_on = lax.ppermute(across_odd, "segment", [(1, 0), (3, 2)])

    def weights_of(layer):
        if layer % 2:
            return (own, neighbour, across_odd, across_odd_on)
        return (own, neighbour, across_even, across_even_on)

    points = grid_in[:, share_row:bias_at].reshape(segments, c, c)
    bias_parts = grid_in[::space, bias_at, : 3 * c].astype(f32).reshape(segments, 3, c)
    biases = bias_parts[:, 0] + bias_parts[:, 1] + bias_parts[:, 2]
    blank = jnp.zeros((segments, c, c), bf16)

    def doubled(mats):
        return jnp.concatenate(
            [jnp.concatenate([mats, blank], axis=2), jnp.concatenate([blank, mats], axis=2)], axis=1
        )

    point_back = doubled(points)
    point_fwd = doubled(jnp.transpose(points, (0, 2, 1)))
    bias_cols = jnp.concatenate([biases] * 2, axis=1)[:, :, None]

    y_forward, y_inverse = np_y_tables(cols, mode_count)
    x_forward, x_inverse = np_x_tables(x_count, kx // 2)
    firsts = [k % space * owned + k // space * 2 for k in range(group)]
    order = [first + i for first in firsts for i in range(2)]

    def gathered(table):
        return jnp.asarray(table[order].reshape(4 * group, cols), bf16)

    def analysis(table):
        full = np.zeros((group, 16, cols))
        for k in range(group):
            s = k % space
            full[k, : 2 * owned] = table[s * owned : (s + 1) * owned].reshape(2 * owned, cols)
            full[k, 8:12] = table[firsts[k] : firsts[k] + 2].reshape(4, cols)
        return jnp.asarray(full, bf16)

    inv_table, fwd_table = (gathered(y_inverse), gathered(y_forward))
    act_table, grad_table = (analysis(y_forward), analysis(y_inverse))
    xf = x_forward.transpose(0, 1, 3, 2).reshape(kx, 2, 2 * x_count)
    lx = np.concatenate(
        [np.concatenate([xf[:, 0], -xf[:, 1]], 1), np.concatenate([xf[:, 1], xf[:, 0]], 1)], 0
    )
    xz = xf.transpose(1, 0, 2).reshape(2 * kx, 2 * x_count)
    xi = x_inverse.transpose(1, 0, 3, 2).reshape(2 * x_count, 2 * kx)
    lx, xz, xi, xa, xb = (jnp.asarray(t, f32) for t in (lx, xz, xi, xi.T.copy(), xz.T.copy()))

    device_lists = [
        [(2 * k + lane) * space + s for k in range(segments // 2) for s in range(space)]
        for lane in range(2)
    ]

    def to_all(block):
        return lax.all_to_all(block, both, 0, 0, tiled=True, axis_index_groups=device_lists)

    def whole(array):
        rank = len(array.shape)
        return pl.BlockSpec(array.shape, lambda *i: (0,) * rank)

    def placed(kernel):
        def body(*refs):
            own_seg = lax.axis_index("segment")
            kernel((own_seg, own_seg // 2 * space + lax.axis_index("space")), *refs)

        return body


    def call(kernel, args, weights, outs, scratch):
        near = pl.BlockSpec(memory_space=pltpu.VMEM)
        return pl.pallas_call(
            placed(kernel),
            in_specs=[near] * len(args)
            + [pl.BlockSpec(memory_space=pl.ANY)] * len(weights),
            out_specs=[near] * len(outs),
            out_shape=outs,
            scratch_shapes=scratch,
            compiler_params=pltpu.CompilerParams(vmem_limit_bytes=VMEM_LIMIT),
        )(*args, *weights)

    lanes = 2 * c
    field = jax.ShapeDtypeStruct((x_half, lanes, cols), bf16)
    ycoef = jax.ShapeDtypeStruct((x_half * 16, lanes), f32)
    sent = jax.ShapeDtypeStruct((group, 2 * x_count, lanes), bf16)
    sent_first = jax.ShapeDtypeStruct((group, 4 * x_count, lanes), bf16)
    point = jax.ShapeDtypeStruct((lanes, lanes), f32)
    mode_scratch = [
        pltpu.VMEM((2,) + own.shape[1:], bf16), pltpu.SemaphoreType.DMA(()),
        pltpu.VMEM((8 * kx, lanes), f32), pltpu.VMEM((8 * kx, lanes), f32),
    ]
    row = pltpu.VMEM((lanes, cols), f32)
    row_scratch = [pltpu.VMEM((group * 2 * x_count, lanes), f32), row, row]
    top_scratch = [row, row] + [pltpu.VMEM((2 * proj_weight.shape[1], cols), f32)] * 2

    zero = jnp.zeros_like(lift_weight.T)
    lift = jnp.concatenate(
        [jnp.concatenate([lift_weight.T, zero], 1), jnp.concatenate([zero, lift_weight.T], 1)], 0
    )
    lift_col = jnp.concatenate([lift_bias] * 2)[:, None]
    where = dict(space=space, rows=row_count, per_chunk=per_chunk)
    act, y0 = pl.pallas_call(
        placed(partial(lift_kernel, depth=depth, **where)),
        out_shape=[field, ycoef],
        compiler_params=pltpu.CompilerParams(vmem_limit_bytes=VMEM_LIMIT),
        name="lift",
    )(grid_in, lift, lift_col, act_table)
    acts, slopes, ya = ([act], [], [y0])
    (mine,) = call(
        first_modes_kernel, (y0, lx, xi), (own, neighbour), [sent_first],
        [pltpu.VMEM(own.shape, bf16)] + mode_scratch[1:],
    )
    across_even = lax.ppermute(
        lax.optimization_barrier((away, mine))[0], "segment", [(2, 0)]
    )
    for layer in range(1, segments):
        recv = to_all(mine)
        table = inv_table
        if layer == 1:
            table = jnp.asarray(y_inverse.reshape(2 * mode_count, cols), bf16)
        act, slope, y, mine = call(
            partial(forward_kernel, layer=layer),
            (recv, acts[-1], point_fwd, bias_cols, table, act_table, lx, xi),
            weights_of(layer), [field, field, ycoef, sent], mode_scratch + row_scratch,
        )
        acts.append(act)
        slopes.append(slope)
        ya.append(y)
        if layer == 1:
            across_even_on = lax.ppermute(
                lax.optimization_barrier((across_even, mine))[0], "segment", [(0, 1)]
            )

    recv = to_all(mine)
    last = segments - 1
    pre_grad, y, pg, mine = call(
        partial(top_kernel, layer=last, first_row=cot_row, **where),
        (recv, acts[last], grid_in, point_fwd, bias_cols, inv_table,
         proj_weight.T, proj_bias[:, None], proj_weight, out_weight.astype(f32)[:, None],
         grad_table, xa, xb),
        weights_of(last), [field, ycoef, point, sent], mode_scratch + row_scratch + top_scratch,
    )
    yg, pgs = ([y], [pg])
    for layer in reversed(range(last)):
        recv = to_all(mine)
        pre_grad, y, pg, mine = call(
            partial(backward_kernel, layer=layer),
            (recv, pre_grad, slopes[layer], acts[layer], point_back, fwd_table,
             grad_table, xa, xb),
            weights_of(layer), [field, ycoef, point, sent], mode_scratch + row_scratch,
        )
        yg.insert(0, y)
        pgs.insert(0, pg)

    pieces = ya + yg + pgs
    summary = jax.ShapeDtypeStruct((2 * x_half * 16 + c, lanes), f32)
    mine, theirs = pl.pallas_call(
        placed(partial(pick_kernel, layers=segments)),
        out_shape=[summary, summary],
        compiler_params=pltpu.CompilerParams(vmem_limit_bytes=VMEM_LIMIT),
        name="pick",
    )(*pieces)
    theirs = lax.ppermute(theirs, "segment", [(0, 1), (1, 0), (2, 3), (3, 2)])
    pieces = [mine, theirs, xz, xa]
    spectral, point_out = pl.pallas_call(
        partial(grads_kernel, scale=1.0 / math.sqrt(batch * x_count * cols)),
        grid=(owned,),
        in_specs=[whole(a) for a in pieces],
        out_specs=[
            pl.BlockSpec((1, kx, 2, c, c), lambda m: (m, 0, 0, 0, 0)),
            pl.BlockSpec((c, c), lambda m: (0, 0)),
        ],
        out_shape=[
            jax.ShapeDtypeStruct((owned, kx, 2, c, c), f32),
            jax.ShapeDtypeStruct((c, c), f32),
        ],
        scratch_shapes=[pltpu.VMEM((4 * kx, lanes), f32)] * 2,
        compiler_params=pltpu.CompilerParams(vmem_limit_bytes=VMEM_LIMIT),
        name="grads",
    )(*pieces)
    return (spectral[None], point_out[None])


def fits_replicated(mesh, inputs, point_weight, spectral_weight):
    segments, space = (mesh.shape["segment"], mesh.shape["space"])
    batch = inputs.shape[0] // mesh.shape["groups"]
    _, rows, depth, cols = inputs.shape
    layers, c, _ = point_weight.shape
    modes, kx = spectral_weight.shape[1:3]
    return (
        batch == 2
        and 2 * c == 128
        and layers == segments == 4
        and modes == 4 * space
        and space in (2, 4)
        and rows % (segments * space) == 0
        and rows % 32 == 0
        and rows <= 64
        and kx == 32
        and depth == 8
        and cols % 128 == 0
        and cols >= 3 * c
        and c * c % (space * cols) == 0
    )


def solution(mesh):
    in_specs = (
        P("groups", "space", None, None),
        P("groups", "space", None),
        P(),
        P(),
        P("segment", None, None),
        P("segment", None),
        P("segment", "space", None, None, None, None),
        P(),
        P(),
        P(),
    )
    out_specs = (
        P(("groups", "segment"), "space", None, None, None, None),
        P(("groups", "segment"), None, None),
    )

    def step(inputs, cotangent, lift_weight, lift_bias, point_weight, layer_bias, spectral_weight, *rest):
        fits = fits_replicated(mesh, inputs, point_weight, spectral_weight)
        mapped = jax.shard_map(
            replicated if fits else on_device,
            mesh=mesh, in_specs=in_specs, out_specs=out_specs, check_vma=False,
        )
        return mapped(
            inputs, cotangent, lift_weight, lift_bias, point_weight, layer_bias, spectral_weight, *rest
        )

    return step
```

```python
from functools import partial
import math

import jax
import jax.numpy as jnp
import numpy as np
from jax import lax
from jax.experimental import pallas as pl
from jax.experimental.pallas import tpu as pltpu
from jax.sharding import PartitionSpec as P

highest = lax.Precision.HIGHEST


def as_sent(array):
    return jax.tree.map(lambda a: a.astype(jnp.bfloat16) if a.dtype == jnp.float32 else a, array)


def passed_along(block, axis, distance):
    devices = range(lax.axis_size(axis))
    route = [(i - distance, i) for i in devices if i - distance in devices]
    return lax.ppermute(block, axis, route)


def y_tables(col_count, mode_count):
    ycells = jnp.arange(col_count, dtype=jnp.int32)[:, None]
    ymodes = jnp.arange(mode_count, dtype=jnp.int32)[None, :]
    angles = (ycells * ymodes % col_count).astype(jnp.float32) * (2.0 * math.pi / col_count)
    factor = 1.0 / math.sqrt(col_count)
    forward = jnp.stack([jnp.cos(angles), -jnp.sin(angles)], axis=1) * factor
    doubled = jnp.where(ymodes == 0, 1.0, 2.0).astype(jnp.float32)
    inverse = jnp.stack([doubled * jnp.cos(angles), -doubled * jnp.sin(angles)], axis=0) * factor
    return (forward.astype(jnp.bfloat16), jnp.transpose(inverse, (0, 2, 1)).astype(jnp.bfloat16))


def x_tables(row_total, mode_count):
    kx_count = 2 * mode_count
    indices = jnp.arange(kx_count, dtype=jnp.int32)
    freq_values = jnp.where(indices < mode_count, indices, indices - kx_count)
    xcells = jnp.arange(row_total, dtype=jnp.int32)
    angles = (freq_values[:, None] * xcells[None, :] % row_total).astype(jnp.float32) * (
        2.0 * math.pi / row_total
    )
    factor = 1.0 / math.sqrt(row_total)
    cosine_part = jnp.cos(angles) * factor
    sine_part = jnp.sin(angles) * factor
    forward = jnp.stack(
        [jnp.stack([cosine_part, sine_part], -1), jnp.stack([-sine_part, cosine_part], -1)], axis=1
    )
    cosine_flip = cosine_part.T
    sine_flip = sine_part.T
    inverse = jnp.stack(
        [jnp.stack([cosine_flip, -sine_flip], -1), jnp.stack([sine_flip, cosine_flip], -1)], axis=1
    )
    return (forward, inverse)


def mode_mult(coeffs, kernel):
    real_in, imag_in = (coeffs[:, :, 0], coeffs[:, :, 1])
    real_kernel, imag_kernel = (kernel[:, :, 0], kernel[:, :, 1])
    product = partial(jnp.einsum, "mjc,mjco->mjo", precision=highest)
    real_out = product(real_in, real_kernel) - product(imag_in, imag_kernel)
    imag_out = product(real_in, imag_kernel) + product(imag_in, real_kernel)
    return jnp.stack([real_out, imag_out], axis=2)


def mode_back(coeffs, mode_grads, kernel):
    real_in, imag_in = (coeffs[:, :, 0], coeffs[:, :, 1])
    real_grad, imag_grad = (mode_grads[:, :, 0], mode_grads[:, :, 1])
    real_kernel, imag_kernel = (kernel[:, :, 0], kernel[:, :, 1])
    outer_sum = partial(jnp.einsum, "mjc,mjo->mjco", precision=highest)
    inner_sum = partial(jnp.einsum, "mjo,mjco->mjc", precision=highest)
    kernel_real = outer_sum(real_in, real_grad) + outer_sum(imag_in, imag_grad)
    kernel_imag = outer_sum(real_in, imag_grad) - outer_sum(imag_in, real_grad)
    coeff_real = inner_sum(real_grad, real_kernel) + inner_sum(imag_grad, imag_kernel)
    coeff_imag = inner_sum(imag_grad, real_kernel) - inner_sum(real_grad, imag_kernel)
    return (
        jnp.stack([kernel_real, kernel_imag], axis=2),
        jnp.stack([coeff_real, coeff_imag], axis=2),
    )


def gelu_grad(pre_act, upstream):
    _, pullback = jax.vjp(jax.nn.gelu, pre_act)
    return pullback(upstream)[0]


def store_slot(buffer, value, slot_clip, is_valid):
    previous = lax.dynamic_index_in_dim(buffer, slot_clip, 0, keepdims=False)
    return lax.dynamic_update_index_in_dim(
        buffer, jnp.where(is_valid, value, previous), slot_clip, 0
    )


def on_device(
    inputs,
    cotangent,
    lift_weight,
    lift_bias,
    point_weight,
    layer_bias,
    spectral_weight,
    proj_weight,
    proj_bias,
    out_weight,
):
    batch_count, row_count, _, col_count = inputs.shape
    segment_count = lax.axis_size("segment")
    segment_index = lax.axis_index("segment")
    space_count = lax.axis_size("space")
    owned_modes = spectral_weight.shape[1]
    kx_count = spectral_weight.shape[2]
    channels = point_weight.shape[1]
    mode_count = kx_count // 2
    y_forward, y_inverse = y_tables(col_count, mode_count)
    x_forward, x_inverse = x_tables(row_count * space_count, mode_count)
    x_forward_adj = jnp.transpose(x_forward, (2, 3, 0, 1))
    x_inverse_adj = jnp.transpose(x_inverse, (2, 3, 0, 1))
    y_forward_wide = y_forward.astype(jnp.float32)
    y_inverse_wide = y_inverse.astype(jnp.float32)
    kernel = spectral_weight[0].astype(jnp.float32)
    point_matrix = point_weight[0]
    bias_vector = layer_bias[0]
    tick_count = batch_count + segment_count - 1

    def to_owners(y_coeffs, x_table):
        exchanged = lax.all_to_all(
            y_coeffs.astype(jnp.bfloat16), "space", split_axis=1, concat_axis=0, tiled=True
        ).astype(y_coeffs.dtype)
        return jnp.einsum("jqxp,xmpc->mjqc", x_table, exchanged, precision=highest)

    def from_owners(owned, x_table):
        spread = jnp.einsum("xpjq,mjqc->xmpc", x_table, owned, precision=highest)
        return lax.all_to_all(
            as_sent(spread), "space", split_axis=0, concat_axis=1, tiled=True
        ).astype(spread.dtype)

    def lifted(pick_slot):
        sample = lax.dynamic_index_in_dim(inputs, pick_slot, 0, keepdims=False)
        mixed = jnp.einsum("xty,tc->xcy", sample, lift_weight, preferred_element_type=jnp.float32)
        return (mixed + lift_bias[None, :, None]).astype(jnp.bfloat16)

    def forward_tick(state_now, tick_now):
        incoming, pre_store, act_store, mode_store = state_now
        pick_slot = jnp.clip(tick_now, 0, batch_count - 1)
        layer_in = lax.cond(segment_index == 0, lambda: lifted(pick_slot), lambda: incoming)
        y_coeffs = jnp.einsum(
            "xcy,ypm->xmpc", layer_in, y_forward, preferred_element_type=jnp.float32
        )
        coeffs = to_owners(y_coeffs, x_forward)
        back_rows = from_owners(mode_mult(coeffs, kernel), x_inverse)
        branch = jnp.einsum("xmpc,pmy->xcy", back_rows, y_inverse_wide, precision=highest)
        pointwise = jnp.einsum(
            "xcy,co->xoy", layer_in, point_matrix, preferred_element_type=jnp.float32
        )
        pre_act = pointwise + branch + bias_vector[None, :, None]
        slot_index = tick_now - segment_index
        is_valid = (slot_index >= 0) & (slot_index < batch_count)
        slot_clip = jnp.clip(slot_index, 0, batch_count - 1)
        pre_store = store_slot(pre_store, pre_act, slot_clip, is_valid)
        act_store = store_slot(act_store, layer_in, slot_clip, is_valid)
        mode_store = store_slot(mode_store, coeffs, slot_clip, is_valid)
        layer_out = jax.nn.gelu(pre_act).astype(jnp.bfloat16)
        sent = passed_along(layer_out, "segment", 1)
        return ((sent, pre_store, act_store, mode_store), None)

    start_state = (
        jnp.zeros((row_count, channels, col_count), jnp.bfloat16),
        jnp.zeros((batch_count, row_count, channels, col_count), jnp.float32),
        jnp.zeros((batch_count, row_count, channels, col_count), jnp.bfloat16),
        jnp.zeros((batch_count, owned_modes, kx_count, 2, channels), jnp.float32),
    )
    final_state, _ = lax.scan(forward_tick, start_state, jnp.arange(tick_count, dtype=jnp.int32))
    _, pre_store, act_store, mode_store = final_state

    def top_grad(slot_clip, pre_act):
        top_act = jax.nn.gelu(pre_act).astype(jnp.bfloat16)
        hidden = jnp.einsum("xcy,ck->xky", top_act, proj_weight, preferred_element_type=jnp.float32)
        hidden = hidden + proj_bias[None, :, None]
        target = lax.dynamic_index_in_dim(cotangent, slot_clip, 0, keepdims=False)
        upstream = (
            out_weight.astype(jnp.float32)[None, :, None] * target.astype(jnp.float32)[:, None, :]
        )
        hidden_grad = gelu_grad(hidden, upstream).astype(jnp.bfloat16)
        return jnp.einsum(
            "xky,ck->xcy", hidden_grad, proj_weight, preferred_element_type=jnp.float32
        ).astype(jnp.bfloat16)

    def backward_tick(state_now, tick_now):
        incoming, point_sum, kernel_sum = state_now
        slot_index = tick_now - (segment_count - 1 - segment_index)
        is_valid = (slot_index >= 0) & (slot_index < batch_count)
        slot_clip = jnp.clip(slot_index, 0, batch_count - 1)
        pre_act = lax.dynamic_index_in_dim(pre_store, slot_clip, 0, keepdims=False)
        layer_in = lax.dynamic_index_in_dim(act_store, slot_clip, 0, keepdims=False)
        coeffs = lax.dynamic_index_in_dim(mode_store, slot_clip, 0, keepdims=False)
        grad_out = lax.cond(
            segment_index == segment_count - 1,
            lambda: top_grad(slot_clip, pre_act),
            lambda: incoming,
        )
        pre_grad = gelu_grad(pre_act, grad_out.astype(jnp.float32)).astype(jnp.bfloat16)
        point_term = jnp.einsum(
            "xcy,xoy->co", layer_in, pre_grad, preferred_element_type=jnp.float32
        )
        y_grads = jnp.einsum(
            "xoy,pmy->xmpo", pre_grad, y_inverse, preferred_element_type=jnp.float32
        )
        mode_grads = to_owners(y_grads, x_inverse_adj)
        kernel_step, coeff_step = mode_back(coeffs, mode_grads, kernel)
        back_rows = from_owners(coeff_step, x_forward_adj)
        back_branch = jnp.einsum("xmpc,ypm->xcy", back_rows, y_forward_wide, precision=highest)
        pointwise_back = jnp.einsum(
            "co,xoy->xcy", point_matrix, pre_grad, preferred_element_type=jnp.float32
        )
        grad_in = (pointwise_back + back_branch).astype(jnp.bfloat16)
        point_sum = point_sum + jnp.where(is_valid, point_term, 0.0)
        kernel_sum = kernel_sum + jnp.where(is_valid, kernel_step, 0.0)
        sent = passed_along(grad_in, "segment", -1)
        return ((sent, point_sum, kernel_sum), None)

    back_start = (
        jnp.zeros((row_count, channels, col_count), jnp.bfloat16),
        jnp.zeros((channels, channels), jnp.float32),
        jnp.zeros((owned_modes, kx_count, 2, channels, channels), jnp.float32),
    )
    back_state, _ = lax.scan(backward_tick, back_start, jnp.arange(tick_count, dtype=jnp.int32))
    _, point_sum, kernel_sum = back_state
    point_total = lax.psum(point_sum, "space")
    factor = 1.0 / math.sqrt(batch_count * row_count * space_count * col_count)
    return (kernel_sum[None], (point_total * factor)[None])


f32, bf16 = (jnp.float32, jnp.bfloat16)
NT = (((1,), (1,)), ((), ()))
NN = (((1,), (0,)), ((), ()))
VMEM_LIMIT = 50 << 20


def np_y_tables(col_count, mode_count):
    ycells = np.arange(col_count)[:, None]
    ymodes = np.arange(mode_count)[None, :]
    angles = (ycells * ymodes % col_count) * (2.0 * math.pi / col_count)
    factor = 1.0 / math.sqrt(col_count)
    doubled = np.where(ymodes == 0, 1.0, 2.0)
    forward = np.stack([np.cos(angles), -np.sin(angles)], axis=0) * factor
    inverse = np.stack([doubled * np.cos(angles), -doubled * np.sin(angles)], axis=0) * factor
    return (forward.transpose(2, 0, 1), inverse.transpose(2, 0, 1))


def np_x_tables(row_total, mode_count):
    kx_count = 2 * mode_count
    indices = np.arange(kx_count)
    freq = np.where(indices < mode_count, indices, indices - kx_count)
    angles = (freq[:, None] * np.arange(row_total)[None, :] % row_total) * (2.0 * math.pi / row_total)
    factor = 1.0 / math.sqrt(row_total)
    c, s = (np.cos(angles) * factor, np.sin(angles) * factor)
    forward = np.stack([np.stack([c, s], -1), np.stack([-s, c], -1)], axis=1)
    inverse = np.stack([np.stack([c.T, -s.T], -1), np.stack([s.T, c.T], -1)], axis=1)
    return (forward, inverse)


def hdot(a, b):
    return jnp.dot(a, b, precision=highest, preferred_element_type=f32)


def gelu_both(v):
    k0 = math.sqrt(2.0 / math.pi)
    k1 = k0 * 0.044715
    v2 = v * v
    share = 0.5 + 0.5 * jnp.tanh(v * (k0 + k1 * v2))
    value = v * share
    slope = share + value * (1.0 - share) * (2.0 * k0 + (6.0 * k1) * v2)
    return (value, slope)


def low_half(shape):
    return lax.broadcasted_iota(jnp.int32, shape, 1) < shape[1] // 2


def swap_halves(a):
    return pltpu.roll(a, a.shape[1] // 2, 1)


def cross(a, b):
    low = low_half(a.shape)
    return (jnp.where(low, a, swap_halves(b)), jnp.where(low, swap_halves(a), b))


def grid_rows(first_ref, first, second_ref, second, x_half):
    parts = []
    for p in range(2):
        parts += cross(
            first_ref[pl.ds(first + p, x_half, stride=16), :],
            second_ref[pl.ds(second + p, x_half, stride=16), :],
        )
    return jnp.concatenate(parts, axis=0)


def own_grid(y_ref, row=8):
    return grid_rows(y_ref, row, y_ref, row + 2, y_ref.shape[0] // 16)


def put_chunk(grid, out_ref, first=0):
    x_half = grid.shape[0] // 4
    for p in range(2):
        base = 2 * p * x_half
        pair = cross(grid[base : base + x_half], grid[base + x_half : base + 2 * x_half])
        for mode in range(2):
            at = first + (2 * mode + p) * x_half
            block = pair[mode].astype(bf16)
            for k in range(out_ref.shape[0]):
                out_ref[k, at : at + x_half] = block


def put_split(t_ref, mode, rows):
    count = rows.shape[0]
    high = rows.astype(bf16).astype(f32)
    t_ref[2 * mode * count : (2 * mode + 1) * count] = high
    t_ref[(2 * mode + 1) * count : (2 * mode + 2) * count] = rows - high


def mode_products(t_ref, w_ref, m_ref, dims, start=0):
    pairs = w_ref.shape[1]
    for j in range(pairs):
        for mode in range(2):
            at = pl.ds(mode * 8 * pairs + j, 8, stride=pairs)
            m_ref[at, :] = lax.dot_general(
                t_ref[at, :].astype(bf16), w_ref[start + mode, j], dims, preferred_element_type=f32
            )
    count = 4 * pairs
    return [
        m_ref[2 * mode * count : (2 * mode + 1) * count]
        + m_ref[(2 * mode + 1) * count : (2 * mode + 2) * count]
        for mode in range(2)
    ]


def first_kx(shape, pairs):
    return (lax.broadcasted_iota(jnp.int32, shape, 0) // pairs) % 2 == 0


def forward_modes(y_ref, w_ref, lx_ref, xi_ref, t_ref, m_ref, out_ref, row=8, start=0):
    pairs = w_ref.shape[1]
    ys = own_grid(y_ref, row)
    sw = swap_halves(ys)
    low = low_half(ys.shape)
    zero = jnp.zeros_like(ys)
    put_split(t_ref, 0, hdot(lx_ref[...], jnp.concatenate([jnp.where(low, ys, zero), jnp.where(low, zero, sw)], axis=0)))
    put_split(t_ref, 1, hdot(lx_ref[...], jnp.concatenate([jnp.where(low, sw, zero), jnp.where(low, zero, ys)], axis=0)))
    m0, m1 = mode_products(t_ref, w_ref, m_ref, NN, start)
    first = first_kx(m0.shape, pairs)
    s0 = jnp.where(first, m0, swap_halves(m0))
    s1 = jnp.where(first, swap_halves(m1), m1)
    first_row = start * out_ref.shape[1] // w_ref.shape[0]
    put_chunk(hdot(xi_ref[...], jnp.where(low_half(m0.shape), s0, s1)), out_ref, first_row)


def backward_modes(y_ref, w_ref, xa_ref, xf_ref, t_ref, m_ref, out_ref):
    pairs = w_ref.shape[1]
    g = hdot(xa_ref[...], own_grid(y_ref))
    sw = swap_halves(g)
    first = first_kx(g.shape, pairs)
    keep = low_half(g.shape) == first
    zero = jnp.zeros_like(g)
    put_split(t_ref, 0, jnp.where(keep, jnp.where(first, g, sw), zero))
    put_split(t_ref, 1, jnp.where(keep, jnp.where(first, sw, g), zero))
    m0, m1 = mode_products(t_ref, w_ref, m_ref, NT)
    half = 2 * pairs
    pr0, pi0, pr1, pi1 = (m0[:half], m0[half:], m1[:half], m1[half:])
    low = low_half(pr0.shape)
    real = jnp.where(low, pr0 + swap_halves(pi0), swap_halves(pr1) + pi1)
    imag = jnp.where(low, pi0 - swap_halves(pr0), swap_halves(pi1) - pr1)
    put_chunk(hdot(xf_ref[...], jnp.concatenate([real, imag], axis=0)), out_ref)


def choose_kernel(seg_ref, layer, w_refs, w_ref, sem, start):
    for seg in range(4):
        pair = seg // 2
        source = w_refs[(0 if seg % 2 == layer % 2 else 1) + (0 if pair == layer // 2 else 2)]
        if pair == layer // 2:
            source = source.at[2 * pair : 2 * pair + 2]

        @pl.when(seg_ref[0] == seg)
        def _(source=source):
            copy = pltpu.make_async_copy(source, w_ref, sem)
            if start:
                copy.start()
            else:
                copy.wait()


def choose_all(seg_ref, w_refs, w_ref, sem, start):
    for lane in range(2):
        @pl.when(seg_ref[0] % 2 == lane)
        def _(lane=lane):
            copy = pltpu.make_async_copy(w_refs[lane], w_ref, sem)
            if start:
                copy.start()
            else:
                copy.wait()


def pack_kernel(in_ref, out_ref):
    out_ref[...] = jnp.concatenate([in_ref[:, 0], in_ref[:, 1]], axis=-1)


def widen(recv_ref, r_ref):
    rows = recv_ref.shape[1]
    for k in range(r_ref.shape[0] // rows):
        r_ref[k * rows : (k + 1) * rows] = recv_ref[k].astype(f32)


def row_product(weight, field, r_ref, table, x, x_half):
    rows = r_ref[pl.ds(x, table.shape[0], stride=x_half), :]
    lhs = jnp.concatenate([weight, rows.T.astype(bf16)], axis=1)
    return jnp.dot(lhs, jnp.concatenate([field, table], axis=0), preferred_element_type=f32)


def chunk_of(x, half_side, space, rows, per_chunk):
    inner = x % rows
    return ((inner // per_chunk) * space + half_side * (space // 2) + x // rows, inner % per_chunk)


def lift_kernel(seg_ref, in_ref, lw_ref, lb_ref, tab_ref, act_ref, y_ref, *, space, rows, per_chunk, depth):
    table = tab_ref[seg_ref[1]]
    for x in range(act_ref.shape[0]):
        cells = []
        for side in range(2):
            k, i = chunk_of(x, side, space, rows, per_chunk)
            cells.append(in_ref[k, i * depth : (i + 1) * depth, :])
        cells = jnp.concatenate(cells, axis=0)
        act = jnp.dot(lw_ref[...], cells, preferred_element_type=f32) + lb_ref[...]
        act = act.astype(bf16)
        act_ref[x] = act
        y_ref[x * 16 : (x + 1) * 16] = lax.dot_general(
            table, act, NT, preferred_element_type=f32
        )


def first_modes_kernel(seg_ref, y_ref, lx_ref, xi_ref, w0, w1, out_ref, w_ref, sem, t_ref, m_ref):
    choose_all(seg_ref, (w0, w1), w_ref, sem, True)
    choose_all(seg_ref, (w0, w1), w_ref, sem, False)
    for start in range(0, w_ref.shape[0], 2):
        forward_modes(y_ref, w_ref, lx_ref, xi_ref, t_ref, m_ref, out_ref, 2 * start, start)


def in_pairs(count, start, finish, scratch):
    start(0, scratch[0])

    def two(i, carry):
        x = 2 * i
        start(x + 1, scratch[1])
        finish(x, scratch[0])
        start(jnp.minimum(x + 2, count - 1), scratch[0])
        finish(x + 1, scratch[1])
        return carry

    lax.fori_loop(0, count // 2, two, 0)


def put_rows(y_ref, x, rows):
    y_ref[pl.ds(pl.multiple_of(x * 16, 16), 16), :] = rows


def forward_kernel(
    seg_ref, recv_ref, act_ref, pw_ref, pb_ref, inv_ref, tab_ref, lx_ref, xi_ref, w0, w1, w2, w3,
    next_ref, slope_ref, y_ref, out_ref, w_ref, sem, t_ref, m_ref, r_ref, p0_ref, p1_ref, *, layer,
):
    x_half = act_ref.shape[0]
    choose_kernel(seg_ref, layer, (w0, w1, w2, w3), w_ref, sem, True)
    widen(recv_ref, r_ref)
    table = tab_ref.at[seg_ref[1]]

    def start(x, ref):
        ref[...] = row_product(pw_ref[layer - 1], act_ref[x], r_ref, inv_ref[...], x, x_half)

    def finish(x, ref):
        value, slope = gelu_both(ref[...] + pb_ref[layer - 1])
        value = value.astype(bf16)
        next_ref[x] = value
        slope_ref[x] = slope.astype(bf16)
        put_rows(y_ref, x, lax.dot_general(table[...], value, NT, preferred_element_type=f32))

    in_pairs(x_half, start, finish, (p0_ref, p1_ref))
    choose_kernel(seg_ref, layer, (w0, w1, w2, w3), w_ref, sem, False)
    forward_modes(y_ref, w_ref, lx_ref, xi_ref, t_ref, m_ref, out_ref)


def adjoint_rows(x, grad, act, table, pre_ref, y_ref, point_ref):
    pre_grad = grad.astype(bf16)
    pre_ref[x] = pre_grad
    both = lax.dot_general(
        jnp.concatenate([table[...], act], axis=0), pre_grad, NT, preferred_element_type=f32
    )
    put_rows(y_ref, x, both[:16])
    point_ref[...] += both[16:]


def top_kernel(
    seg_ref, recv_ref, act_ref, in_ref, pw_ref, pb_ref, inv_ref, up_ref, hb_ref, down_ref, ow_ref,
    tab_ref, xa_ref, xf_ref, w0, w1, w2, w3,
    pre_ref, y_ref, point_ref, out_ref, w_ref, sem, t_ref, m_ref, r_ref,
    p0_ref, p1_ref, s0_ref, s1_ref, h0_ref, h1_ref,
    *, layer, space, rows, per_chunk, first_row,
):
    x_half = act_ref.shape[0]
    choose_kernel(seg_ref, layer, (w0, w1, w2, w3), w_ref, sem, True)
    widen(recv_ref, r_ref)
    point_ref[...] = jnp.zeros_like(point_ref)
    table = tab_ref.at[seg_ref[1]]
    hidden_count = up_ref.shape[0]
    size = act_ref.shape[1] // 2

    def start(x, ref):
        ref[...] = row_product(pw_ref[layer], act_ref[x], r_ref, inv_ref[...], x, x_half)

    def middle(ref, slope_ref, hidden_ref):
        value, slope = gelu_both(ref[...] + pb_ref[layer])
        slope_ref[...] = slope
        value = value.astype(bf16)
        for side in range(2):
            hidden_ref[side * hidden_count : (side + 1) * hidden_count] = jnp.dot(
                up_ref[...], value[side * size : (side + 1) * size], preferred_element_type=f32
            )

    def finish(x, slope_ref, hidden_ref):
        grads = []
        for side in range(2):
            hidden = hidden_ref[side * hidden_count : (side + 1) * hidden_count]
            _, hidden_slope = gelu_both(hidden + hb_ref[...])
            chunk, within = chunk_of(x, side, space, rows, per_chunk)
            cots = in_ref[chunk, first_row : first_row + per_chunk, :].astype(f32)
            cot = cots[:1]
            for other in range(1, per_chunk):
                cot = jnp.where(within == other, cots[other : other + 1], cot)
            grads.append(
                cot * jnp.dot(
                    down_ref[...], (hidden_slope * ow_ref[...]).astype(bf16), preferred_element_type=f32
                )
            )
        grad = jnp.concatenate(grads, axis=0) * slope_ref[...]
        adjoint_rows(x, grad, act_ref[x], table, pre_ref, y_ref, point_ref)

    last = x_half - 1
    start(0, p0_ref)
    middle(p0_ref, s0_ref, h0_ref)
    start(1, p1_ref)

    def two(i, carry):
        x = 2 * i
        start(jnp.minimum(x + 2, last), p0_ref)
        middle(p1_ref, s1_ref, h1_ref)
        finish(x, s0_ref, h0_ref)
        start(jnp.minimum(x + 3, last), p1_ref)
        middle(p0_ref, s0_ref, h0_ref)
        finish(x + 1, s1_ref, h1_ref)
        return carry

    lax.fori_loop(0, x_half // 2, two, 0)
    choose_kernel(seg_ref, layer, (w0, w1, w2, w3), w_ref, sem, False)
    backward_modes(y_ref, w_ref, xa_ref, xf_ref, t_ref, m_ref, out_ref)


def backward_kernel(
    seg_ref, recv_ref, grad_ref, slope_ref, act_ref, pw_ref, fwd_ref, tab_ref, xa_ref, xf_ref,
    w0, w1, w2, w3,
    pre_ref, y_ref, point_ref, out_ref, w_ref, sem, t_ref, m_ref, r_ref, p0_ref, p1_ref, *, layer,
):
    x_half = act_ref.shape[0]
    if layer:
        choose_kernel(seg_ref, layer, (w0, w1, w2, w3), w_ref, sem, True)
    widen(recv_ref, r_ref)
    point_ref[...] = jnp.zeros_like(point_ref)
    table = tab_ref.at[seg_ref[1]]

    def start(x, ref):
        ref[...] = row_product(pw_ref[layer + 1], grad_ref[x], r_ref, fwd_ref[...], x, x_half)

    def finish(x, ref):
        grad = ref[...] * slope_ref[x].astype(f32)
        adjoint_rows(x, grad, act_ref[x], table, pre_ref, y_ref, point_ref)

    in_pairs(x_half, start, finish, (p0_ref, p1_ref))
    if layer:
        choose_kernel(seg_ref, layer, (w0, w1, w2, w3), w_ref, sem, False)
        backward_modes(y_ref, w_ref, xa_ref, xf_ref, t_ref, m_ref, out_ref)
    else:
        out_ref[...] = jnp.zeros_like(out_ref)


def pick_kernel(seg_ref, *refs, layers):
    ya_refs, yg_refs, pg_refs = (refs[:layers], refs[layers : 2 * layers], refs[2 * layers : 3 * layers])
    count = ya_refs[0].shape[0]
    seg = seg_ref[0]
    partner = seg + 1 - 2 * (seg % 2)
    for out_ref, wanted in zip(refs[3 * layers :], (seg, partner)):
        for layer in range(layers):
            @pl.when(wanted == layer)
            def _(layer=layer, out_ref=out_ref):
                out_ref[:count] = ya_refs[layer][...]
                out_ref[count : 2 * count] = yg_refs[layer][...]
                pg = pg_refs[layer][...]
                half = pg.shape[0] // 2
                out_ref[2 * count :] = pg[:half] + swap_halves(pg[half:])


def grads_kernel(mine_ref, theirs_ref, xz_ref, xa_ref, out_ref, point_ref, a_ref, b_ref, *, scale):
    mode = pl.program_id(0)
    c = point_ref.shape[0]
    count = (mine_ref.shape[0] - c) // 2
    x_half = count // 16

    @pl.when(mode == 0)
    def _():
        point_ref[...] = (mine_ref[2 * count :, :c] + theirs_ref[2 * count :, :c]) * scale

    z = hdot(xz_ref[...], grid_rows(mine_ref, 2 * mode, theirs_ref, 2 * mode, x_half))
    at = count + 2 * mode
    g = hdot(xa_ref[...], grid_rows(mine_ref, at, theirs_ref, at, x_half))
    rows = z.shape[0]
    kx = rows // 2
    zs, gs = (swap_halves(z), swap_halves(g))
    a_ref[:rows] = z
    a_ref[rows:] = zs
    low = low_half((kx, z.shape[1]))
    b_ref[:kx] = jnp.where(low, g[:kx], gs[kx:])
    b_ref[kx:rows] = jnp.where(low, g[kx:], -gs[:kx])
    b_ref[rows : rows + kx] = jnp.where(low, gs[:kx], g[kx:])
    b_ref[rows + kx :] = jnp.where(low, gs[kx:], -g[:kx])
    for j in range(kx):
        a = a_ref[pl.ds(j, 4, stride=kx), :][:, :c]
        b = b_ref[pl.ds(j, 4, stride=kx), :]
        ah, bh = (a.astype(bf16).astype(f32), b.astype(bf16).astype(f32))
        left = jnp.concatenate([ah, a - ah, ah], axis=0).T.astype(bf16)
        right = jnp.concatenate([bh, bh, b - bh], axis=0).astype(bf16)
        out_ref[0, j, 0] = jnp.dot(left, right[:, :c], preferred_element_type=f32)
        out_ref[0, j, 1] = jnp.dot(left, right[:, c:], preferred_element_type=f32)


def replicated(
    inputs, cotangent, lift_weight, lift_bias, point_weight, layer_bias, spectral_weight,
    proj_weight, proj_bias, out_weight,
):
    batch, row_count, depth, cols = inputs.shape
    segments, space = (lax.axis_size("segment"), lax.axis_size("space"))
    seg, place = (lax.axis_index("segment"), lax.axis_index("space"))
    pair = seg // 2
    both = ("segment", "space")
    owned, kx = spectral_weight.shape[1:3]
    c = point_weight.shape[1]
    x_count = row_count * space
    x_half = x_count // 2
    mode_count = owned * space
    per_chunk = row_count // segments
    pairs = kx // 2
    group = segments // 2 * space

    cells = lax.dynamic_slice_in_dim(inputs, seg * per_chunk, per_chunk, 1)
    cells = cells.reshape(batch, per_chunk * depth, cols)
    cots = lax.dynamic_slice_in_dim(cotangent, seg * per_chunk, per_chunk, 1)
    weight_rows = c * c // space // cols
    share = lax.dynamic_index_in_dim(
        point_weight.reshape(space, weight_rows, cols), place, 0, keepdims=False
    )
    high = lax.reduce_precision(layer_bias[0], 8, 7)
    mid = lax.reduce_precision(layer_bias[0] - high, 8, 7)
    rest = layer_bias[0] - high - mid
    bias_row = jnp.concatenate([high, mid, rest, jnp.zeros((cols - 3 * c,), f32)]).astype(bf16)
    common = jnp.concatenate([share, bias_row[None]], axis=0)
    chunk = jnp.concatenate([cells, cots, jnp.broadcast_to(common[None], (batch,) + common.shape)], axis=1)
    cot_row = per_chunk * depth
    share_row = cot_row + per_chunk
    bias_at = share_row + weight_rows
    chunk = jnp.pad(chunk, ((0, 0), (0, -chunk.shape[1] % 8), (0, 0)))
    chunk = jnp.broadcast_to(chunk[None, :, None], (segments // 2, batch, space) + chunk.shape[1:])
    stack = spectral_weight[0].reshape(owned, 2, pairs, 2 * c, c)
    pack = pl.pallas_call(
        pack_kernel,
        grid=(owned,),
        in_specs=[pl.BlockSpec((1, 2, pairs, 2 * c, c), lambda m: (m, 0, 0, 0, 0))],
        out_specs=pl.BlockSpec((1, pairs, 2 * c, 2 * c), lambda m: (m, 0, 0, 0)),
        out_shape=jax.ShapeDtypeStruct((owned, pairs, 2 * c, 2 * c), bf16),
        compiler_params=pltpu.CompilerParams(vmem_limit_bytes=VMEM_LIMIT),
        name="pack",
    )
    own = pack(stack)
    swap = [(0, 1), (1, 0), (2, 3), (3, 2)]
    neighbour = lax.ppermute(own, "segment", swap)
    away = lax.dynamic_slice_in_dim(own, 2 * (1 - pair), 2, 0)
    across_odd = lax.ppermute(away, "segment", [(1, 3), (3, 1)])

    grid_in = lax.all_to_all(
        chunk.reshape((segments * space,) + chunk.shape[3:]), both, 0, 0, tiled=True
    )

    def weights_of(layer):
        if layer % 2:
            return (own, neighbour, across_odd, across_odd_on)
        return (own, neighbour, across_even, across_even_on)

    points = grid_in[:, share_row:bias_at].reshape(segments, c, c)
    bias_parts = grid_in[::space, bias_at, : 3 * c].astype(f32).reshape(segments, 3, c)
    biases = bias_parts[:, 0] + bias_parts[:, 1] + bias_parts[:, 2]
    blank = jnp.zeros((segments, c, c), bf16)

    def doubled(mats):
        return jnp.concatenate(
            [jnp.concatenate([mats, blank], axis=2), jnp.concatenate([blank, mats], axis=2)], axis=1
        )

    point_back = doubled(points)
    point_fwd = doubled(jnp.transpose(points, (0, 2, 1)))
    bias_cols = jnp.concatenate([biases] * 2, axis=1)[:, :, None]

    y_forward, y_inverse = np_y_tables(cols, mode_count)
    x_forward, x_inverse = np_x_tables(x_count, kx // 2)
    firsts = [k % space * owned + k // space * 2 for k in range(group)]
    order = [first + i for first in firsts for i in range(2)]

    def gathered(table):
        return jnp.asarray(table[order].reshape(4 * group, cols), bf16)

    def analysis(table):
        full = np.zeros((group, 16, cols))
        for k in range(group):
            s = k % space
            full[k, : 2 * owned] = table[s * owned : (s + 1) * owned].reshape(2 * owned, cols)
            full[k, 8:12] = table[firsts[k] : firsts[k] + 2].reshape(4, cols)
        return jnp.asarray(full, bf16)

    inv_table, fwd_table = (gathered(y_inverse), gathered(y_forward))
    act_table, grad_table = (analysis(y_forward), analysis(y_inverse))
    xf = x_forward.transpose(0, 1, 3, 2).reshape(kx, 2, 2 * x_count)
    lx = np.concatenate(
        [np.concatenate([xf[:, 0], -xf[:, 1]], 1), np.concatenate([xf[:, 1], xf[:, 0]], 1)], 0
    )
    xz = xf.transpose(1, 0, 2).reshape(2 * kx, 2 * x_count)
    xi = x_inverse.transpose(1, 0, 3, 2).reshape(2 * x_count, 2 * kx)
    lx, xz, xi, xa, xb = (jnp.asarray(t, f32) for t in (lx, xz, xi, xi.T.copy(), xz.T.copy()))

    device_lists = [
        [(2 * k + lane) * space + s for k in range(segments // 2) for s in range(space)]
        for lane in range(2)
    ]

    def to_all(block):
        return lax.all_to_all(block, both, 0, 0, tiled=True, axis_index_groups=device_lists)

    def whole(array):
        rank = len(array.shape)
        return pl.BlockSpec(array.shape, lambda *i: (0,) * rank)

    def placed(kernel):
        def body(*refs):
            own_seg = lax.axis_index("segment")
            kernel((own_seg, own_seg // 2 * space + lax.axis_index("space")), *refs)

        return body


    def call(kernel, args, weights, outs, scratch):
        near = pl.BlockSpec(memory_space=pltpu.VMEM)
        return pl.pallas_call(
            placed(kernel),
            in_specs=[near] * len(args)
            + [pl.BlockSpec(memory_space=pl.ANY)] * len(weights),
            out_specs=[near] * len(outs),
            out_shape=outs,
            scratch_shapes=scratch,
            compiler_params=pltpu.CompilerParams(vmem_limit_bytes=VMEM_LIMIT),
        )(*args, *weights)

    lanes = 2 * c
    field = jax.ShapeDtypeStruct((x_half, lanes, cols), bf16)
    ycoef = jax.ShapeDtypeStruct((x_half * 16, lanes), f32)
    sent = jax.ShapeDtypeStruct((group, 2 * x_count, lanes), bf16)
    sent_first = jax.ShapeDtypeStruct((group, 4 * x_count, lanes), bf16)
    point = jax.ShapeDtypeStruct((lanes, lanes), f32)
    mode_scratch = [
        pltpu.VMEM((2,) + own.shape[1:], bf16), pltpu.SemaphoreType.DMA(()),
        pltpu.VMEM((8 * kx, lanes), f32), pltpu.VMEM((8 * kx, lanes), f32),
    ]
    row = pltpu.VMEM((lanes, cols), f32)
    row_scratch = [pltpu.VMEM((group * 2 * x_count, lanes), f32), row, row]
    top_scratch = [row, row] + [pltpu.VMEM((2 * proj_weight.shape[1], cols), f32)] * 2

    zero = jnp.zeros_like(lift_weight.T)
    lift = jnp.concatenate(
        [jnp.concatenate([lift_weight.T, zero], 1), jnp.concatenate([zero, lift_weight.T], 1)], 0
    )
    lift_col = jnp.concatenate([lift_bias] * 2)[:, None]
    where = dict(space=space, rows=row_count, per_chunk=per_chunk)
    act, y0 = pl.pallas_call(
        placed(partial(lift_kernel, depth=depth, **where)),
        out_shape=[field, ycoef],
        compiler_params=pltpu.CompilerParams(vmem_limit_bytes=VMEM_LIMIT),
        name="lift",
    )(grid_in, lift, lift_col, act_table)
    acts, slopes, ya = ([act], [], [y0])
    (mine,) = call(
        first_modes_kernel, (y0, lx, xi), (own, neighbour), [sent_first],
        [pltpu.VMEM(own.shape, bf16)] + mode_scratch[1:],
    )
    across_even = lax.ppermute(
        lax.optimization_barrier((away, mine))[0], "segment", [(2, 0)]
    )
    for layer in range(1, segments):
        recv = to_all(mine)
        table = inv_table
        if layer == 1:
            across_odd_on = lax.ppermute(
                lax.optimization_barrier((across_odd, recv))[0], "segment", [(1, 0), (3, 2)]
            )
            table = jnp.asarray(y_inverse.reshape(2 * mode_count, cols), bf16)
        act, slope, y, mine = call(
            partial(forward_kernel, layer=layer),
            (recv, acts[-1], point_fwd, bias_cols, table, act_table, lx, xi),
            weights_of(layer), [field, field, ycoef, sent], mode_scratch + row_scratch,
        )
        acts.append(act)
        slopes.append(slope)
        ya.append(y)
        if layer == 1:
            across_even_on = lax.ppermute(
                lax.optimization_barrier((across_even, mine))[0], "segment", [(0, 1)]
            )

    recv = to_all(mine)
    last = segments - 1
    pre_grad, y, pg, mine = call(
        partial(top_kernel, layer=last, first_row=cot_row, **where),
        (recv, acts[last], grid_in, point_fwd, bias_cols, inv_table,
         proj_weight.T, proj_bias[:, None], proj_weight, out_weight.astype(f32)[:, None],
         grad_table, xa, xb),
        weights_of(last), [field, ycoef, point, sent], mode_scratch + row_scratch + top_scratch,
    )
    yg, pgs = ([y], [pg])
    for layer in reversed(range(last)):
        recv = to_all(mine)
        pre_grad, y, pg, mine = call(
            partial(backward_kernel, layer=layer),
            (recv, pre_grad, slopes[layer], acts[layer], point_back, fwd_table,
             grad_table, xa, xb),
            weights_of(layer), [field, ycoef, point, sent], mode_scratch + row_scratch,
        )
        yg.insert(0, y)
        pgs.insert(0, pg)

    pieces = ya + yg + pgs
    summary = jax.ShapeDtypeStruct((2 * x_half * 16 + c, lanes), f32)
    mine, theirs = pl.pallas_call(
        placed(partial(pick_kernel, layers=segments)),
        out_shape=[summary, summary],
        compiler_params=pltpu.CompilerParams(vmem_limit_bytes=VMEM_LIMIT),
        name="pick",
    )(*pieces)
    theirs = lax.ppermute(theirs, "segment", [(0, 1), (1, 0), (2, 3), (3, 2)])
    pieces = [mine, theirs, xz, xa]
    spectral, point_out = pl.pallas_call(
        partial(grads_kernel, scale=1.0 / math.sqrt(batch * x_count * cols)),
        grid=(owned,),
        in_specs=[whole(a) for a in pieces],
        out_specs=[
            pl.BlockSpec((1, kx, 2, c, c), lambda m: (m, 0, 0, 0, 0)),
            pl.BlockSpec((c, c), lambda m: (0, 0)),
        ],
        out_shape=[
            jax.ShapeDtypeStruct((owned, kx, 2, c, c), f32),
            jax.ShapeDtypeStruct((c, c), f32),
        ],
        scratch_shapes=[pltpu.VMEM((4 * kx, lanes), f32)] * 2,
        compiler_params=pltpu.CompilerParams(vmem_limit_bytes=VMEM_LIMIT),
        name="grads",
    )(*pieces)
    return (spectral[None], point_out[None])


def fits_replicated(mesh, inputs, point_weight, spectral_weight):
    segments, space = (mesh.shape["segment"], mesh.shape["space"])
    batch = inputs.shape[0] // mesh.shape["groups"]
    _, rows, depth, cols = inputs.shape
    layers, c, _ = point_weight.shape
    modes, kx = spectral_weight.shape[1:3]
    return (
        batch == 2
        and 2 * c == 128
        and layers == segments == 4
        and modes == 4 * space
        and space in (2, 4)
        and rows % (segments * space) == 0
        and rows % 32 == 0
        and rows <= 64
        and kx == 32
        and depth == 8
        and cols % 128 == 0
        and cols >= 3 * c
        and c * c % (space * cols) == 0
    )


def solution(mesh):
    in_specs = (
        P("groups", "space", None, None),
        P("groups", "space", None),
        P(),
        P(),
        P("segment", None, None),
        P("segment", None),
        P("segment", "space", None, None, None, None),
        P(),
        P(),
        P(),
    )
    out_specs = (
        P(("groups", "segment"), "space", None, None, None, None),
        P(("groups", "segment"), None, None),
    )

    def step(inputs, cotangent, lift_weight, lift_bias, point_weight, layer_bias, spectral_weight, *rest):
        fits = fits_replicated(mesh, inputs, point_weight, spectral_weight)
        mapped = jax.shard_map(
            replicated if fits else on_device,
            mesh=mesh, in_specs=in_specs, out_specs=out_specs, check_vma=False,
        )
        return mapped(
            inputs, cotangent, lift_weight, lift_bias, point_weight, layer_bias, spectral_weight, *rest
        )

    return step
```

```python
from functools import partial
import math

import jax
import jax.numpy as jnp
import numpy as np
from jax import lax
from jax.experimental import pallas as pl
from jax.experimental.pallas import tpu as pltpu
from jax.sharding import PartitionSpec as P

highest = lax.Precision.HIGHEST


def as_sent(array):
    return jax.tree.map(lambda a: a.astype(jnp.bfloat16) if a.dtype == jnp.float32 else a, array)


def passed_along(block, axis, distance):
    devices = range(lax.axis_size(axis))
    route = [(i - distance, i) for i in devices if i - distance in devices]
    return lax.ppermute(block, axis, route)


def y_tables(col_count, mode_count):
    ycells = jnp.arange(col_count, dtype=jnp.int32)[:, None]
    ymodes = jnp.arange(mode_count, dtype=jnp.int32)[None, :]
    angles = (ycells * ymodes % col_count).astype(jnp.float32) * (2.0 * math.pi / col_count)
    factor = 1.0 / math.sqrt(col_count)
    forward = jnp.stack([jnp.cos(angles), -jnp.sin(angles)], axis=1) * factor
    doubled = jnp.where(ymodes == 0, 1.0, 2.0).astype(jnp.float32)
    inverse = jnp.stack([doubled * jnp.cos(angles), -doubled * jnp.sin(angles)], axis=0) * factor
    return (forward.astype(jnp.bfloat16), jnp.transpose(inverse, (0, 2, 1)).astype(jnp.bfloat16))


def x_tables(row_total, mode_count):
    kx_count = 2 * mode_count
    indices = jnp.arange(kx_count, dtype=jnp.int32)
    freq_values = jnp.where(indices < mode_count, indices, indices - kx_count)
    xcells = jnp.arange(row_total, dtype=jnp.int32)
    angles = (freq_values[:, None] * xcells[None, :] % row_total).astype(jnp.float32) * (
        2.0 * math.pi / row_total
    )
    factor = 1.0 / math.sqrt(row_total)
    cosine_part = jnp.cos(angles) * factor
    sine_part = jnp.sin(angles) * factor
    forward = jnp.stack(
        [jnp.stack([cosine_part, sine_part], -1), jnp.stack([-sine_part, cosine_part], -1)], axis=1
    )
    cosine_flip = cosine_part.T
    sine_flip = sine_part.T
    inverse = jnp.stack(
        [jnp.stack([cosine_flip, -sine_flip], -1), jnp.stack([sine_flip, cosine_flip], -1)], axis=1
    )
    return (forward, inverse)


def mode_mult(coeffs, kernel):
    real_in, imag_in = (coeffs[:, :, 0], coeffs[:, :, 1])
    real_kernel, imag_kernel = (kernel[:, :, 0], kernel[:, :, 1])
    product = partial(jnp.einsum, "mjc,mjco->mjo", precision=highest)
    real_out = product(real_in, real_kernel) - product(imag_in, imag_kernel)
    imag_out = product(real_in, imag_kernel) + product(imag_in, real_kernel)
    return jnp.stack([real_out, imag_out], axis=2)


def mode_back(coeffs, mode_grads, kernel):
    real_in, imag_in = (coeffs[:, :, 0], coeffs[:, :, 1])
    real_grad, imag_grad = (mode_grads[:, :, 0], mode_grads[:, :, 1])
    real_kernel, imag_kernel = (kernel[:, :, 0], kernel[:, :, 1])
    outer_sum = partial(jnp.einsum, "mjc,mjo->mjco", precision=highest)
    inner_sum = partial(jnp.einsum, "mjo,mjco->mjc", precision=highest)
    kernel_real = outer_sum(real_in, real_grad) + outer_sum(imag_in, imag_grad)
    kernel_imag = outer_sum(real_in, imag_grad) - outer_sum(imag_in, real_grad)
    coeff_real = inner_sum(real_grad, real_kernel) + inner_sum(imag_grad, imag_kernel)
    coeff_imag = inner_sum(imag_grad, real_kernel) - inner_sum(real_grad, imag_kernel)
    return (
        jnp.stack([kernel_real, kernel_imag], axis=2),
        jnp.stack([coeff_real, coeff_imag], axis=2),
    )


def gelu_grad(pre_act, upstream):
    _, pullback = jax.vjp(jax.nn.gelu, pre_act)
    return pullback(upstream)[0]


def store_slot(buffer, value, slot_clip, is_valid):
    previous = lax.dynamic_index_in_dim(buffer, slot_clip, 0, keepdims=False)
    return lax.dynamic_update_index_in_dim(
        buffer, jnp.where(is_valid, value, previous), slot_clip, 0
    )


def on_device(
    inputs,
    cotangent,
    lift_weight,
    lift_bias,
    point_weight,
    layer_bias,
    spectral_weight,
    proj_weight,
    proj_bias,
    out_weight,
):
    batch_count, row_count, _, col_count = inputs.shape
    segment_count = lax.axis_size("segment")
    segment_index = lax.axis_index("segment")
    space_count = lax.axis_size("space")
    owned_modes = spectral_weight.shape[1]
    kx_count = spectral_weight.shape[2]
    channels = point_weight.shape[1]
    mode_count = kx_count // 2
    y_forward, y_inverse = y_tables(col_count, mode_count)
    x_forward, x_inverse = x_tables(row_count * space_count, mode_count)
    x_forward_adj = jnp.transpose(x_forward, (2, 3, 0, 1))
    x_inverse_adj = jnp.transpose(x_inverse, (2, 3, 0, 1))
    y_forward_wide = y_forward.astype(jnp.float32)
    y_inverse_wide = y_inverse.astype(jnp.float32)
    kernel = spectral_weight[0].astype(jnp.float32)
    point_matrix = point_weight[0]
    bias_vector = layer_bias[0]
    tick_count = batch_count + segment_count - 1

    def to_owners(y_coeffs, x_table):
        exchanged = lax.all_to_all(
            y_coeffs.astype(jnp.bfloat16), "space", split_axis=1, concat_axis=0, tiled=True
        ).astype(y_coeffs.dtype)
        return jnp.einsum("jqxp,xmpc->mjqc", x_table, exchanged, precision=highest)

    def from_owners(owned, x_table):
        spread = jnp.einsum("xpjq,mjqc->xmpc", x_table, owned, precision=highest)
        return lax.all_to_all(
            as_sent(spread), "space", split_axis=0, concat_axis=1, tiled=True
        ).astype(spread.dtype)

    def lifted(pick_slot):
        sample = lax.dynamic_index_in_dim(inputs, pick_slot, 0, keepdims=False)
        mixed = jnp.einsum("xty,tc->xcy", sample, lift_weight, preferred_element_type=jnp.float32)
        return (mixed + lift_bias[None, :, None]).astype(jnp.bfloat16)

    def forward_tick(state_now, tick_now):
        incoming, pre_store, act_store, mode_store = state_now
        pick_slot = jnp.clip(tick_now, 0, batch_count - 1)
        layer_in = lax.cond(segment_index == 0, lambda: lifted(pick_slot), lambda: incoming)
        y_coeffs = jnp.einsum(
            "xcy,ypm->xmpc", layer_in, y_forward, preferred_element_type=jnp.float32
        )
        coeffs = to_owners(y_coeffs, x_forward)
        back_rows = from_owners(mode_mult(coeffs, kernel), x_inverse)
        branch = jnp.einsum("xmpc,pmy->xcy", back_rows, y_inverse_wide, precision=highest)
        pointwise = jnp.einsum(
            "xcy,co->xoy", layer_in, point_matrix, preferred_element_type=jnp.float32
        )
        pre_act = pointwise + branch + bias_vector[None, :, None]
        slot_index = tick_now - segment_index
        is_valid = (slot_index >= 0) & (slot_index < batch_count)
        slot_clip = jnp.clip(slot_index, 0, batch_count - 1)
        pre_store = store_slot(pre_store, pre_act, slot_clip, is_valid)
        act_store = store_slot(act_store, layer_in, slot_clip, is_valid)
        mode_store = store_slot(mode_store, coeffs, slot_clip, is_valid)
        layer_out = jax.nn.gelu(pre_act).astype(jnp.bfloat16)
        sent = passed_along(layer_out, "segment", 1)
        return ((sent, pre_store, act_store, mode_store), None)

    start_state = (
        jnp.zeros((row_count, channels, col_count), jnp.bfloat16),
        jnp.zeros((batch_count, row_count, channels, col_count), jnp.float32),
        jnp.zeros((batch_count, row_count, channels, col_count), jnp.bfloat16),
        jnp.zeros((batch_count, owned_modes, kx_count, 2, channels), jnp.float32),
    )
    final_state, _ = lax.scan(forward_tick, start_state, jnp.arange(tick_count, dtype=jnp.int32))
    _, pre_store, act_store, mode_store = final_state

    def top_grad(slot_clip, pre_act):
        top_act = jax.nn.gelu(pre_act).astype(jnp.bfloat16)
        hidden = jnp.einsum("xcy,ck->xky", top_act, proj_weight, preferred_element_type=jnp.float32)
        hidden = hidden + proj_bias[None, :, None]
        target = lax.dynamic_index_in_dim(cotangent, slot_clip, 0, keepdims=False)
        upstream = (
            out_weight.astype(jnp.float32)[None, :, None] * target.astype(jnp.float32)[:, None, :]
        )
        hidden_grad = gelu_grad(hidden, upstream).astype(jnp.bfloat16)
        return jnp.einsum(
            "xky,ck->xcy", hidden_grad, proj_weight, preferred_element_type=jnp.float32
        ).astype(jnp.bfloat16)

    def backward_tick(state_now, tick_now):
        incoming, point_sum, kernel_sum = state_now
        slot_index = tick_now - (segment_count - 1 - segment_index)
        is_valid = (slot_index >= 0) & (slot_index < batch_count)
        slot_clip = jnp.clip(slot_index, 0, batch_count - 1)
        pre_act = lax.dynamic_index_in_dim(pre_store, slot_clip, 0, keepdims=False)
        layer_in = lax.dynamic_index_in_dim(act_store, slot_clip, 0, keepdims=False)
        coeffs = lax.dynamic_index_in_dim(mode_store, slot_clip, 0, keepdims=False)
        grad_out = lax.cond(
            segment_index == segment_count - 1,
            lambda: top_grad(slot_clip, pre_act),
            lambda: incoming,
        )
        pre_grad = gelu_grad(pre_act, grad_out.astype(jnp.float32)).astype(jnp.bfloat16)
        point_term = jnp.einsum(
            "xcy,xoy->co", layer_in, pre_grad, preferred_element_type=jnp.float32
        )
        y_grads = jnp.einsum(
            "xoy,pmy->xmpo", pre_grad, y_inverse, preferred_element_type=jnp.float32
        )
        mode_grads = to_owners(y_grads, x_inverse_adj)
        kernel_step, coeff_step = mode_back(coeffs, mode_grads, kernel)
        back_rows = from_owners(coeff_step, x_forward_adj)
        back_branch = jnp.einsum("xmpc,ypm->xcy", back_rows, y_forward_wide, precision=highest)
        pointwise_back = jnp.einsum(
            "co,xoy->xcy", point_matrix, pre_grad, preferred_element_type=jnp.float32
        )
        grad_in = (pointwise_back + back_branch).astype(jnp.bfloat16)
        point_sum = point_sum + jnp.where(is_valid, point_term, 0.0)
        kernel_sum = kernel_sum + jnp.where(is_valid, kernel_step, 0.0)
        sent = passed_along(grad_in, "segment", -1)
        return ((sent, point_sum, kernel_sum), None)

    back_start = (
        jnp.zeros((row_count, channels, col_count), jnp.bfloat16),
        jnp.zeros((channels, channels), jnp.float32),
        jnp.zeros((owned_modes, kx_count, 2, channels, channels), jnp.float32),
    )
    back_state, _ = lax.scan(backward_tick, back_start, jnp.arange(tick_count, dtype=jnp.int32))
    _, point_sum, kernel_sum = back_state
    point_total = lax.psum(point_sum, "space")
    factor = 1.0 / math.sqrt(batch_count * row_count * space_count * col_count)
    return (kernel_sum[None], (point_total * factor)[None])


f32, bf16 = (jnp.float32, jnp.bfloat16)
NT = (((1,), (1,)), ((), ()))
NN = (((1,), (0,)), ((), ()))
VMEM_LIMIT = 50 << 20


def np_y_tables(col_count, mode_count):
    ycells = np.arange(col_count)[:, None]
    ymodes = np.arange(mode_count)[None, :]
    angles = (ycells * ymodes % col_count) * (2.0 * math.pi / col_count)
    factor = 1.0 / math.sqrt(col_count)
    doubled = np.where(ymodes == 0, 1.0, 2.0)
    forward = np.stack([np.cos(angles), -np.sin(angles)], axis=0) * factor
    inverse = np.stack([doubled * np.cos(angles), -doubled * np.sin(angles)], axis=0) * factor
    return (forward.transpose(2, 0, 1), inverse.transpose(2, 0, 1))


def np_x_tables(row_total, mode_count):
    kx_count = 2 * mode_count
    indices = np.arange(kx_count)
    freq = np.where(indices < mode_count, indices, indices - kx_count)
    angles = (freq[:, None] * np.arange(row_total)[None, :] % row_total) * (2.0 * math.pi / row_total)
    factor = 1.0 / math.sqrt(row_total)
    c, s = (np.cos(angles) * factor, np.sin(angles) * factor)
    forward = np.stack([np.stack([c, s], -1), np.stack([-s, c], -1)], axis=1)
    inverse = np.stack([np.stack([c.T, -s.T], -1), np.stack([s.T, c.T], -1)], axis=1)
    return (forward, inverse)


def hdot(a, b):
    return jnp.dot(a, b, precision=highest, preferred_element_type=f32)


def gelu_both(v):
    k0 = math.sqrt(2.0 / math.pi)
    k1 = k0 * 0.044715
    v2 = v * v
    share = 0.5 + 0.5 * jnp.tanh(v * (k0 + k1 * v2))
    value = v * share
    slope = share + value * (1.0 - share) * (2.0 * k0 + (6.0 * k1) * v2)
    return (value, slope)


def low_half(shape):
    return lax.broadcasted_iota(jnp.int32, shape, 1) < shape[1] // 2


def swap_halves(a):
    return pltpu.roll(a, a.shape[1] // 2, 1)


def cross(a, b):
    low = low_half(a.shape)
    return (jnp.where(low, a, swap_halves(b)), jnp.where(low, swap_halves(a), b))


def grid_rows(first_ref, first, second_ref, second, x_half):
    parts = []
    for p in range(2):
        parts += cross(
            first_ref[pl.ds(first + p, x_half, stride=16), :],
            second_ref[pl.ds(second + p, x_half, stride=16), :],
        )
    return jnp.concatenate(parts, axis=0)


def own_grid(y_ref, row=8):
    return grid_rows(y_ref, row, y_ref, row + 2, y_ref.shape[0] // 16)


def put_chunk(grid, out_ref, first=0):
    x_half = grid.shape[0] // 4
    for p in range(2):
        base = 2 * p * x_half
        pair = cross(grid[base : base + x_half], grid[base + x_half : base + 2 * x_half])
        for mode in range(2):
            at = first + (2 * mode + p) * x_half
            block = pair[mode].astype(bf16)
            for k in range(out_ref.shape[0]):
                out_ref[k, at : at + x_half] = block


def put_split(t_ref, mode, rows):
    count = rows.shape[0]
    high = rows.astype(bf16).astype(f32)
    t_ref[2 * mode * count : (2 * mode + 1) * count] = high
    t_ref[(2 * mode + 1) * count : (2 * mode + 2) * count] = rows - high


def mode_products(t_ref, w_ref, m_ref, dims, start=0):
    pairs = w_ref.shape[1]
    for j in range(pairs):
        for mode in range(2):
            at = pl.ds(mode * 8 * pairs + j, 8, stride=pairs)
            m_ref[at, :] = lax.dot_general(
                t_ref[at, :].astype(bf16), w_ref[start + mode, j], dims, preferred_element_type=f32
            )
    count = 4 * pairs
    return [
        m_ref[2 * mode * count : (2 * mode + 1) * count]
        + m_ref[(2 * mode + 1) * count : (2 * mode + 2) * count]
        for mode in range(2)
    ]


def first_kx(shape, pairs):
    return (lax.broadcasted_iota(jnp.int32, shape, 0) // pairs) % 2 == 0


def forward_modes(y_ref, w_ref, lx_ref, xi_ref, t_ref, m_ref, out_ref, row=8, start=0):
    pairs = w_ref.shape[1]
    ys = own_grid(y_ref, row)
    sw = swap_halves(ys)
    low = low_half(ys.shape)
    zero = jnp.zeros_like(ys)
    put_split(t_ref, 0, hdot(lx_ref[...], jnp.concatenate([jnp.where(low, ys, zero), jnp.where(low, zero, sw)], axis=0)))
    put_split(t_ref, 1, hdot(lx_ref[...], jnp.concatenate([jnp.where(low, sw, zero), jnp.where(low, zero, ys)], axis=0)))
    m0, m1 = mode_products(t_ref, w_ref, m_ref, NN, start)
    first = first_kx(m0.shape, pairs)
    s0 = jnp.where(first, m0, swap_halves(m0))
    s1 = jnp.where(first, swap_halves(m1), m1)
    first_row = start * out_ref.shape[1] // w_ref.shape[0]
    put_chunk(hdot(xi_ref[...], jnp.where(low_half(m0.shape), s0, s1)), out_ref, first_row)


def backward_modes(y_ref, w_ref, xa_ref, xf_ref, t_ref, m_ref, out_ref):
    pairs = w_ref.shape[1]
    g = hdot(xa_ref[...], own_grid(y_ref))
    sw = swap_halves(g)
    first = first_kx(g.shape, pairs)
    keep = low_half(g.shape) == first
    zero = jnp.zeros_like(g)
    put_split(t_ref, 0, jnp.where(keep, jnp.where(first, g, sw), zero))
    put_split(t_ref, 1, jnp.where(keep, jnp.where(first, sw, g), zero))
    m0, m1 = mode_products(t_ref, w_ref, m_ref, NT)
    half = 2 * pairs
    pr0, pi0, pr1, pi1 = (m0[:half], m0[half:], m1[:half], m1[half:])
    low = low_half(pr0.shape)
    real = jnp.where(low, pr0 + swap_halves(pi0), swap_halves(pr1) + pi1)
    imag = jnp.where(low, pi0 - swap_halves(pr0), swap_halves(pi1) - pr1)
    put_chunk(hdot(xf_ref[...], jnp.concatenate([real, imag], axis=0)), out_ref)


def choose_kernel(seg_ref, layer, w_refs, w_ref, sem, start):
    for seg in range(4):
        pair = seg // 2
        source = w_refs[(0 if seg % 2 == layer % 2 else 1) + (0 if pair == layer // 2 else 2)]
        if pair == layer // 2:
            source = source.at[2 * pair : 2 * pair + 2]

        @pl.when(seg_ref[0] == seg)
        def _(source=source):
            copy = pltpu.make_async_copy(source, w_ref, sem)
            if start:
                copy.start()
            else:
                copy.wait()


def choose_all(seg_ref, w_refs, w_ref, sem, start):
    for lane in range(2):
        @pl.when(seg_ref[0] % 2 == lane)
        def _(lane=lane):
            copy = pltpu.make_async_copy(w_refs[lane], w_ref, sem)
            if start:
                copy.start()
            else:
                copy.wait()


def pack_kernel(in_ref, out_ref):
    out_ref[...] = jnp.concatenate([in_ref[:, 0], in_ref[:, 1]], axis=-1)


def widen(recv_ref, r_ref):
    rows = recv_ref.shape[1]
    for k in range(r_ref.shape[0] // rows):
        r_ref[k * rows : (k + 1) * rows] = recv_ref[k].astype(f32)


def row_product(weight, field, r_ref, table, x, x_half):
    rows = r_ref[pl.ds(x, table.shape[0], stride=x_half), :]
    lhs = jnp.concatenate([weight, rows.T.astype(bf16)], axis=1)
    return jnp.dot(lhs, jnp.concatenate([field, table], axis=0), preferred_element_type=f32)


def chunk_of(x, half_side, space, rows, per_chunk):
    inner = x % rows
    return ((inner // per_chunk) * space + half_side * (space // 2) + x // rows, inner % per_chunk)


def lift_kernel(seg_ref, in_ref, lw_ref, lb_ref, tab_ref, act_ref, y_ref, *, space, rows, per_chunk, depth):
    table = tab_ref[seg_ref[1]]
    for x in range(act_ref.shape[0]):
        cells = []
        for side in range(2):
            k, i = chunk_of(x, side, space, rows, per_chunk)
            cells.append(in_ref[k, i * depth : (i + 1) * depth, :])
        cells = jnp.concatenate(cells, axis=0)
        act = jnp.dot(lw_ref[...], cells, preferred_element_type=f32) + lb_ref[...]
        act = act.astype(bf16)
        act_ref[x] = act
        y_ref[x * 16 : (x + 1) * 16] = lax.dot_general(
            table, act, NT, preferred_element_type=f32
        )


def first_modes_kernel(seg_ref, y_ref, lx_ref, xi_ref, w0, w1, out_ref, w_ref, sem, t_ref, m_ref):
    choose_all(seg_ref, (w0, w1), w_ref, sem, True)
    choose_all(seg_ref, (w0, w1), w_ref, sem, False)
    for start in range(0, w_ref.shape[0], 2):
        forward_modes(y_ref, w_ref, lx_ref, xi_ref, t_ref, m_ref, out_ref, 2 * start, start)


def in_pairs(count, start, finish, scratch):
    start(0, scratch[0])

    def two(i, carry):
        x = 2 * i
        start(x + 1, scratch[1])
        finish(x, scratch[0])
        start(jnp.minimum(x + 2, count - 1), scratch[0])
        finish(x + 1, scratch[1])
        return carry

    lax.fori_loop(0, count // 2, two, 0)


def put_rows(y_ref, x, rows):
    y_ref[pl.ds(pl.multiple_of(x * 16, 16), 16), :] = rows


def forward_kernel(
    seg_ref, recv_ref, act_ref, pw_ref, pb_ref, inv_ref, tab_ref, lx_ref, xi_ref, w0, w1, w2, w3,
    next_ref, slope_ref, y_ref, out_ref, w_ref, sem, t_ref, m_ref, r_ref, p0_ref, p1_ref, *, layer,
):
    x_half = act_ref.shape[0]
    choose_kernel(seg_ref, layer, (w0, w1, w2, w3), w_ref, sem, True)
    widen(recv_ref, r_ref)
    table = tab_ref.at[seg_ref[1]]

    def start(x, ref):
        ref[...] = row_product(pw_ref[layer - 1], act_ref[x], r_ref, inv_ref[...], x, x_half)

    def finish(x, ref):
        value, slope = gelu_both(ref[...] + pb_ref[layer - 1])
        value = value.astype(bf16)
        next_ref[x] = value
        slope_ref[x] = slope.astype(bf16)
        put_rows(y_ref, x, lax.dot_general(table[...], value, NT, preferred_element_type=f32))

    in_pairs(x_half, start, finish, (p0_ref, p1_ref))
    choose_kernel(seg_ref, layer, (w0, w1, w2, w3), w_ref, sem, False)
    forward_modes(y_ref, w_ref, lx_ref, xi_ref, t_ref, m_ref, out_ref)


def adjoint_rows(x, grad, act, table, pre_ref, y_ref, point_ref):
    pre_grad = grad.astype(bf16)
    pre_ref[x] = pre_grad
    both = lax.dot_general(
        jnp.concatenate([table[...], act], axis=0), pre_grad, NT, preferred_element_type=f32
    )
    put_rows(y_ref, x, both[:16])
    point_ref[...] += both[16:]


def top_kernel(
    seg_ref, recv_ref, act_ref, in_ref, pw_ref, pb_ref, inv_ref, up_ref, hb_ref, down_ref, ow_ref,
    tab_ref, xa_ref, xf_ref, w0, w1, w2, w3,
    pre_ref, y_ref, point_ref, out_ref, w_ref, sem, t_ref, m_ref, r_ref,
    p0_ref, p1_ref, s0_ref, s1_ref, h0_ref, h1_ref,
    *, layer, space, rows, per_chunk, first_row,
):
    x_half = act_ref.shape[0]
    choose_kernel(seg_ref, layer, (w0, w1, w2, w3), w_ref, sem, True)
    widen(recv_ref, r_ref)
    point_ref[...] = jnp.zeros_like(point_ref)
    table = tab_ref.at[seg_ref[1]]
    hidden_count = up_ref.shape[0]
    size = act_ref.shape[1] // 2

    def start(x, ref):
        ref[...] = row_product(pw_ref[layer], act_ref[x], r_ref, inv_ref[...], x, x_half)

    def middle(ref, slope_ref, hidden_ref):
        value, slope = gelu_both(ref[...] + pb_ref[layer])
        slope_ref[...] = slope
        value = value.astype(bf16)
        for side in range(2):
            hidden_ref[side * hidden_count : (side + 1) * hidden_count] = jnp.dot(
                up_ref[...], value[side * size : (side + 1) * size], preferred_element_type=f32
            )

    def finish(x, slope_ref, hidden_ref):
        grads = []
        for side in range(2):
            hidden = hidden_ref[side * hidden_count : (side + 1) * hidden_count]
            _, hidden_slope = gelu_both(hidden + hb_ref[...])
            chunk, within = chunk_of(x, side, space, rows, per_chunk)
            cots = in_ref[chunk, first_row : first_row + per_chunk, :].astype(f32)
            cot = cots[:1]
            for other in range(1, per_chunk):
                cot = jnp.where(within == other, cots[other : other + 1], cot)
            grads.append(
                cot * jnp.dot(
                    down_ref[...], (hidden_slope * ow_ref[...]).astype(bf16), preferred_element_type=f32
                )
            )
        grad = jnp.concatenate(grads, axis=0) * slope_ref[...]
        adjoint_rows(x, grad, act_ref[x], table, pre_ref, y_ref, point_ref)

    last = x_half - 1
    start(0, p0_ref)
    middle(p0_ref, s0_ref, h0_ref)
    start(1, p1_ref)

    def two(i, carry):
        x = 2 * i
        start(jnp.minimum(x + 2, last), p0_ref)
        middle(p1_ref, s1_ref, h1_ref)
        finish(x, s0_ref, h0_ref)
        start(jnp.minimum(x + 3, last), p1_ref)
        middle(p0_ref, s0_ref, h0_ref)
        finish(x + 1, s1_ref, h1_ref)
        return carry

    lax.fori_loop(0, x_half // 2, two, 0)
    choose_kernel(seg_ref, layer, (w0, w1, w2, w3), w_ref, sem, False)
    backward_modes(y_ref, w_ref, xa_ref, xf_ref, t_ref, m_ref, out_ref)


def backward_kernel(
    seg_ref, recv_ref, grad_ref, slope_ref, act_ref, pw_ref, fwd_ref, tab_ref, xa_ref, xf_ref,
    w0, w1, w2, w3,
    pre_ref, y_ref, point_ref, out_ref, w_ref, sem, t_ref, m_ref, r_ref, p0_ref, p1_ref, *, layer,
):
    x_half = act_ref.shape[0]
    if layer:
        choose_kernel(seg_ref, layer, (w0, w1, w2, w3), w_ref, sem, True)
    widen(recv_ref, r_ref)
    point_ref[...] = jnp.zeros_like(point_ref)
    table = tab_ref.at[seg_ref[1]]

    def start(x, ref):
        ref[...] = row_product(pw_ref[layer + 1], grad_ref[x], r_ref, fwd_ref[...], x, x_half)

    def finish(x, ref):
        grad = ref[...] * slope_ref[x].astype(f32)
        adjoint_rows(x, grad, act_ref[x], table, pre_ref, y_ref, point_ref)

    in_pairs(x_half, start, finish, (p0_ref, p1_ref))
    if layer:
        choose_kernel(seg_ref, layer, (w0, w1, w2, w3), w_ref, sem, False)
        backward_modes(y_ref, w_ref, xa_ref, xf_ref, t_ref, m_ref, out_ref)
    else:
        out_ref[...] = jnp.zeros_like(out_ref)


def pick_kernel(seg_ref, *refs, layers):
    ya_refs, yg_refs, pg_refs = (refs[:layers], refs[layers : 2 * layers], refs[2 * layers : 3 * layers])
    count = ya_refs[0].shape[0]
    seg = seg_ref[0]
    partner = seg + 1 - 2 * (seg % 2)
    for out_ref, wanted in zip(refs[3 * layers :], (seg, partner)):
        for layer in range(layers):
            @pl.when(wanted == layer)
            def _(layer=layer, out_ref=out_ref):
                out_ref[:count] = ya_refs[layer][...]
                out_ref[count : 2 * count] = yg_refs[layer][...]
                pg = pg_refs[layer][...]
                half = pg.shape[0] // 2
                out_ref[2 * count :] = pg[:half] + swap_halves(pg[half:])


def grads_kernel(mine_ref, theirs_ref, xz_ref, xa_ref, out_ref, point_ref, a_ref, b_ref, *, scale):
    mode = pl.program_id(0)
    c = point_ref.shape[0]
    count = (mine_ref.shape[0] - c) // 2
    x_half = count // 16

    @pl.when(mode == 0)
    def _():
        point_ref[...] = (mine_ref[2 * count :, :c] + theirs_ref[2 * count :, :c]) * scale

    z = hdot(xz_ref[...], grid_rows(mine_ref, 2 * mode, theirs_ref, 2 * mode, x_half))
    at = count + 2 * mode
    g = hdot(xa_ref[...], grid_rows(mine_ref, at, theirs_ref, at, x_half))
    rows = z.shape[0]
    kx = rows // 2
    zs, gs = (swap_halves(z), swap_halves(g))
    a_ref[:rows] = z
    a_ref[rows:] = zs
    low = low_half((kx, z.shape[1]))
    b_ref[:kx] = jnp.where(low, g[:kx], gs[kx:])
    b_ref[kx:rows] = jnp.where(low, g[kx:], -gs[:kx])
    b_ref[rows : rows + kx] = jnp.where(low, gs[:kx], g[kx:])
    b_ref[rows + kx :] = jnp.where(low, gs[kx:], -g[:kx])
    for j in range(kx):
        a = a_ref[pl.ds(j, 4, stride=kx), :][:, :c]
        b = b_ref[pl.ds(j, 4, stride=kx), :]
        ah, bh = (a.astype(bf16).astype(f32), b.astype(bf16).astype(f32))
        left = jnp.concatenate([ah, a - ah, ah], axis=0).T.astype(bf16)
        right = jnp.concatenate([bh, bh, b - bh], axis=0).astype(bf16)
        out_ref[0, j, 0] = jnp.dot(left, right[:, :c], preferred_element_type=f32)
        out_ref[0, j, 1] = jnp.dot(left, right[:, c:], preferred_element_type=f32)


def replicated(
    inputs, cotangent, lift_weight, lift_bias, point_weight, layer_bias, spectral_weight,
    proj_weight, proj_bias, out_weight,
):
    batch, row_count, depth, cols = inputs.shape
    segments, space = (lax.axis_size("segment"), lax.axis_size("space"))
    seg, place = (lax.axis_index("segment"), lax.axis_index("space"))
    pair = seg // 2
    both = ("segment", "space")
    owned, kx = spectral_weight.shape[1:3]
    c = point_weight.shape[1]
    x_count = row_count * space
    x_half = x_count // 2
    mode_count = owned * space
    per_chunk = row_count // segments
    pairs = kx // 2
    group = segments // 2 * space

    cells = lax.dynamic_slice_in_dim(inputs, seg * per_chunk, per_chunk, 1)
    cells = cells.reshape(batch, per_chunk * depth, cols)
    cots = lax.dynamic_slice_in_dim(cotangent, seg * per_chunk, per_chunk, 1)
    weight_rows = c * c // space // cols
    share = lax.dynamic_index_in_dim(
        point_weight.reshape(space, weight_rows, cols), place, 0, keepdims=False
    )
    high = lax.reduce_precision(layer_bias[0], 8, 7)
    mid = lax.reduce_precision(layer_bias[0] - high, 8, 7)
    rest = layer_bias[0] - high - mid
    bias_row = jnp.concatenate([high, mid, rest, jnp.zeros((cols - 3 * c,), f32)]).astype(bf16)
    common = jnp.concatenate([share, bias_row[None]], axis=0)
    chunk = jnp.concatenate([cells, cots, jnp.broadcast_to(common[None], (batch,) + common.shape)], axis=1)
    cot_row = per_chunk * depth
    share_row = cot_row + per_chunk
    bias_at = share_row + weight_rows
    chunk = jnp.pad(chunk, ((0, 0), (0, -chunk.shape[1] % 8), (0, 0)))
    chunk = jnp.broadcast_to(chunk[None, :, None], (segments // 2, batch, space) + chunk.shape[1:])
    stack = spectral_weight[0].reshape(owned, 2, pairs, 2 * c, c)
    pack = pl.pallas_call(
        pack_kernel,
        grid=(owned,),
        in_specs=[pl.BlockSpec((1, 2, pairs, 2 * c, c), lambda m: (m, 0, 0, 0, 0))],
        out_specs=pl.BlockSpec((1, pairs, 2 * c, 2 * c), lambda m: (m, 0, 0, 0)),
        out_shape=jax.ShapeDtypeStruct((owned, pairs, 2 * c, 2 * c), bf16),
        compiler_params=pltpu.CompilerParams(vmem_limit_bytes=VMEM_LIMIT),
        name="pack",
    )
    own = pack(stack)
    swap = [(0, 1), (1, 0), (2, 3), (3, 2)]
    neighbour = lax.ppermute(own, "segment", swap)
    away = lax.dynamic_slice_in_dim(own, 2 * (1 - pair), 2, 0)
    across_odd = lax.ppermute(away, "segment", [(1, 3), (3, 1)])

    grid_in = lax.all_to_all(
        chunk.reshape((segments * space,) + chunk.shape[3:]), both, 0, 0, tiled=True
    )

    def weights_of(layer):
        if layer % 2:
            return (own, neighbour, across_odd, across_odd_on)
        return (own, neighbour, across_even, across_even_on)

    points = grid_in[:, share_row:bias_at].reshape(segments, c, c)
    bias_parts = grid_in[::space, bias_at, : 3 * c].astype(f32).reshape(segments, 3, c)
    biases = bias_parts[:, 0] + bias_parts[:, 1] + bias_parts[:, 2]
    blank = jnp.zeros((segments, c, c), bf16)

    def doubled(mats):
        return jnp.concatenate(
            [jnp.concatenate([mats, blank], axis=2), jnp.concatenate([blank, mats], axis=2)], axis=1
        )

    point_back = doubled(points)
    point_fwd = doubled(jnp.transpose(points, (0, 2, 1)))
    bias_cols = jnp.concatenate([biases] * 2, axis=1)[:, :, None]

    y_forward, y_inverse = np_y_tables(cols, mode_count)
    x_forward, x_inverse = np_x_tables(x_count, kx // 2)
    firsts = [k % space * owned + k // space * 2 for k in range(group)]
    order = [first + i for first in firsts for i in range(2)]

    def gathered(table):
        return jnp.asarray(table[order].reshape(4 * group, cols), bf16)

    def analysis(table):
        full = np.zeros((group, 16, cols))
        for k in range(group):
            s = k % space
            full[k, : 2 * owned] = table[s * owned : (s + 1) * owned].reshape(2 * owned, cols)
            full[k, 8:12] = table[firsts[k] : firsts[k] + 2].reshape(4, cols)
        return jnp.asarray(full, bf16)

    inv_table, fwd_table = (gathered(y_inverse), gathered(y_forward))
    act_table, grad_table = (analysis(y_forward), analysis(y_inverse))
    xf = x_forward.transpose(0, 1, 3, 2).reshape(kx, 2, 2 * x_count)
    lx = np.concatenate(
        [np.concatenate([xf[:, 0], -xf[:, 1]], 1), np.concatenate([xf[:, 1], xf[:, 0]], 1)], 0
    )
    xz = xf.transpose(1, 0, 2).reshape(2 * kx, 2 * x_count)
    xi = x_inverse.transpose(1, 0, 3, 2).reshape(2 * x_count, 2 * kx)
    lx, xz, xi, xa, xb = (jnp.asarray(t, f32) for t in (lx, xz, xi, xi.T.copy(), xz.T.copy()))

    device_lists = [
        [(2 * k + lane) * space + s for k in range(segments // 2) for s in range(space)]
        for lane in range(2)
    ]

    def to_all(block):
        return lax.all_to_all(block, both, 0, 0, tiled=True, axis_index_groups=device_lists)

    def whole(array):
        rank = len(array.shape)
        return pl.BlockSpec(array.shape, lambda *i: (0,) * rank)

    def placed(kernel):
        def body(*refs):
            own_seg = lax.axis_index("segment")
            kernel((own_seg, own_seg // 2 * space + lax.axis_index("space")), *refs)

        return body


    def call(kernel, args, weights, outs, scratch):
        near = pl.BlockSpec(memory_space=pltpu.VMEM)
        return pl.pallas_call(
            placed(kernel),
            in_specs=[near] * len(args)
            + [pl.BlockSpec(memory_space=pl.ANY)] * len(weights),
            out_specs=[near] * len(outs),
            out_shape=outs,
            scratch_shapes=scratch,
            compiler_params=pltpu.CompilerParams(vmem_limit_bytes=VMEM_LIMIT),
        )(*args, *weights)

    lanes = 2 * c
    field = jax.ShapeDtypeStruct((x_half, lanes, cols), bf16)
    ycoef = jax.ShapeDtypeStruct((x_half * 16, lanes), f32)
    sent = jax.ShapeDtypeStruct((group, 2 * x_count, lanes), bf16)
    sent_first = jax.ShapeDtypeStruct((group, 4 * x_count, lanes), bf16)
    point = jax.ShapeDtypeStruct((lanes, lanes), f32)
    mode_scratch = [
        pltpu.VMEM((2,) + own.shape[1:], bf16), pltpu.SemaphoreType.DMA(()),
        pltpu.VMEM((8 * kx, lanes), f32), pltpu.VMEM((8 * kx, lanes), f32),
    ]
    row = pltpu.VMEM((lanes, cols), f32)
    row_scratch = [pltpu.VMEM((group * 2 * x_count, lanes), f32), row, row]
    top_scratch = [row, row] + [pltpu.VMEM((2 * proj_weight.shape[1], cols), f32)] * 2

    zero = jnp.zeros_like(lift_weight.T)
    lift = jnp.concatenate(
        [jnp.concatenate([lift_weight.T, zero], 1), jnp.concatenate([zero, lift_weight.T], 1)], 0
    )
    lift_col = jnp.concatenate([lift_bias] * 2)[:, None]
    where = dict(space=space, rows=row_count, per_chunk=per_chunk)
    act, y0 = pl.pallas_call(
        placed(partial(lift_kernel, depth=depth, **where)),
        out_shape=[field, ycoef],
        compiler_params=pltpu.CompilerParams(vmem_limit_bytes=VMEM_LIMIT),
        name="lift",
    )(grid_in, lift, lift_col, act_table)
    acts, slopes, ya = ([act], [], [y0])
    (mine,) = call(
        first_modes_kernel, (y0, lx, xi), (own, neighbour), [sent_first],
        [pltpu.VMEM(own.shape, bf16)] + mode_scratch[1:],
    )
    across_even = lax.ppermute(away, "segment", [(2, 0)])
    for layer in range(1, segments):
        recv = to_all(mine)
        table = inv_table
        if layer == 1:
            ready = lax.optimization_barrier((across_odd, recv, point_fwd, bias_cols))[0]
            across_odd_on = lax.ppermute(ready, "segment", [(1, 0), (3, 2)])
            table = jnp.asarray(y_inverse.reshape(2 * mode_count, cols), bf16)
        act, slope, y, mine = call(
            partial(forward_kernel, layer=layer),
            (recv, acts[-1], point_fwd, bias_cols, table, act_table, lx, xi),
            weights_of(layer), [field, field, ycoef, sent], mode_scratch + row_scratch,
        )
        acts.append(act)
        slopes.append(slope)
        ya.append(y)
        if layer == 1:
            across_even_on = lax.ppermute(
                lax.optimization_barrier((across_even, mine))[0], "segment", [(0, 1)]
            )

    recv = to_all(mine)
    last = segments - 1
    pre_grad, y, pg, mine = call(
        partial(top_kernel, layer=last, first_row=cot_row, **where),
        (recv, acts[last], grid_in, point_fwd, bias_cols, inv_table,
         proj_weight.T, proj_bias[:, None], proj_weight, out_weight.astype(f32)[:, None],
         grad_table, xa, xb),
        weights_of(last), [field, ycoef, point, sent], mode_scratch + row_scratch + top_scratch,
    )
    yg, pgs = ([y], [pg])
    for layer in reversed(range(last)):
        recv = to_all(mine)
        pre_grad, y, pg, mine = call(
            partial(backward_kernel, layer=layer),
            (recv, pre_grad, slopes[layer], acts[layer], point_back, fwd_table,
             grad_table, xa, xb),
            weights_of(layer), [field, ycoef, point, sent], mode_scratch + row_scratch,
        )
        yg.insert(0, y)
        pgs.insert(0, pg)

    pieces = ya + yg + pgs
    summary = jax.ShapeDtypeStruct((2 * x_half * 16 + c, lanes), f32)
    mine, theirs = pl.pallas_call(
        placed(partial(pick_kernel, layers=segments)),
        out_shape=[summary, summary],
        compiler_params=pltpu.CompilerParams(vmem_limit_bytes=VMEM_LIMIT),
        name="pick",
    )(*pieces)
    theirs = lax.ppermute(theirs, "segment", [(0, 1), (1, 0), (2, 3), (3, 2)])
    pieces = [mine, theirs, xz, xa]
    spectral, point_out = pl.pallas_call(
        partial(grads_kernel, scale=1.0 / math.sqrt(batch * x_count * cols)),
        grid=(owned,),
        in_specs=[whole(a) for a in pieces],
        out_specs=[
            pl.BlockSpec((1, kx, 2, c, c), lambda m: (m, 0, 0, 0, 0)),
            pl.BlockSpec((c, c), lambda m: (0, 0)),
        ],
        out_shape=[
            jax.ShapeDtypeStruct((owned, kx, 2, c, c), f32),
            jax.ShapeDtypeStruct((c, c), f32),
        ],
        scratch_shapes=[pltpu.VMEM((4 * kx, lanes), f32)] * 2,
        compiler_params=pltpu.CompilerParams(vmem_limit_bytes=VMEM_LIMIT),
        name="grads",
    )(*pieces)
    return (spectral[None], point_out[None])


def fits_replicated(mesh, inputs, point_weight, spectral_weight):
    segments, space = (mesh.shape["segment"], mesh.shape["space"])
    batch = inputs.shape[0] // mesh.shape["groups"]
    _, rows, depth, cols = inputs.shape
    layers, c, _ = point_weight.shape
    modes, kx = spectral_weight.shape[1:3]
    return (
        batch == 2
        and 2 * c == 128
        and layers == segments == 4
        and modes == 4 * space
        and space in (2, 4)
        and rows % (segments * space) == 0
        and rows % 32 == 0
        and rows <= 64
        and kx == 32
        and depth == 8
        and cols % 128 == 0
        and cols >= 3 * c
        and c * c % (space * cols) == 0
    )


def solution(mesh):
    in_specs = (
        P("groups", "space", None, None),
        P("groups", "space", None),
        P(),
        P(),
        P("segment", None, None),
        P("segment", None),
        P("segment", "space", None, None, None, None),
        P(),
        P(),
        P(),
    )
    out_specs = (
        P(("groups", "segment"), "space", None, None, None, None),
        P(("groups", "segment"), None, None),
    )

    def step(inputs, cotangent, lift_weight, lift_bias, point_weight, layer_bias, spectral_weight, *rest):
        fits = fits_replicated(mesh, inputs, point_weight, spectral_weight)
        mapped = jax.shard_map(
            replicated if fits else on_device,
            mesh=mesh, in_specs=in_specs, out_specs=out_specs, check_vma=False,
        )
        return mapped(
            inputs, cotangent, lift_weight, lift_bias, point_weight, layer_bias, spectral_weight, *rest
        )

    return step
```
